32 devices in a mesh: dp: 8 (over y, x, core), mp: 4 (over z).
Axes of the slice: x: 2, y: 2, z: 4, core: 2. Of those that a mesh axis runs over, the one named last changes fastest.
Arguments:
- tokens: bfloat16 [17408, 1024], P(('dp', 'mp')), may hold values from -6 to 6
- groups: int32 [17408], P(('dp', 'mp')), may hold values from 0 to 15
- lengths: int32 [16], P('dp'), may hold values from 272 to 1088, as said below
- qkv_weight: bfloat16 [3, 1024, 1024], P(None, None, 'mp'), may hold values from -0.1875 to 0.1875
- qv_bias: bfloat16 [2, 1024], P(None, 'mp'), may hold values from -3 to 3
- out_weight: bfloat16 [1024, 1024], P('mp'), may hold values from -1.5 to 1.5
- out_bias: bfloat16 [1024], replicated, may hold values from -2 to 2
- up_weight: bfloat16 [1024, 4096], P(None, 'mp'), may hold values from -0.1875 to 0.1875
- up_bias: bfloat16 [4096], P('mp'), may hold values from -3 to 3
- down_weight: bfloat16 [4096, 1024], P('mp'), may hold values from -0.09375 to 0.09375
- down_bias: bfloat16 [1024], replicated, may hold values from -2 to 2
- norm_gain: bfloat16 [4, 1024], replicated, may hold values from 0.5 to 1.5
- norm_bias: bfloat16 [4, 1024], replicated, may hold values from -2 to 2
- group_table: bfloat16 [16, 1024], replicated, may hold values from -3 to 3
- cotangent: bfloat16 [17408, 1024], P(('dp', 'mp')), may hold values from -6 to 6
Outputs:
- output: bfloat16 [17408, 1024], P(('dp', 'mp'))
- input_grad: float32 [17408, 1024], P(('dp', 'mp'))
- qkv_grad: float32 [3, 1024, 1024], P(None, None, 'mp')
- qv_bias_grad: float32 [2, 1024], P(None, 'mp')
- out_weight_grad: float32 [1024, 1024], P('mp')
- out_bias_grad: float32 [1024], replicated
- up_weight_grad: float32 [1024, 4096], P(None, 'mp')
- up_bias_grad: float32 [4096], P('mp')
- down_weight_grad: float32 [4096, 1024], P('mp')
- down_bias_grad: float32 [1024], replicated
- norm_gain_grad: float32 [4, 1024], replicated
- norm_bias_grad: float32 [4, 1024], replicated
- group_table_grad: float32 [16, 1024], replicated
The draws below stay inside these ranges and needn't reach their ends.
Inputs may be any that keep to these rules, and one draw needn't show every extreme that they name: `lengths`: each sequence's valid length; some sequence has all 1088 tokens valid and some only 272.
All inputs are finite; a program needn't handle non-finite values.
Results may differ from the reference program's by a relative error of at most 0.009.
Values may be sent and summed in bfloat16 or wider, within the bound.
No kernel may reach another device: no remote copies, remote signals or barrier semaphores. Data moves between devices by JAX's collectives and lax.ppermute only.
A program may use at most 192 MiB of HBM per device.

```python
import math
import jax
import jax.numpy as jnp
import numpy as np
from jax import lax

D = 1024
HEADS = 16
HEAD_DIM = 64
FF = 4096
SEQ_LEN = 1088
GROUPS = 16
SEQS = 16
TOKENS = 17408


def draw_lengths(key, part):
    key_base = jax.random.fold_in(key, 11)
    key_spot = jax.random.fold_in(key, 23)
    drawn = jax.random.randint(key_base, (SEQS,), SEQ_LEN // 4, SEQ_LEN + 1)
    full_row = jax.random.randint(key_spot, (), 0, SEQS)
    positions = jnp.arange(SEQS)
    drawn = jnp.where(positions == full_row, SEQ_LEN, drawn)
    drawn = jnp.where(positions == (full_row + SEQS // 2) % SEQS, SEQ_LEN // 4, drawn)
    return drawn.astype(jnp.int32)


def plant(values, stream_key, smallest, top_value):
    longest = values.shape.index(max(values.shape))
    spots = []
    for shift in (0, 1):
        where = [jax.random.randint(jax.random.fold_in(stream_key, axis), (), 0, length) for axis, length in enumerate(values.shape)]
        where[longest] = (where[longest] + shift) % values.shape[longest]
        spots.append(tuple(where))
    return values.at[spots[0]].set(smallest).at[spots[1]].set(top_value)


def steps_of(own_key, dims, shards, low, top_value):
    factor_of, own = 1.0, jax.random.fold_in(own_key, 6)
    for dim, parts in shards:
        draws = jnp.exp(jax.random.uniform(jax.random.fold_in(own, dim), (parts,), jnp.float32, low / len(shards), top_value / len(shards)))
        factor_of = factor_of * jnp.repeat(draws, dims[dim] // parts).reshape([-1 if axis == dim else 1 for axis in range(len(dims))])
    return factor_of


def cumulative_ranks(number_of, lean):
    weights = [(1 << 20) // math.isqrt(rank ** lean) + 1 for rank in range(1, number_of + 1)]
    scale = 1 + sum(weights) // (1 << 30)
    return np.cumsum(np.array([max(1, weight // scale) for weight in weights]))


def ranked_ids(key, extent, count, slope):
    listing = cumulative_ranks(count, slope)
    pick = jax.random.randint(jax.random.fold_in(key, 1), extent, 0, int(listing[count - 1]))
    standing = jnp.searchsorted(jnp.asarray(listing, jnp.int32), pick, side="right")
    return jax.random.permutation(jax.random.fold_in(key, 2), count)[standing].astype(jnp.int32)


def scatter_about(own_key, dims, width, most, split=(), kind=jnp.bfloat16):
    array = jax.random.normal(own_key, dims, jnp.float32) * width
    if len(split) > 0:
        array = steps_of(own_key, dims, split, -0.22, 0.18) * array
    return jnp.clip(array, min=-most, max=most).astype(kind)


def setup_inputs(seed: int = 0) -> dict:
    splits = jax.random.split(jax.random.key(seed), 16)
    tokens = scatter_about(splits[0], (TOKENS, D), 1.0, 6.0, ((0, 32),))
    groups = plant(ranked_ids(splits[1], (TOKENS,), GROUPS, 2), jax.random.fold_in(splits[1], 3), 0, GROUPS - 1).astype(jnp.int32)
    lengths = draw_lengths(jax.random.fold_in(splits[15], 71), 0)
    qkv_weight = scatter_about(splits[3], (3, D, D), D ** -0.5, 0.1875, ((2, 4),))
    qv_bias = scatter_about(splits[4], (2, D), 0.5, 3.0, ((1, 4),))
    out_weight = scatter_about(splits[5], (D, D), 16 ** -0.5, 1.5, ((0, 4),))
    out_bias = scatter_about(splits[6], (D,), 0.3, 2.0)
    up_weight = scatter_about(splits[7], (D, FF), D ** -0.5, 0.1875, ((1, 4),))
    up_bias = scatter_about(splits[8], (FF,), 0.5, 3.0, ((0, 4),))
    down_weight = scatter_about(splits[9], (FF, D), FF ** -0.5, 0.09375, ((0, 4),))
    down_bias = scatter_about(splits[10], (D,), 0.3, 2.0)
    norm_gain = jnp.clip(1.0 + 0.1 * jax.random.normal(splits[11], (4, D), jnp.float32), 0.5, 1.5).astype(jnp.bfloat16)
    norm_bias = scatter_about(splits[12], (4, D), 0.3, 2.0)
    group_table = scatter_about(splits[13], (GROUPS, D), 0.5, 3.0)
    cotangent = scatter_about(splits[14], (TOKENS, D), 1.0, 6.0, ((0, 32),))
    return dict(tokens=tokens, groups=groups, lengths=lengths, qkv_weight=qkv_weight, qv_bias=qv_bias, out_weight=out_weight, out_bias=out_bias, up_weight=up_weight, up_bias=up_bias, down_weight=down_weight, down_bias=down_bias, norm_gain=norm_gain, norm_bias=norm_bias, group_table=group_table, cotangent=cotangent)


RELAX_ALPHA = 32.0
NORM_EPSILON = 1e-05
MASKED_SCORE = -1000000000.0
PRECISE = lax.Precision.HIGHEST

@jax.custom_vjp
def low(v):
    return lax.optimization_barrier(v.astype(jnp.bfloat16)).astype(jnp.float32)

@jax.custom_vjp
def low_back(v):
    return v

def low_keep(v):
    return (low(v), None)

def low_pass(kept, grad):
    return (grad,)

def back_keep(v):
    return (v, None)

def back_low(kept, grad):
    return (low(grad),)
low.defvjp(low_keep, low_pass)
low_back.defvjp(back_keep, back_low)

def product(left, right):
    return jnp.dot(left, right, precision=PRECISE, preferred_element_type=jnp.float32)

def layer_norm(inputs, gain_row, shift_row):
    centred = inputs - lax.optimization_barrier(jnp.mean(inputs, axis=-1, keepdims=True))
    factor = lax.rsqrt(lax.optimization_barrier(jnp.mean(centred * centred, axis=-1, keepdims=True)) + NORM_EPSILON)
    return centred * factor * gain_row + shift_row

def one_sequence(params, seq_tokens, seq_groups, length):
    qkv_w, qv_b, out_w, out_b, up_w, up_b, down_w, down_b, gains, shifts, table = params
    residual = seq_tokens + table[seq_groups]
    normed = low(layer_norm(residual, gains[0], shifts[0]))
    factor = 1.0 / (RELAX_ALPHA * math.sqrt(HEAD_DIM))
    head_shape = (SEQ_LEN, HEADS, HEAD_DIM)
    queries = low(low_back(product(normed, qkv_w[0]) + qv_b[0]) * factor).reshape(head_shape)
    keys = low(low_back(product(normed, qkv_w[1]))).reshape(head_shape)
    values = low(low_back(product(normed, qkv_w[2]) + qv_b[1])).reshape(head_shape)
    scores = low_back(jnp.einsum('qhd,khd->hqk', queries, keys, precision=PRECISE))
    row_ids = lax.broadcasted_iota(jnp.int32, (SEQ_LEN, SEQ_LEN), 0)
    columns = lax.broadcasted_iota(jnp.int32, (SEQ_LEN, SEQ_LEN), 1)
    visible = (columns <= row_ids) & (columns < length)
    scores = jnp.where(visible[None], scores, MASKED_SCORE)
    row_top = lax.optimization_barrier(jnp.max(scores, axis=-1, keepdims=True))
    exponent = jnp.exp((scores - row_top) * RELAX_ALPHA)
    probs_low = low(exponent / lax.optimization_barrier(jnp.sum(exponent, axis=-1, keepdims=True)))
    attended = jnp.einsum('hqk,khd->qhd', probs_low, values, precision=PRECISE).reshape(SEQ_LEN, D)
    attended = low(low_back(attended))
    branch = low_back(product(attended, out_w) + out_b)
    middle = residual + layer_norm(branch, gains[1], shifts[1])
    mid_normed = low(layer_norm(middle, gains[2], shifts[2]))
    pre_act = low_back(product(mid_normed, up_w) + up_b)
    activated = low(jax.nn.gelu(pre_act))
    ffn_out = low_back(product(activated, down_w) + down_b)
    return middle + layer_norm(ffn_out, gains[3], shifts[3])

def reference(tokens, groups, lengths, qkv_weight, qv_bias, out_weight, out_bias, up_weight, up_bias, down_weight, down_bias, norm_gain, norm_bias, group_table, cotangent):
    params = tuple((param.astype(jnp.float32) for param in (qkv_weight, qv_bias, out_weight, out_bias, up_weight, up_bias, down_weight, down_bias, norm_gain, norm_bias, group_table)))

    def forward(inputs, weights):

        def scan_step(carried, seq_item):
            seq_tokens, seq_groups, seq_length = seq_item
            return (carried, jax.checkpoint(one_sequence)(weights, seq_tokens, seq_groups, seq_length))
        carried, results = lax.scan(scan_step, None, (inputs.reshape(SEQS, SEQ_LEN, D), groups.reshape(SEQS, SEQ_LEN), lengths))
        return results.reshape(TOKENS, D)
    result, pullback = jax.vjp(forward, tokens.astype(jnp.float32), params)
    input_grad, grads = pullback(cotangent.astype(jnp.float32))
    qkv_g, qv_g, outw_g, outb_g, upw_g, upb_g, downw_g, downb_g, gain_g, bias_g, table_g = grads
    return (result.astype(jnp.bfloat16), input_grad, qkv_g, qv_g, outw_g, outb_g, upw_g, upb_g, downw_g, downb_g, gain_g, bias_g, table_g)
```

```python
import functools
import math

import jax
import jax.numpy as jnp
from jax import lax
from jax.experimental import pallas as pl
from jax.experimental.pallas import tpu as pltpu
from jax.sharding import PartitionSpec as P

HEAD_DIM = 64
SEQ_LEN = 1088
RELAX_ALPHA = 32.0
NORM_EPSILON = 1e-05
MASKED_SCORE = -1000000000.0
PRECISE = lax.Precision.HIGHEST
BF16 = jnp.bfloat16
F32 = jnp.float32
LANES = 128


def swap(value, axis, mask):
    count = lax.axis_size(axis)
    return lax.ppermute(value, axis, [(i, i ^ mask) for i in range(count)])


def norm_forward(inputs, gain_row, shift_row):
    centred = inputs - jnp.mean(inputs, axis=-1, keepdims=True)
    factor = lax.rsqrt(jnp.mean(centred * centred, axis=-1, keepdims=True) + NORM_EPSILON)
    normal = centred * factor
    return (normal * gain_row + shift_row, normal, factor)


def norm_backward(upstream, normal, factor, gain_row):
    scaled = upstream * gain_row
    adjusted = (
        scaled
        - jnp.mean(scaled, axis=-1, keepdims=True)
        - normal * jnp.mean(scaled * normal, axis=-1, keepdims=True)
    )
    return (adjusted * factor, jnp.sum(upstream * normal, axis=0), jnp.sum(upstream, axis=0))


def dot_nn(a, b):
    return lax.dot_general(a, b, (((1,), (0,)), ((), ())), preferred_element_type=F32)


def dot_nt(a, b):
    return lax.dot_general(a, b, (((1,), (1,)), ((), ())), preferred_element_type=F32)


def dot_tn(a, b):
    return lax.dot_general(a, b, (((0,), (0,)), ((), ())), preferred_element_type=F32)


def query_tile(rows):
    return rows // 2 if (rows // 2) % 16 == 0 else rows


def attend_kernel(blocks, rows, q_ref, k_ref, v_ref, kc_ref, out_ref, aug_ref):
    tile = query_tile(rows)
    lane = lax.broadcasted_iota(jnp.int32, (1, LANES), 1)
    first = lane < HEAD_DIM
    k_pair, v_pair, k_const = k_ref[...], v_ref[...], kc_ref[...]
    q_pair = q_ref[...]
    outs = []
    augs = []
    for head in range(2):
        mine = first if head == 0 else jnp.logical_not(first)
        special = lane == (HEAD_DIM if head == 0 else 0)
        keys = jnp.where(mine, k_pair, k_const)
        queries = jnp.where(mine, q_pair, jnp.where(special, 1.0, 0.0).astype(BF16))
        head_out = []
        head_aug = []
        for start in range(0, rows, tile):
            reach = start + tile
            q_tile = queries[start:reach]
            own = dot_nt(q_tile, keys[:reach])
            row_ids = start + lax.broadcasted_iota(jnp.int32, (tile, reach), 0)
            columns = lax.broadcasted_iota(jnp.int32, (tile, reach), 1)
            pieces = [jnp.where(columns <= row_ids, own, MASKED_SCORE)]
            for block in range(1, blocks):
                pieces.append(dot_nt(q_tile, keys[block * rows : (block + 1) * rows]))
            top = functools.reduce(
                jnp.maximum, [jnp.max(piece, axis=-1, keepdims=True) for piece in pieces]
            )
            total = jnp.zeros((tile, 1), F32)
            gathered = jnp.zeros((tile, LANES), F32)
            for block, piece in enumerate(pieces):
                exponent = jnp.exp(piece - top)
                total = total + jnp.sum(exponent, axis=-1, keepdims=True)
                span = v_pair[:reach] if block == 0 else v_pair[block * rows : (block + 1) * rows]
                gathered = gathered + dot_nn(exponent.astype(BF16), span)
            head_out.append(gathered / total)
            log_sum = -(top + jnp.log(total))
            high = log_sum.astype(BF16)
            rest = log_sum - high.astype(F32)
            mid = rest.astype(BF16)
            low = (rest - mid.astype(F32)).astype(BF16)
            zero = jnp.zeros((tile, LANES), BF16)
            spot = lane % HEAD_DIM
            aug = jnp.where(spot == 0, jnp.ones_like(zero), zero)
            aug = jnp.where(spot == 1, high, aug)
            aug = jnp.where(spot == 2, mid, aug)
            aug = jnp.where(spot == 3, low, aug)
            head_aug.append(aug)
        outs.append(head_out)
        augs.append(head_aug)
    for index, start in enumerate(range(0, rows, tile)):
        out_ref[start : start + tile, :] = jnp.where(
            first, outs[0][index], outs[1][index]
        ).astype(BF16)
        aug_ref[start : start + tile, :] = jnp.where(first, augs[1][index], augs[0][index])


def attend(queries, keys, values, key_const):
    rows, width = queries.shape
    span = keys.shape[0]
    pair = lambda count: pl.BlockSpec((count, LANES), lambda i: (0, i))
    return pl.pallas_call(
        functools.partial(attend_kernel, span // rows, rows),
        grid=(width // LANES,),
        in_specs=[
            pair(rows),
            pair(span),
            pair(span),
            pl.BlockSpec((span, LANES), lambda i: (0, 0)),
        ],
        out_specs=[pair(rows), pair(rows)],
        out_shape=[
            jax.ShapeDtypeStruct((rows, width), BF16),
            jax.ShapeDtypeStruct((rows, width), BF16),
        ],
        name="attend",
        compiler_params=pltpu.CompilerParams(vmem_limit_bytes=40 << 20),
        cost_estimate=pl.CostEstimate(
            flops=16 * rows * span * width,
            bytes_accessed=2 * width * (3 * rows + 2 * span),
            transcendentals=rows * span * width // HEAD_DIM,
        ),
    )(queries, keys, values, key_const)


def attend_back_kernel(
    blocks, rows, q_ref, k_ref, v_ref, kc_ref, aug_ref, go_ref, out_ref, dq_ref, dk_ref, dv_ref
):
    key_tile = query_tile(rows)
    lane = lax.broadcasted_iota(jnp.int32, (1, LANES), 1)
    first = lane < HEAD_DIM
    spot = lane % HEAD_DIM
    k_pair, v_pair, k_const = k_ref[...], v_ref[...], kc_ref[...]
    q_pair, aug, go_pair = q_ref[...], aug_ref[...], go_ref[...]
    weighed = go_pair.astype(F32) * out_ref[...].astype(F32)
    v_const = jnp.where((spot >= 1) & (spot <= 3), 1.0, 0.0).astype(BF16)
    grads_q = []
    grads_k = []
    grads_v = []
    for head in range(2):
        mine = first if head == 0 else jnp.logical_not(first)
        keys = jnp.where(mine, k_pair, k_const)
        queries = jnp.where(mine, q_pair, aug)
        values = jnp.where(mine, v_pair, v_const)
        delta = -jnp.sum(jnp.where(mine, weighed, 0.0), axis=-1, keepdims=True)
        high = delta.astype(BF16)
        rest = delta - high.astype(F32)
        mid = rest.astype(BF16)
        low = (rest - mid.astype(F32)).astype(BF16)
        go_aug = jnp.where(spot == 1, high, jnp.zeros((rows, LANES), BF16))
        go_aug = jnp.where(spot == 2, mid, go_aug)
        go_aug = jnp.where(spot == 3, low, go_aug)
        grads = jnp.where(mine, go_pair, go_aug)
        grad_q = jnp.zeros((rows, LANES), F32)
        head_k = []
        head_v = []
        for start in range(0, blocks * rows, key_tile):
            stop = start + key_tile
            scores = dot_nt(keys[start:stop], queries)
            exact = jnp.exp(scores)
            if start < rows:
                key_ids = start + lax.broadcasted_iota(jnp.int32, (key_tile, rows), 0)
                query_ids = lax.broadcasted_iota(jnp.int32, (key_tile, rows), 1)
                exact = jnp.where(key_ids <= query_ids, exact, 0.0)
            centred = dot_nt(values[start:stop], grads)
            grad_scores = (exact * centred).astype(BF16)
            head_v.append(dot_nn(exact.astype(BF16), go_pair))
            head_k.append(dot_nn(grad_scores, q_pair))
            grad_q = grad_q + dot_tn(grad_scores, k_pair[start:stop])
        grads_q.append(grad_q)
        grads_k.append(head_k)
        grads_v.append(head_v)
    dq_ref[...] = (jnp.where(first, grads_q[0], grads_q[1]) * 0.125).astype(BF16)
    for index, start in enumerate(range(0, blocks * rows, key_tile)):
        dk_ref[start : start + key_tile, :] = jnp.where(
            first, grads_k[0][index], grads_k[1][index]
        ).astype(BF16)
        dv_ref[start : start + key_tile, :] = jnp.where(
            first, grads_v[0][index], grads_v[1][index]
        ).astype(BF16)


def attend_back(queries, keys, values, key_const, aug, grad_out, out):
    rows, width = queries.shape
    span = keys.shape[0]
    pair = lambda count: pl.BlockSpec((count, LANES), lambda i: (0, i))
    return pl.pallas_call(
        functools.partial(attend_back_kernel, span // rows, rows),
        grid=(width // LANES,),
        in_specs=[
            pair(rows),
            pair(span),
            pair(span),
            pl.BlockSpec((span, LANES), lambda i: (0, 0)),
            pair(rows),
            pair(rows),
            pair(rows),
        ],
        out_specs=[pair(rows), pair(span), pair(span)],
        out_shape=[
            jax.ShapeDtypeStruct((rows, width), BF16),
            jax.ShapeDtypeStruct((span, width), BF16),
            jax.ShapeDtypeStruct((span, width), BF16),
        ],
        name="attend_back",
        compiler_params=pltpu.CompilerParams(vmem_limit_bytes=48 << 20),
        cost_estimate=pl.CostEstimate(
            flops=40 * rows * span * width,
            bytes_accessed=2 * width * (5 * rows + 4 * span),
            transcendentals=rows * span * width // HEAD_DIM,
        ),
    )(queries, keys, values, key_const, aug, grad_out, out)


def chip_masks(dp):
    bits = dp.bit_length() - 2
    low = bits // 2
    along_x = [2 << i for i in range(low)]
    along_y = [2 << i for i in range(low, bits)]
    return along_x, along_y


def pack(weight):
    width, full = weight.shape
    if width == full:
        return weight
    return weight.reshape(width, full // width, width).transpose(1, 0, 2).reshape(full, width)


def spread(own):
    along_x, along_y = chip_masks(lax.axis_size("dp"))
    found = []
    for half, order in zip(own, (along_x + along_y, along_y + along_x)):
        masks, held = [0], half[None]
        arrays = []
        for step, mask in enumerate(order):
            got = swap(held, "dp", mask)
            got_masks = [m ^ mask for m in masks]
            if step + 1 < len(order):
                held = jnp.concatenate([held, got], axis=0)
                masks = masks + got_masks
            else:
                arrays += [(masks, held), (got_masks, got)]
        if not order:
            arrays = [(masks, held)]
        arrays += [([m ^ 1 for m in masks], swap(held, "dp", 1)) for masks, held in arrays]
        found.append(arrays)
    return found


def place_kernel(plan, counts, scal_ref, *refs):
    n_in, n_out = counts
    ins, outs, sems = refs[:n_in], refs[n_in : n_in + n_out], refs[n_in + n_out]
    device = scal_ref[0]
    copies = [
        pltpu.make_async_copy(source(ins), target(outs, device), sems.at[index])
        for index, (source, target) in enumerate(plan)
    ]
    for copy in copies:
        copy.start()
    for copy in copies:
        copy.wait()


def place(plan, inputs, out_shapes, device, name):
    return pl.pallas_call(
        functools.partial(place_kernel, plan, (len(inputs), len(out_shapes))),
        grid_spec=pltpu.PrefetchScalarGridSpec(
            num_scalar_prefetch=1,
            grid=(),
            in_specs=[pl.BlockSpec(memory_space=pl.ANY)] * len(inputs),
            out_specs=[pl.BlockSpec(memory_space=pltpu.VMEM)] * len(out_shapes),
            scratch_shapes=[pltpu.SemaphoreType.DMA((len(plan),))],
        ),
        out_shape=out_shapes,
        name=name,
        compiler_params=pltpu.CompilerParams(vmem_limit_bytes=40 << 20),
        cost_estimate=pl.CostEstimate(
            flops=0,
            transcendentals=0,
            bytes_accessed=2 * sum(math.prod(s.shape) * 2 for s in out_shapes),
        ),
    )(device.reshape(1), *inputs)


def position(device, mask, dp):
    other = device ^ mask
    return (other & 1) * (dp // 2) + (other >> 1)


def gather_group(parts, kinds, device, name):
    dp, mp = lax.axis_size("dp"), lax.axis_size("mp")
    full, width = parts[0].shape
    rows = full // dp
    half = len(parts) // 2
    stacked = jnp.stack(
        [
            lax.dynamic_slice_in_dim(part, position(device, 0, dp) * rows, rows, axis=0)
            for part in parts
        ]
    )
    across = jnp.stack([swap(stacked, "mp", r) for r in range(1, mp)])
    found = spread((across[:, :half], across[:, half:]))
    inputs = list(parts)
    plan = []

    def target_of(which, kind, r, start, count):
        def target(outs, device):
            begin = start(device)
            if kind == "c":
                return outs[which].at[pl.ds(begin, count), pl.ds(r * width, width)]
            if count == full:
                raise ValueError
            block = begin // width
            return outs[which].at[
                pl.ds(pl.multiple_of(r * width + begin % width, count), count),
                pl.ds(pl.multiple_of(block * width, width), width),
            ]

        return target

    for which, kind in enumerate(kinds):
        if kind == "c":
            plan.append(
                (
                    lambda ins, which=which: ins[which],
                    lambda outs, device, which=which: outs[which].at[:, pl.ds(0, width)],
                )
            )
        else:
            for block in range(full // width):
                plan.append(
                    (
                        lambda ins, which=which, block=block: ins[which].at[
                            pl.ds(block * width, width), :
                        ],
                        lambda outs, device, which=which, block=block: outs[which].at[
                            pl.ds(0, width), pl.ds(block * width, width)
                        ],
                    )
                )
    for side, arrays in enumerate(found):
        for masks, held in arrays:
            spot = len(inputs)
            inputs.append(held)
            for index, mask in enumerate(masks):
                for r in range(1, mp):
                    for inner in range(half):
                        which = side * half + inner
                        start = lambda device, mask=mask: pl.multiple_of(
                            position(device, mask, dp) * rows, rows
                        )
                        plan.append(
                            (
                                lambda ins, spot=spot, index=index, r=r, inner=inner: ins[
                                    spot
                                ].at[index, r - 1, inner],
                                target_of(which, kinds[which], r, start, rows),
                            )
                        )
    shapes = [
        jax.ShapeDtypeStruct((full, mp * width) if kind == "c" else (mp * width, full), BF16)
        for kind in kinds
    ]
    return place(plan, inputs, shapes, device, name)


def halve(value, axis, bit):
    return (
        lax.dynamic_index_in_dim(value, 1 - bit, axis, keepdims=False),
        lax.dynamic_index_in_dim(value, bit, axis, keepdims=False),
    )


def sum_chips(value, order, device):
    lead, quarters, rows, columns = value.shape
    bits = quarters.bit_length() - 1
    value = value.reshape((lead,) + (2,) * bits + (rows, columns))
    left = list(range(bits - 1, -1, -1))
    for mask in order:
        which = mask.bit_length() - 2
        axis = 1 + left.index(which)
        left.remove(which)
        send, keep = halve(value, axis, (device >> (which + 1)) & 1)
        got = swap(send, "dp", mask)
        value = (keep.astype(F32) + got.astype(F32)).astype(BF16)
    return value.reshape(lead, rows, columns)


def sum_layers(pieces):
    total = pieces[0].astype(F32)
    for r in range(1, len(pieces)):
        total = total + swap(pieces[r], "mp", r).astype(F32)
    return total.astype(BF16)


def fill(shape, arrays, where):
    out = jnp.zeros(shape, F32)
    for masks, held in arrays:
        for index, mask in enumerate(masks):
            out = lax.dynamic_update_slice(out, held[index].astype(F32), where(mask))
    return out


def sum_small(value):
    for mask in [1 << i for i in range(lax.axis_size("dp").bit_length() - 1)]:
        value = value + swap(value, "dp", mask)
    for mask in [1 << i for i in range(lax.axis_size("mp").bit_length() - 1)]:
        value = value + swap(value, "mp", mask)
    return value


def on_device(
    tokens,
    groups,
    lengths,
    qkv_weight,
    qv_bias,
    out_weight,
    out_bias,
    up_weight,
    up_bias,
    down_weight,
    down_bias,
    norm_gain,
    norm_bias,
    group_table,
    cotangent,
):
    dp, mp = lax.axis_size("dp"), lax.axis_size("mp")
    device, layer = lax.axis_index("dp"), lax.axis_index("mp")
    core = device & 1
    rows, full = tokens.shape
    width = qkv_weight.shape[2]
    hidden = up_weight.shape[1]
    blocks = SEQ_LEN // rows
    place_in_seq = layer % blocks
    length = lax.dynamic_index_in_dim(lengths, layer // blocks, keepdims=False)
    along_x, along_y = chip_masks(dp)
    quarters = dp // 2
    gains = norm_gain.astype(F32)
    shifts = norm_bias.astype(F32)

    wq, wk, wv, wo = gather_group(
        [qkv_weight[0], qkv_weight[1], qkv_weight[2], pack(out_weight)],
        "cccr",
        device,
        "place_attention",
    )
    w_up, w_down = gather_group([up_weight, pack(down_weight)], "cr", device, "place_ffn")
    order_of = layer ^ jnp.arange(mp)
    small_here = jnp.concatenate([qv_bias[0], qv_bias[1], up_bias])
    small_all = jnp.stack([small_here] + [swap(small_here, "mp", r) for r in range(1, mp)])
    small_all = small_all.astype(F32)
    q_bias = small_all[:, :width].reshape(-1)
    v_bias = small_all[:, width : 2 * width].reshape(-1)
    u_bias = small_all[:, 2 * width :].reshape(-1)

    onehot = (
        groups[:, None] == lax.broadcasted_iota(jnp.int32, (1, group_table.shape[0]), 1)
    ).astype(BF16)
    residual = tokens.astype(F32) + jnp.dot(onehot, group_table, preferred_element_type=F32)
    normed, norm_one, inv_one = norm_forward(residual, gains[0], shifts[0])
    normed_low = normed.astype(BF16)
    seq_normed = jnp.concatenate(
        [normed_low] + [swap(normed_low, "mp", m) for m in range(1, blocks)], axis=0
    )
    factor = 1.0 / math.sqrt(HEAD_DIM) / RELAX_ALPHA
    queries = (((dot_nn(normed_low, wq) + q_bias) * factor).astype(BF16) * RELAX_ALPHA).astype(BF16)
    keys = dot_nn(seq_normed, wk).astype(BF16)
    values = (dot_nn(seq_normed, wv) + v_bias).astype(BF16)

    key_ids = lax.broadcasted_iota(jnp.int32, (blocks, rows, 1), 1)
    block_ids = place_in_seq ^ lax.broadcasted_iota(jnp.int32, (blocks, rows, 1), 0)
    shown = (block_ids <= place_in_seq) & (block_ids * rows + key_ids < length)
    spot = lax.broadcasted_iota(jnp.int32, (blocks, rows, LANES), 2) % HEAD_DIM
    key_const = jnp.where(
        spot == 0,
        jnp.where(shown, 0.0, MASKED_SCORE),
        jnp.where(spot <= 3, 1.0, 0.0),
    )
    key_const = key_const.astype(BF16).reshape(blocks * rows, LANES)
    attended, aug = attend(queries, keys, values, key_const)

    branch = dot_nn(attended, wo) + out_bias.astype(F32)
    branch_out, norm_two, inv_two = norm_forward(branch, gains[1], shifts[1])
    middle = residual + branch_out
    mid_normed, norm_three, inv_three = norm_forward(middle, gains[2], shifts[2])
    mid_low = mid_normed.astype(BF16)
    pre_act = dot_nn(mid_low, w_up) + u_bias
    activated, gelu_pull = jax.vjp(jax.nn.gelu, pre_act)
    activated_low = activated.astype(BF16)
    ffn_out = dot_nn(activated_low, w_down) + down_bias.astype(F32)
    ffn_normed, norm_four, inv_four = norm_forward(ffn_out, gains[3], shifts[3])
    output = (middle + ffn_normed).astype(BF16)

    upstream = cotangent.astype(F32)
    grad_ffn, gain_four, shift_four = norm_backward(upstream, norm_four, inv_four, gains[3])
    grad_ffn_low = grad_ffn.astype(BF16)
    down_bias_part = jnp.sum(grad_ffn_low.astype(F32), axis=0)
    half = full // 2

    def split(value):
        return (
            lax.dynamic_slice_in_dim(value, (1 - core) * half, half, axis=1),
            lax.dynamic_slice_in_dim(value, core * half, half, axis=1),
        )

    def both_cores(send, keep):
        return (keep() + swap(send().astype(BF16), "dp", 1).astype(F32)).astype(BF16)

    gf_send, gf_keep = split(grad_ffn_low)
    down_sum = both_cores(
        lambda: dot_tn(activated_low, gf_send), lambda: dot_tn(activated_low, gf_keep)
    ).reshape(mp, quarters, hidden // quarters, half)
    grad_act = dot_nt(grad_ffn_low, w_down)
    (grad_pre,) = gelu_pull(grad_act)
    grad_pre_low = grad_pre.astype(BF16)
    up_bias_part = jnp.sum(grad_pre_low.astype(F32), axis=0)
    mid_send, mid_keep = split(mid_low)
    up_sum = both_cores(
        lambda: dot_tn(mid_send, grad_pre_low), lambda: dot_tn(mid_keep, grad_pre_low)
    ).reshape(1, quarters, half // quarters, mp * hidden)
    down_piece = sum_chips(down_sum, along_x + along_y, device)
    up_piece = sum_chips(up_sum, along_y + along_x, device)[0]
    down_mine = sum_layers([down_piece[r] for r in range(mp)])
    up_mine = sum_layers([up_piece[:, r * hidden : (r + 1) * hidden] for r in range(mp)])
    up_all, down_all = spread((up_mine, down_mine))

    def quarter_of(mask):
        return (device ^ mask) >> 1

    def core_of(mask):
        return (device ^ mask) & 1

    up_rows = half // quarters
    up_grad = fill(
        (full, hidden), up_all, lambda m: (core_of(m) * half + quarter_of(m) * up_rows, 0)
    )
    down_rows = hidden // quarters
    down_grad = fill(
        (hidden, full), down_all, lambda m: (quarter_of(m) * down_rows, core_of(m) * half)
    )

    grad_mid = dot_nt(grad_pre_low, w_up)
    back_three, gain_three, shift_three = norm_backward(grad_mid, norm_three, inv_three, gains[2])
    grad_middle = upstream + back_three
    grad_branch, gain_two, shift_two = norm_backward(grad_middle, norm_two, inv_two, gains[1])
    grad_branch_low = grad_branch.astype(BF16)
    out_bias_part = jnp.sum(grad_branch_low.astype(F32), axis=0)
    gb_send, gb_keep = split(grad_branch_low)
    out_sum = both_cores(
        lambda: dot_tn(attended, gb_send), lambda: dot_tn(attended, gb_keep)
    ).reshape(mp, quarters, width // quarters, half)
    grad_attended = dot_nt(grad_branch_low, wo).astype(BF16)
    grad_q, grad_k, grad_v = attend_back(
        queries, keys, values, key_const, aug, grad_attended, attended
    )
    q_bias_part = jnp.sum(grad_q.astype(F32), axis=0)
    v_bias_part = jnp.sum(grad_v.astype(F32), axis=0)
    grad_seq = dot_nt(grad_k, wk) + dot_nt(grad_v, wv)
    grad_normed = dot_nt(grad_q, wq) + grad_seq[:rows]
    for m in range(1, blocks):
        grad_normed = grad_normed + swap(
            grad_seq[m * rows : (m + 1) * rows].astype(BF16), "mp", m
        ).astype(F32)
    seq_send, seq_keep = split(seq_normed)
    qkv_sum = both_cores(
        lambda: jnp.concatenate(
            [dot_tn(seq_send[:rows], grad_q), dot_tn(seq_send, grad_k), dot_tn(seq_send, grad_v)],
            axis=1,
        ),
        lambda: jnp.concatenate(
            [dot_tn(seq_keep[:rows], grad_q), dot_tn(seq_keep, grad_k), dot_tn(seq_keep, grad_v)],
            axis=1,
        ),
    ).reshape(1, quarters, half // quarters, 3 * full)
    out_piece = sum_chips(out_sum, along_x + along_y, device)
    qkv_piece = sum_chips(qkv_sum, along_y + along_x, device)[0]
    out_mine = sum_layers([out_piece[r] for r in range(mp)])
    qkv_mine = sum_layers(
        [
            jnp.stack(
                [
                    qkv_piece[:, c * full + r * width : c * full + (r + 1) * width]
                    for c in range(3)
                ]
            )
            for r in range(mp)
        ]
    )
    qkv_all, out_all = spread((qkv_mine, out_mine))
    qkv_grad = fill(
        (3, full, width), qkv_all, lambda m: (0, core_of(m) * half + quarter_of(m) * up_rows, 0)
    )
    out_rows = width // quarters
    out_grad = fill(
        (width, full), out_all, lambda m: (quarter_of(m) * out_rows, core_of(m) * half)
    )

    back_one, gain_one, shift_one = norm_backward(grad_normed, norm_one, inv_one, gains[0])
    input_grad = grad_middle + back_one
    table_part = jnp.dot(
        onehot.astype(F32).T, input_grad, precision=PRECISE, preferred_element_type=F32
    )
    by_layer = jnp.concatenate(
        [q_bias_part.reshape(mp, -1), v_bias_part.reshape(mp, -1), up_bias_part.reshape(mp, -1)],
        axis=1,
    )
    by_layer = jnp.take(by_layer, order_of, axis=0)
    wide = by_layer.shape[1]
    by_layer = jnp.pad(by_layer, ((0, 0), (0, -wide % full))).reshape(-1, full)
    parts = jnp.concatenate(
        [
            jnp.stack([gain_one, gain_two, gain_three, gain_four]),
            jnp.stack([shift_one, shift_two, shift_three, shift_four]),
            jnp.stack([out_bias_part, down_bias_part]),
            table_part,
            by_layer,
        ]
    )
    parts = sum_small(parts)
    gain_grad, shift_grad = parts[:4], parts[4:8]
    out_bias_grad, down_bias_grad = parts[8], parts[9]
    n_groups = group_table.shape[0]
    table_grad = parts[10 : 10 + n_groups]
    by_layer = parts[10 + n_groups :].reshape(mp, -1)
    mine = lax.dynamic_index_in_dim(by_layer, layer, keepdims=False)
    qv_bias_grad = mine[: 2 * width].reshape(2, width)
    up_bias_grad = mine[2 * width : 2 * width + hidden]
    return (
        output,
        input_grad,
        qkv_grad,
        qv_bias_grad,
        out_grad,
        out_bias_grad,
        up_grad,
        up_bias_grad,
        down_grad,
        down_bias_grad,
        gain_grad,
        shift_grad,
        table_grad,
    )


def solution(mesh):
    placed = (
        P(("dp", "mp"), None),
        P(("dp", "mp")),
        P("dp"),
        P(None, None, "mp"),
        P(None, "mp"),
        P("mp", None),
        P(),
        P(None, "mp"),
        P("mp"),
        P("mp", None),
        P(),
        P(),
        P(),
        P(),
        P(("dp", "mp"), None),
    )
    return jax.shard_map(
        on_device,
        mesh=mesh,
        in_specs=placed,
        out_specs=(
            P(("dp", "mp"), None),
            P(("dp", "mp"), None),
            P(None, None, "mp"),
            P(None, "mp"),
            P("mp", None),
            P(),
            P(None, "mp"),
            P("mp"),
            P("mp", None),
            P(),
            P(),
            P(),
            P(),
        ),
        check_vma=False,
    )
```

```python
import functools
import math

import jax
import jax.numpy as jnp
from jax import lax
from jax.experimental import pallas as pl
from jax.experimental.pallas import tpu as pltpu
from jax.sharding import PartitionSpec as P

HEAD_DIM = 64
SEQ_LEN = 1088
RELAX_ALPHA = 32.0
NORM_EPSILON = 1e-05
MASKED_SCORE = -1000000000.0
PRECISE = lax.Precision.HIGHEST
BF16 = jnp.bfloat16
F32 = jnp.float32
LANES = 128
LIGHT = pl.CostEstimate(flops=1000, bytes_accessed=1000, transcendentals=0)


def swap(value, axis, mask):
    count = lax.axis_size(axis)
    return lax.ppermute(value, axis, [(i, i ^ mask) for i in range(count)])


def normalize(inputs):
    centred = inputs - jnp.mean(inputs, axis=-1, keepdims=True)
    factor = lax.rsqrt(jnp.mean(centred * centred, axis=-1, keepdims=True) + NORM_EPSILON)
    return centred * factor, factor


def norm_forward(inputs, gain_row, shift_row):
    centred = inputs - jnp.mean(inputs, axis=-1, keepdims=True)
    factor = lax.rsqrt(jnp.mean(centred * centred, axis=-1, keepdims=True) + NORM_EPSILON)
    normal = centred * factor
    return (normal * gain_row + shift_row, normal, factor)


def norm_backward(upstream, normal, factor, gain_row):
    scaled = upstream * gain_row
    adjusted = (
        scaled
        - jnp.mean(scaled, axis=-1, keepdims=True)
        - normal * jnp.mean(scaled * normal, axis=-1, keepdims=True)
    )
    return (adjusted * factor, jnp.sum(upstream * normal, axis=0), jnp.sum(upstream, axis=0))


def dot_nn(a, b):
    return lax.dot_general(a, b, (((1,), (0,)), ((), ())), preferred_element_type=F32)


def dot_nt(a, b):
    return lax.dot_general(a, b, (((1,), (1,)), ((), ())), preferred_element_type=F32)


def dot_tn(a, b):
    return lax.dot_general(a, b, (((0,), (0,)), ((), ())), preferred_element_type=F32)


def query_tile(rows):
    return rows // 2 if (rows // 2) % 16 == 0 else rows


def attend_kernel(blocks, rows, q_ref, k_ref, v_ref, kc_ref, out_ref, aug_ref):
    tile = query_tile(rows)
    lane = lax.broadcasted_iota(jnp.int32, (1, LANES), 1)
    first = lane < HEAD_DIM
    k_pair, v_pair, k_const = k_ref[...], v_ref[...], kc_ref[...]
    q_pair = q_ref[...]
    outs = []
    augs = []
    for head in range(2):
        mine = first if head == 0 else jnp.logical_not(first)
        special = lane == (HEAD_DIM if head == 0 else 0)
        keys = jnp.where(mine, k_pair, k_const)
        queries = jnp.where(mine, q_pair, jnp.where(special, 1.0, 0.0).astype(BF16))
        head_out = []
        head_aug = []
        for start in range(0, rows, tile):
            reach = start + tile
            q_tile = queries[start:reach]
            own = dot_nt(q_tile, keys[:reach])
            row_ids = start + lax.broadcasted_iota(jnp.int32, (tile, reach), 0)
            columns = lax.broadcasted_iota(jnp.int32, (tile, reach), 1)
            pieces = [jnp.where(columns <= row_ids, own, MASKED_SCORE)]
            for block in range(1, blocks):
                pieces.append(dot_nt(q_tile, keys[block * rows : (block + 1) * rows]))
            top = functools.reduce(
                jnp.maximum, [jnp.max(piece, axis=-1, keepdims=True) for piece in pieces]
            )
            total = jnp.zeros((tile, 1), F32)
            gathered = jnp.zeros((tile, LANES), F32)
            for block, piece in enumerate(pieces):
                exponent = jnp.exp(piece - top)
                total = total + jnp.sum(exponent, axis=-1, keepdims=True)
                span = v_pair[:reach] if block == 0 else v_pair[block * rows : (block + 1) * rows]
                gathered = gathered + dot_nn(exponent.astype(BF16), span)
            head_out.append(gathered / total)
            log_sum = -(top + jnp.log(total))
            high = log_sum.astype(BF16)
            rest = log_sum - high.astype(F32)
            mid = rest.astype(BF16)
            low = (rest - mid.astype(F32)).astype(BF16)
            zero = jnp.zeros((tile, LANES), BF16)
            spot = lane % HEAD_DIM
            aug = jnp.where(spot == 0, jnp.ones_like(zero), zero)
            aug = jnp.where(spot == 1, high, aug)
            aug = jnp.where(spot == 2, mid, aug)
            aug = jnp.where(spot == 3, low, aug)
            head_aug.append(aug)
        outs.append(head_out)
        augs.append(head_aug)
    for index, start in enumerate(range(0, rows, tile)):
        out_ref[start : start + tile, :] = jnp.where(
            first, outs[0][index], outs[1][index]
        ).astype(BF16)
        aug_ref[start : start + tile, :] = jnp.where(first, augs[1][index], augs[0][index])


def attend(queries, keys, values, key_const, begin, count):
    rows = queries.shape[0]
    span = keys.shape[0]
    first = begin // LANES
    pair = lambda height: pl.BlockSpec((height, LANES), lambda i: (0, first + i))
    made = lambda height: pl.BlockSpec((height, LANES), lambda i: (0, i))
    return pl.pallas_call(
        functools.partial(attend_kernel, span // rows, rows),
        grid=(count // LANES,),
        in_specs=[
            pair(rows),
            pair(span),
            pair(span),
            pl.BlockSpec((span, LANES), lambda i: (0, 0)),
        ],
        out_specs=[made(rows), made(rows)],
        out_shape=[
            jax.ShapeDtypeStruct((rows, count), BF16),
            jax.ShapeDtypeStruct((rows, count), BF16),
        ],
        name="attend",
        compiler_params=pltpu.CompilerParams(vmem_limit_bytes=40 << 20),
        cost_estimate=LIGHT,
    )(queries, keys, values, key_const)


def attend_back_kernel(
    blocks, rows, q_ref, k_ref, v_ref, kc_ref, aug_ref, go_ref, out_ref, dq_ref, dk_ref, dv_ref
):
    key_tile = query_tile(rows)
    lane = lax.broadcasted_iota(jnp.int32, (1, LANES), 1)
    first = lane < HEAD_DIM
    spot = lane % HEAD_DIM
    k_pair, v_pair, k_const = k_ref[...], v_ref[...], kc_ref[...]
    q_pair, aug, go_pair = q_ref[...], aug_ref[...], go_ref[...]
    weighed = go_pair.astype(F32) * out_ref[...].astype(F32)
    v_const = jnp.where((spot >= 1) & (spot <= 3), 1.0, 0.0).astype(BF16)
    grads_q = []
    grads_k = []
    grads_v = []
    for head in range(2):
        mine = first if head == 0 else jnp.logical_not(first)
        keys = jnp.where(mine, k_pair, k_const)
        queries = jnp.where(mine, q_pair, aug)
        values = jnp.where(mine, v_pair, v_const)
        delta = -jnp.sum(jnp.where(mine, weighed, 0.0), axis=-1, keepdims=True)
        high = delta.astype(BF16)
        rest = delta - high.astype(F32)
        mid = rest.astype(BF16)
        low = (rest - mid.astype(F32)).astype(BF16)
        go_aug = jnp.where(spot == 1, high, jnp.zeros((rows, LANES), BF16))
        go_aug = jnp.where(spot == 2, mid, go_aug)
        go_aug = jnp.where(spot == 3, low, go_aug)
        grads = jnp.where(mine, go_pair, go_aug)
        grad_q = jnp.zeros((rows, LANES), F32)
        head_k = []
        head_v = []
        for start in range(0, blocks * rows, key_tile):
            stop = start + key_tile
            scores = dot_nt(keys[start:stop], queries)
            exact = jnp.exp(scores)
            if start < rows:
                key_ids = start + lax.broadcasted_iota(jnp.int32, (key_tile, rows), 0)
                query_ids = lax.broadcasted_iota(jnp.int32, (key_tile, rows), 1)
                exact = jnp.where(key_ids <= query_ids, exact, 0.0)
            centred = dot_nt(values[start:stop], grads)
            grad_scores = (exact * centred).astype(BF16)
            head_v.append(dot_nn(exact.astype(BF16), go_pair))
            head_k.append(dot_nn(grad_scores, q_pair))
            grad_q = grad_q + dot_tn(grad_scores, k_pair[start:stop])
        grads_q.append(grad_q)
        grads_k.append(head_k)
        grads_v.append(head_v)
    dq_ref[...] = (jnp.where(first, grads_q[0], grads_q[1]) * 0.125).astype(BF16)
    for index, start in enumerate(range(0, blocks * rows, key_tile)):
        dk_ref[start : start + key_tile, :] = jnp.where(
            first, grads_k[0][index], grads_k[1][index]
        ).astype(BF16)
        dv_ref[start : start + key_tile, :] = jnp.where(
            first, grads_v[0][index], grads_v[1][index]
        ).astype(BF16)


def attend_back(queries, keys, values, key_const, aug, grad_out, out, begin):
    rows = queries.shape[0]
    count = aug.shape[1]
    span = keys.shape[0]
    first = begin // LANES
    pair = lambda height: pl.BlockSpec((height, LANES), lambda i: (0, first + i))
    made = lambda height: pl.BlockSpec((height, LANES), lambda i: (0, i))
    return pl.pallas_call(
        functools.partial(attend_back_kernel, span // rows, rows),
        grid=(count // LANES,),
        in_specs=[
            pair(rows),
            pair(span),
            pair(span),
            pl.BlockSpec((span, LANES), lambda i: (0, 0)),
            made(rows),
            pair(rows),
            made(rows),
        ],
        out_specs=[made(rows), made(span), made(span)],
        out_shape=[
            jax.ShapeDtypeStruct((rows, count), BF16),
            jax.ShapeDtypeStruct((span, count), BF16),
            jax.ShapeDtypeStruct((span, count), BF16),
        ],
        name="attend_back",
        compiler_params=pltpu.CompilerParams(vmem_limit_bytes=48 << 20),
        cost_estimate=LIGHT,
    )(queries, keys, values, key_const, aug, grad_out, out)


def chip_masks(dp):
    bits = dp.bit_length() - 2
    low = bits // 2
    along_x = [2 << i for i in range(low)]
    along_y = [2 << i for i in range(low, bits)]
    return along_x, along_y


def position(device, mask, dp):
    other = device ^ mask
    return (other & 1) * (dp // 2) + (other >> 1)


def own_slice(weight, by_rows, device, width):
    dp = lax.axis_size("dp")
    if by_rows:
        full = weight.shape[1]
        start = position(device, 0, dp) * (full // dp)
        piece = lax.dynamic_slice(weight, (start % width, start // width * width), (full // dp, width))
        return piece[None]
    rows = weight.shape[1] // dp
    return lax.dynamic_slice_in_dim(weight, position(device, 0, dp) * rows, rows, axis=1)


class Flow:
    def __init__(self, steps):
        self.steps = steps
        self.result = None
        self.over = False
        self.held = None
        self.move(None)

    def move(self, value):
        try:
            self.held = self.steps.send(value)
        except StopIteration as stop:
            self.result, self.over, self.held = stop.value, True, None


def ordered(flows, values):
    live = [flow for flow in flows if not flow.over]
    values, held = lax.optimization_barrier((values, [flow.held for flow in live]))
    for flow, item in zip(live, held):
        flow.move(item)
    return values


def begin(flows, *values):
    values = ordered(flows, values)
    return values if len(values) > 1 else values[0]


def meet(flows, *values):
    values = ordered(flows, values)
    return begin(flows, *values)


def layer_steps(value):
    mp = lax.axis_size("mp")
    got = {0: value}
    for count in range(1, mp.bit_length()):
        ranks = [r for r in range(mp) if r.bit_count() == count]
        sent = [got[r & (r - 1)] for r in ranks]
        if count > 1:
            sent = yield tuple(sent)
        found = yield tuple(swap(item, "mp", r & -r) for r, item in zip(ranks, sent))
        got.update(zip(ranks, found))
    return [got[r] for r in range(mp)]


def spread_steps(sides):
    along_x, along_y = chip_masks(lax.axis_size("dp"))
    orders = (along_x + along_y, along_y + along_x)
    masks = [[0], [0]]
    held = [side[None] for side in sides]
    arrays = []
    for step in range(len(along_x + along_y)):
        held = yield tuple(held)
        got = yield tuple(swap(value, "dp", order[step]) for value, order in zip(held, orders))
        for side, order in enumerate(orders):
            moved = [m ^ order[step] for m in masks[side]]
            if step + 1 < len(order):
                masks[side] = masks[side] + moved
            else:
                arrays += [(side, masks[side], held[side]), (side, moved, got[side])]
        held = [jnp.concatenate([one, two], axis=0) for one, two in zip(held, got)]
    own = yield tuple(value for _, _, value in arrays)
    other = yield tuple(swap(value, "dp", 1) for value in own)
    return [(side, m, value) for (side, m, _), value in zip(arrays, own)] + [
        (side, [k ^ 1 for k in m], value) for (side, m, _), value in zip(arrays, other)
    ]


def gather_flow(stacked, extra=None):
    count, rows, width = stacked.shape
    flat = stacked.reshape(count * rows, width)
    if extra is not None:
        flat = jnp.concatenate([flat, extra], axis=0)
    (flat,) = yield (flat,)
    found = yield from layer_steps(flat)
    across = jnp.stack([item[: count * rows].reshape(count, rows, width) for item in found[1:]])
    half = rows // 2
    arrays = yield from spread_steps((across[:, :, :half], across[:, :, half:]))
    return arrays, [item[count * rows :] for item in found]


class Weights:
    def __init__(self, own, arrays):
        self.own, self.arrays = own, arrays
        sample = arrays[0][2]
        self.full, self.width = sample.shape[3] * 2 * lax.axis_size("dp"), sample.shape[4]
        self.inputs = [shard for shard, _, _ in own] + [value for _, _, value in arrays]
        self.n_own = len(own)

    def specs(self):
        return [pl.BlockSpec(memory_space=pl.ANY)] * len(self.inputs)

    def scratch(self, mp, which):
        count = self.full // self.width + (mp - 1) * sum(len(m) for _, m, _ in self.arrays)
        return [
            pltpu.VMEM((mp, len(which), self.full, self.width), BF16),
            pltpu.SemaphoreType.DMA((count + 4,)),
        ]

    def copies(self, refs, held, sems, device, mp, dp, which):
        made = [[] for _ in range(mp)]
        spot = 0

        def add(r, source, target):
            nonlocal spot
            made[r].append((source, target, sems.at[spot]))
            spot += 1

        first, last = which[0], which[-1] + 1
        for ref, (_, index, by_rows) in zip(refs, self.own):
            if by_rows and first <= index < last:
                for block in range(self.full // self.width):
                    columns = pl.ds(block * self.width, self.width)
                    add(0, ref.at[:, columns], held.at[0, index - first, columns, :])
            elif not by_rows and first == index:
                add(0, ref, held.at[0, 0 : ref.shape[0]])
        half = self.full // dp // 2
        for r in range(1, mp):
            for ref, (side, masks, _) in zip(refs[self.n_own :], self.arrays):
                for index, mask in enumerate(masks):
                    start = pl.multiple_of((position(device, mask, dp) * 2 + side) * half, half)
                    add(
                        r,
                        ref.at[index, r - 1, first:last],
                        held.at[r, :, pl.ds(start, half), :],
                    )
        return made


def start_all(copies):
    for copy in copies:
        pltpu.make_async_copy(*copy).start()


def wait_all(copies):
    for copy in copies:
        pltpu.make_async_copy(*copy).wait()


def wait_step(step, copies, begin=0):
    for r in range(begin, len(copies)):

        @pl.when(step == r)
        def _():
            wait_all(copies[r])


def tiles(count, size, body):
    if count == size:
        body(0)
    else:

        for i in range(count // size):
            body(i * size)


def row_tile(rows):
    return 272 if rows % 272 == 0 else 16


COLUMNS = 256


def column_tile(width):
    return min(COLUMNS, width)


def whole(shape):
    return pl.BlockSpec(shape, lambda i, *_: (0,) * len(shape))


def project_kernel(group, blocks, scale, scal, *refs):
    n_in = len(group.inputs)
    x_refs, bias_ref = refs[:blocks], refs[blocks]
    w_refs = refs[blocks + 1 : blocks + 1 + n_in]
    q_ref, k_ref, v_ref, held, sems = refs[blocks + 1 + n_in :]
    r = pl.program_id(0)
    mp, dp = lax.axis_size("mp"), lax.axis_size("dp")
    copies = group.copies(w_refs, held, sems, scal[0], mp, dp, [0, 1, 2])
    rows = q_ref.shape[0]

    @pl.when(r == 0)
    def _():
        start_all(sum(copies, []))

    wait_step(r, copies)

    size = column_tile(group.width)
    for begin in range(0, group.width, size):
        columns = slice(begin, begin + size)
        q = dot_nn(x_refs[0][...], held[r, 0, :, columns]) + bias_ref[0:1, columns].astype(F32)
        q_ref[:, columns] = ((q * scale).astype(BF16) * RELAX_ALPHA).astype(BF16)
        for block in range(blocks):
            x = x_refs[block][...]
            place = slice(block * rows, (block + 1) * rows)
            k_ref[place, columns] = dot_nn(x, held[r, 1, :, columns]).astype(BF16)
            v = dot_nn(x, held[r, 2, :, columns]) + bias_ref[1:2, columns].astype(F32)
            v_ref[place, columns] = v.astype(BF16)


def project(normed, biases, group, device):
    mp = lax.axis_size("mp")
    rows, full = normed[0].shape
    blocks = len(normed)
    width = group.width
    made = lambda height: pl.BlockSpec((height, width), lambda i, *_: (0, i))
    return pl.pallas_call(
        functools.partial(project_kernel, group, blocks, 1.0 / math.sqrt(HEAD_DIM) / RELAX_ALPHA),
        grid_spec=pltpu.PrefetchScalarGridSpec(
            num_scalar_prefetch=1,
            grid=(mp,),
            in_specs=[whole((rows, full))] * blocks
            + [pl.BlockSpec((8, width), lambda i, *_: (0, i))]
            + group.specs(),
            out_specs=[made(rows), made(blocks * rows), made(blocks * rows)],
            scratch_shapes=group.scratch(mp, [0, 1, 2]),
        ),
        out_shape=[
            jax.ShapeDtypeStruct((rows, full), BF16),
            jax.ShapeDtypeStruct((blocks * rows, full), BF16),
            jax.ShapeDtypeStruct((blocks * rows, full), BF16),
        ],
        name="project",
        compiler_params=pltpu.CompilerParams(vmem_limit_bytes=48 << 20),
        cost_estimate=LIGHT,
    )(device.reshape(1), *normed, biases, *group.inputs)


def up_kernel(group_a, group_u, scal, *refs):
    (att_a, att_b, residual_ref, rows_ref, bias_ref), refs = refs[:5], refs[5:]
    wa, refs = refs[: len(group_a.inputs)], refs[len(group_a.inputs) :]
    wu, refs = refs[: len(group_u.inputs)], refs[len(group_u.inputs) :]
    branch_ref, middle_ref, mid_ref, act_ref, slope_ref, held_o, sem_o, held_u, sem_u = refs
    r = pl.program_id(0)
    mp, dp = lax.axis_size("mp"), lax.axis_size("dp")
    copies_o = sum(group_a.copies(wa, held_o, sem_o, scal[0], mp, dp, [3]), [])
    copies_u = group_u.copies(wu, held_u, sem_u, scal[0], mp, dp, [0])
    rows, full = middle_ref.shape
    width = group_a.width
    part = att_a.shape[1]

    @pl.when(r == 0)
    def _():
        start_all(copies_o)
        start_all(sum(copies_u, []))
        wait_all(copies_o)
        for block in range(full // width):
            columns = slice(block * width, (block + 1) * width)
            total = jnp.zeros((rows, width), F32)
            for layer in range(mp):
                source = att_a if layer * width < part else att_b
                first = layer * width % part
                total = total + dot_nn(source[:, first : first + width], held_o[layer, 0, columns, :])
            branch_ref[:, columns] = total + rows_ref[0:1, columns]

        def norm_rows(start):
            place = pl.ds(start, row_tile(rows))
            normal, _ = normalize(branch_ref[place, :])
            middle = residual_ref[place, :] + normal * rows_ref[1:2, :] + rows_ref[2:3, :]
            middle_ref[place, :] = middle
            normal, _ = normalize(middle)
            mid_ref[place, :] = (normal * rows_ref[3:4, :] + rows_ref[4:5, :]).astype(BF16)

        tiles(rows, row_tile(rows), norm_rows)

    wait_step(r, copies_u)

    size = column_tile(group_u.width)

    def activate(start):
        columns = pl.ds(start, size)
        u = dot_nn(mid_ref[...], held_u[r, 0, :, columns]) + bias_ref[0:1, columns]
        scale = math.sqrt(2.0 / math.pi)
        square = u * u
        bent = jnp.tanh(scale * u * (1.0 + 0.044715 * square))
        lifted = 0.5 + 0.5 * bent
        act_ref[:, columns] = (u * lifted).astype(BF16)
        slope = lifted + (0.5 * scale) * u * (1.0 - bent * bent) * (
            1.0 + (3.0 * 0.044715) * square
        )
        slope_ref[:, columns] = slope.astype(BF16)

    tiles(group_u.width, size, activate)


def feed_up(att_a, att_b, residual, vectors, u_bias, group_a, group_u, device):
    mp = lax.axis_size("mp")
    rows, full = residual.shape
    hidden = group_u.width
    made = pl.BlockSpec((rows, hidden), lambda i, *_: (0, i))
    return pl.pallas_call(
        functools.partial(up_kernel, group_a, group_u),
        grid_spec=pltpu.PrefetchScalarGridSpec(
            num_scalar_prefetch=1,
            grid=(mp,),
            in_specs=[whole(att_a.shape), whole(att_b.shape), whole((rows, full)), whole((8, full))]
            + [pl.BlockSpec((8, hidden), lambda i, *_: (0, i))]
            + group_a.specs()
            + group_u.specs(),
            out_specs=[whole((rows, full)), whole((rows, full)), whole((rows, full)), made, made],
            scratch_shapes=group_a.scratch(mp, [3]) + group_u.scratch(mp, [0]),
        ),
        out_shape=[
            jax.ShapeDtypeStruct((rows, full), F32),
            jax.ShapeDtypeStruct((rows, full), F32),
            jax.ShapeDtypeStruct((rows, full), BF16),
            jax.ShapeDtypeStruct((rows, mp * hidden), BF16),
            jax.ShapeDtypeStruct((rows, mp * hidden), BF16),
        ],
        name="feed_up",
        compiler_params=pltpu.CompilerParams(vmem_limit_bytes=56 << 20),
        cost_estimate=LIGHT,
    )(
        device.reshape(1), att_a, att_b, residual, vectors, u_bias, *group_a.inputs, *group_u.inputs
    )


def down_kernel(group_d, scal, *refs):
    (act_ref, middle_ref, cot_ref, rows_ref), refs = refs[:4], refs[4:]
    wd, refs = refs[: len(group_d.inputs)], refs[len(group_d.inputs) :]
    out_ref, grad_ref, sums_ref, held, sems, total = refs
    r = pl.program_id(0)
    mp, dp = lax.axis_size("mp"), lax.axis_size("dp")
    copies = group_d.copies(wd, held, sems, scal[0], mp, dp, [0])
    rows, full = middle_ref.shape
    width = group_d.width

    @pl.when(r == 0)
    def _():
        start_all(sum(copies, []))
        total[...] = jnp.zeros_like(total)

    wait_step(r, copies)

    size = column_tile(width)
    for block in range(full // width):

        def add(start):
            columns = pl.ds(block * width + start, size)
            total[:, columns] += dot_nn(
                act_ref[...], held[r, 0, block * width : (block + 1) * width, pl.ds(start, size)]
            )

        tiles(width, size, add)

    @pl.when(r == mp - 1)
    def _():
        sums_ref[...] = jnp.zeros_like(sums_ref)

        def norm_rows(start):
            place = pl.ds(start, row_tile(rows))
            normal, factor = normalize(total[place, :] + rows_ref[0:1, :])
            gain = rows_ref[1:2, :]
            out_ref[place, :] = (
                middle_ref[place, :] + (normal * gain + rows_ref[2:3, :])
            ).astype(BF16)
            upstream = cot_ref[place, :].astype(F32)
            scaled = upstream * gain
            grad = (
                scaled
                - jnp.mean(scaled, axis=-1, keepdims=True)
                - normal * jnp.mean(scaled * normal, axis=-1, keepdims=True)
            ) * factor
            grad = grad.astype(BF16)
            grad_ref[place, :] = grad
            sums_ref[0:8, :] += fold(upstream * normal)
            sums_ref[8:16, :] += fold(upstream)
            sums_ref[16:24, :] += fold(grad.astype(F32))

        tiles(rows, row_tile(rows), norm_rows)


def fold(value):
    return functools.reduce(jnp.add, [value[i : i + 8] for i in range(0, value.shape[0], 8)])


def feed_down(act, middle, cotangent, vectors, group_d, device):
    mp = lax.axis_size("mp")
    rows, full = middle.shape
    hidden = group_d.width
    return pl.pallas_call(
        functools.partial(down_kernel, group_d),
        grid_spec=pltpu.PrefetchScalarGridSpec(
            num_scalar_prefetch=1,
            grid=(mp,),
            in_specs=[pl.BlockSpec((rows, hidden), lambda i, *_: (0, i))]
            + [whole((rows, full)), whole((rows, full)), whole((8, full))]
            + group_d.specs(),
            out_specs=[whole((rows, full)), whole((rows, full)), whole((24, full))],
            scratch_shapes=group_d.scratch(mp, [0]) + [pltpu.VMEM((rows, full), F32)],
        ),
        out_shape=[
            jax.ShapeDtypeStruct((rows, full), BF16),
            jax.ShapeDtypeStruct((rows, full), BF16),
            jax.ShapeDtypeStruct((24, full), F32),
        ],
        name="feed_down",
        compiler_params=pltpu.CompilerParams(vmem_limit_bytes=48 << 20),
        cost_estimate=LIGHT,
    )(device.reshape(1), act, middle, cotangent, vectors, *group_d.inputs)


def back_kernel(group_a, group_u, group_d, scal, *refs):
    (grad_ref, slope_ref, branch_ref, middle_ref, cot_ref, rows_ref), refs = refs[:6], refs[6:]
    wa, refs = refs[: len(group_a.inputs)], refs[len(group_a.inputs) :]
    wu, refs = refs[: len(group_u.inputs)], refs[len(group_u.inputs) :]
    wd, refs = refs[: len(group_d.inputs)], refs[len(group_d.inputs) :]
    (pre_ref, mid_ref, low_ref, att_ref, sums_ref, u_sum_ref), refs = refs[:6], refs[6:]
    held_o, sem_o, held_u, sem_u, held_d, sem_d, total = refs
    r = pl.program_id(0)
    mp, dp = lax.axis_size("mp"), lax.axis_size("dp")
    copies_o = sum(group_a.copies(wa, held_o, sem_o, scal[0], mp, dp, [3]), [])
    copies_u = group_u.copies(wu, held_u, sem_u, scal[0], mp, dp, [0])
    copies_d = group_d.copies(wd, held_d, sem_d, scal[0], mp, dp, [0])
    copies = [one + two for one, two in zip(copies_d, copies_u)]
    rows, full = middle_ref.shape
    hidden = group_d.width
    size = column_tile(hidden)

    @pl.when(r == 0)
    def _():
        start_all(sum(copies, []) + copies_o)
        total[...] = jnp.zeros_like(total)

    wait_step(r, copies)

    def slopes(start):
        columns = pl.ds(start, size)
        grad = jnp.zeros((rows, size), F32)
        for block in range(full // hidden):
            grad = grad + dot_nt(
                grad_ref[:, block * hidden : (block + 1) * hidden],
                held_d[r, 0, pl.ds(block * hidden + start, size), :],
            )
        pre = (grad * slope_ref[:, columns].astype(F32)).astype(BF16)
        pre_ref[:, columns] = pre
        u_sum_ref[:, columns] = fold(pre.astype(F32))

    tiles(hidden, size, slopes)
    wide = column_tile(full)

    def add(start):
        columns = pl.ds(start, wide)
        total[:, columns] += dot_nt(pre_ref[...], held_u[r, 0, columns, :])

    tiles(full, wide, add)

    @pl.when(r == mp - 1)
    def _():
        sums_ref[...] = jnp.zeros_like(sums_ref)

        def norm_rows(start):
            place = pl.ds(start, row_tile(rows))

            def backward(upstream, inputs, gain):
                normal, factor = normalize(inputs)
                scaled = upstream * gain
                grad = (
                    scaled
                    - jnp.mean(scaled, axis=-1, keepdims=True)
                    - normal * jnp.mean(scaled * normal, axis=-1, keepdims=True)
                ) * factor
                return grad, fold(upstream * normal), fold(upstream)

            grad_mid, gain_sum, shift_sum = backward(
                total[place, :], middle_ref[place, :], rows_ref[0:1, :]
            )
            sums_ref[0:8, :] += gain_sum
            sums_ref[8:16, :] += shift_sum
            grad_middle = cot_ref[place, :].astype(F32) + grad_mid
            mid_ref[place, :] = grad_middle
            grad_branch, gain_sum, shift_sum = backward(
                grad_middle, branch_ref[place, :], rows_ref[1:2, :]
            )
            sums_ref[16:24, :] += gain_sum
            sums_ref[24:32, :] += shift_sum
            low = grad_branch.astype(BF16)
            low_ref[place, :] = low
            sums_ref[32:40, :] += fold(low.astype(F32))

        tiles(rows, row_tile(rows), norm_rows)
        wait_all(copies_o)
        width = group_a.width
        for layer in range(mp):
            grad = jnp.zeros((rows, width), F32)
            for block in range(full // width):
                columns = slice(block * width, (block + 1) * width)
                grad = grad + dot_nt(low_ref[:, columns], held_o[layer, 0, columns, :])
            att_ref[:, layer * width : (layer + 1) * width] = grad.astype(BF16)


def feed_back(grad, slope, branch, middle, cotangent, vectors, group_a, group_u, group_d, device):
    mp = lax.axis_size("mp")
    rows, full = middle.shape
    hidden = group_d.width
    step = pl.BlockSpec((rows, hidden), lambda i, *_: (0, i))
    return pl.pallas_call(
        functools.partial(back_kernel, group_a, group_u, group_d),
        grid_spec=pltpu.PrefetchScalarGridSpec(
            num_scalar_prefetch=1,
            grid=(mp,),
            in_specs=[whole((rows, full)), step]
            + [whole((rows, full))] * 3
            + [whole((8, full))]
            + group_a.specs()
            + group_u.specs()
            + group_d.specs(),
            out_specs=[step]
            + [whole((rows, full))] * 3
            + [whole((40, full)), pl.BlockSpec((8, hidden), lambda i, *_: (0, i))],
            scratch_shapes=group_a.scratch(mp, [3])
            + group_u.scratch(mp, [0])
            + group_d.scratch(mp, [0])
            + [pltpu.VMEM((rows, full), F32)],
        ),
        out_shape=[
            jax.ShapeDtypeStruct((rows, mp * hidden), BF16),
            jax.ShapeDtypeStruct((rows, full), F32),
            jax.ShapeDtypeStruct((rows, full), BF16),
            jax.ShapeDtypeStruct((rows, full), BF16),
            jax.ShapeDtypeStruct((40, full), F32),
            jax.ShapeDtypeStruct((8, mp * hidden), F32),
        ],
        name="feed_back",
        compiler_params=pltpu.CompilerParams(vmem_limit_bytes=58 << 20),
        cost_estimate=LIGHT,
    )(
        device.reshape(1),
        grad,
        slope,
        branch,
        middle,
        cotangent,
        vectors,
        *group_a.inputs,
        *group_u.inputs,
        *group_d.inputs,
    )


def unproject_kernel(group, begin, steps, scal, *refs):
    (dq_ref, dk_ref, dv_ref), refs = refs[:3], refs[3:]
    w_refs, refs = refs[: len(group.inputs)], refs[len(group.inputs) :]
    near_ref, far_ref, held, sems, total = refs
    step = pl.program_id(0)
    mp, dp = lax.axis_size("mp"), lax.axis_size("dp")
    copies = group.copies(w_refs, held, sems, scal[0], mp, dp, [0, 1, 2])
    copies = copies[begin : begin + steps]
    rows, full = near_ref.shape

    @pl.when(step == 0)
    def _():
        start_all(sum(copies, []))
        total[...] = jnp.zeros_like(total)

    wait_step(step, copies)
    r = begin + step
    size = column_tile(full)

    def add(start):
        columns = pl.ds(start, size)
        grad = dot_nt(dk_ref[...], held[r, 1, columns, :]) + dot_nt(
            dv_ref[...], held[r, 2, columns, :]
        )
        total[:, columns] += grad
        total[0:rows, columns] += dot_nt(dq_ref[...], held[r, 0, columns, :])

    tiles(full, size, add)

    @pl.when(step == pl.num_programs(0) - 1)
    def _():
        near_ref[...] = total[0:rows, :]
        far_ref[...] = total[rows:, :].astype(BF16)


def unproject(grads, group, begin, device):
    grad_q, grad_k, grad_v = grads
    mp = lax.axis_size("mp")
    rows, count = grad_q.shape
    span = grad_k.shape[0]
    full, width = group.full, group.width
    made = lambda height: pl.BlockSpec((height, width), lambda i, *_: (0, i))
    return pl.pallas_call(
        functools.partial(unproject_kernel, group, begin, count // width),
        grid_spec=pltpu.PrefetchScalarGridSpec(
            num_scalar_prefetch=1,
            grid=(count // width,),
            in_specs=[made(rows), made(span), made(span)] + group.specs(),
            out_specs=[whole((rows, full)), whole((span - rows, full))],
            scratch_shapes=group.scratch(mp, [0, 1, 2]) + [pltpu.VMEM((span, full), F32)],
        ),
        out_shape=[
            jax.ShapeDtypeStruct((rows, full), F32),
            jax.ShapeDtypeStruct((span - rows, full), BF16),
        ],
        name="unproject",
        compiler_params=pltpu.CompilerParams(vmem_limit_bytes=48 << 20),
        cost_estimate=LIGHT,
    )(device.reshape(1), grad_q, grad_k, grad_v, *group.inputs)


def other_half_kernel(scal, left_ref, right_ref, out_ref):
    out_ref[...] = dot_tn(left_ref[...], right_ref[...]).astype(BF16)


def split_rows(total, bit_at, bit, outs):
    send_ref, keep_ref = outs
    count, rows, _ = send_ref.shape
    for j in range(count):
        base = ((j >> bit_at) << (bit_at + 1)) | (j & ((1 << bit_at) - 1))
        for ref, value in ((send_ref, 1 - bit), (keep_ref, bit)):
            start = pl.multiple_of((base + (value << bit_at)) * rows, rows)
            ref[j] = total[pl.ds(start, rows), :].astype(BF16)


def this_half_kernel(bits_at, scal, left_ref, right_ref, got_ref, *refs):
    outs, total = refs[:-1], refs[-1]
    total[...] = dot_tn(left_ref[...], right_ref[...]) + got_ref[...].astype(F32)
    step = pl.program_id(0)
    count = pl.num_programs(0) // 2
    for side in range(2):

        @pl.when(step // count == side)
        def _():
            split_rows(
                total,
                bits_at[side],
                (scal[0] >> (bits_at[side] + 1)) & 1,
                outs[2 * side : 2 * side + 2],
            )


def first_bits():
    along_x, along_y = chip_masks(lax.axis_size("dp"))
    return [order[0].bit_length() - 2 for order in (along_x + along_y, along_y + along_x)]


def other_half(left, right, device):
    rows, full = left.shape
    size = right.shape[1] // lax.axis_size("mp")
    return pl.pallas_call(
        other_half_kernel,
        grid_spec=pltpu.PrefetchScalarGridSpec(
            num_scalar_prefetch=1,
            grid=(right.shape[1] // size,),
            in_specs=[
                pl.BlockSpec((rows, full // 2), lambda i, scal: (0, 1 - scal[0] % 2)),
                pl.BlockSpec((rows, size), lambda i, scal: (0, i)),
            ],
            out_specs=pl.BlockSpec((full // 2, size), lambda i, scal: (0, i)),
        ),
        out_shape=jax.ShapeDtypeStruct((full // 2, right.shape[1]), BF16),
        name="other_half",
        compiler_params=pltpu.CompilerParams(vmem_limit_bytes=32 << 20),
        cost_estimate=LIGHT,
    )(device.reshape(1), left, right)


def this_half(left, right, got, device):
    rows, full = left.shape
    mp = lax.axis_size("mp")
    size = right.shape[1] // mp
    quarters = lax.axis_size("dp") // 2
    shape = (quarters // 2, full // 2 // quarters, mp // 2 * size)
    block = (quarters // 2, full // 2 // quarters, size)
    last = mp // 2 - 1
    sides = [lambda i, scal: (0, 0, jnp.minimum(i, last))] * 2 + [
        lambda i, scal: (0, 0, jnp.maximum(i - last - 1, 0))
    ] * 2
    return pl.pallas_call(
        functools.partial(this_half_kernel, first_bits()),
        grid_spec=pltpu.PrefetchScalarGridSpec(
            num_scalar_prefetch=1,
            grid=(mp,),
            in_specs=[
                pl.BlockSpec((rows, full // 2), lambda i, scal: (0, scal[0] % 2)),
                pl.BlockSpec((rows, size), lambda i, scal: (0, i)),
                pl.BlockSpec((full // 2, size), lambda i, scal: (0, i)),
            ],
            out_specs=[pl.BlockSpec(block, index) for index in sides],
            scratch_shapes=[pltpu.VMEM((full // 2, size), F32)],
        ),
        out_shape=[jax.ShapeDtypeStruct(shape, BF16)] * 4,
        name="this_half",
        compiler_params=pltpu.CompilerParams(vmem_limit_bytes=40 << 20),
        cost_estimate=LIGHT,
    )(device.reshape(1), left, right, got)


def attention_dots(width, lefts, branch, grads, attended, layer, put):
    grad_q, grad_k, grad_v = grads
    rows = grad_q.shape[0]
    columns = slice(layer * width, (layer + 1) * width)
    put(0, dot_tn(lefts[0][...], grad_q[:, columns]))
    for index, grad in ((1, grad_k), (2, grad_v)):
        total = dot_tn(lefts[0][...], grad[0:rows, columns])
        for block in range(1, len(lefts)):
            total = total + dot_tn(
                lefts[block][...], grad[block * rows : (block + 1) * rows, columns]
            )
        put(index, total)
    put(3, dot_tn(branch[...], attended[:, columns]))


def attention_other_kernel(width, blocks, scal, *refs):
    lefts, (branch, *grads, attended, out_ref) = refs[:blocks], refs[blocks:]
    for layer in range(attended.shape[1] // width):

        def put(index, value):
            place = (layer * 4 + index) * width
            out_ref[:, place : place + width] = value.astype(BF16)

        attention_dots(width, lefts, branch, grads, attended, layer, put)


def attention_this_kernel(width, blocks, bits_at, scal, *refs):
    lefts, (branch, *grads, attended, got_ref) = refs[:blocks], refs[blocks : blocks + 6]
    outs, total = refs[blocks + 6 : -1], refs[-1]
    layers = attended.shape[1] // width
    for side in range(2):
        for local in range(layers // 2):
            layer = side * (layers // 2) + local

            def put(index, value):
                place = (layer * 4 + index) * width
                total[:, index * width : (index + 1) * width] = value + got_ref[
                    :, place : place + width
                ].astype(F32)

            attention_dots(width, lefts, branch, grads, attended, layer, put)
            columns = pl.ds(local * 4 * width, 4 * width)
            split_rows(
                total,
                bits_at[side],
                (scal[0] >> (bits_at[side] + 1)) & 1,
                [ref.at[:, :, columns] for ref in outs[2 * side : 2 * side + 2]],
            )


def attention_specs(normed, branch, grads, attended, core_of):
    rows, full = branch.shape
    left = pl.BlockSpec((rows, full // 2), lambda i, scal: (0, core_of(scal)))
    return [left] * (len(normed) + 1) + [whole(g.shape) for g in grads] + [whole(attended.shape)]


def attention_other(normed, branch, grads, attended, width, device):
    full = branch.shape[1]
    out = (full // 2, 4 * attended.shape[1])
    return pl.pallas_call(
        functools.partial(attention_other_kernel, width, len(normed)),
        grid_spec=pltpu.PrefetchScalarGridSpec(
            num_scalar_prefetch=1,
            grid=(1,),
            in_specs=attention_specs(normed, branch, grads, attended, lambda s: 1 - s[0] % 2),
            out_specs=whole(out),
        ),
        out_shape=jax.ShapeDtypeStruct(out, BF16),
        name="attention_other",
        compiler_params=pltpu.CompilerParams(vmem_limit_bytes=40 << 20),
        cost_estimate=LIGHT,
    )(device.reshape(1), *normed, branch, *grads, attended)


def attention_this(normed, branch, grads, attended, got, width, device):
    full = branch.shape[1]
    quarters = lax.axis_size("dp") // 2
    shape = (quarters // 2, full // 2 // quarters, 2 * attended.shape[1])
    return pl.pallas_call(
        functools.partial(attention_this_kernel, width, len(normed), first_bits()),
        grid_spec=pltpu.PrefetchScalarGridSpec(
            num_scalar_prefetch=1,
            grid=(1,),
            in_specs=attention_specs(normed, branch, grads, attended, lambda s: s[0] % 2)
            + [whole(got.shape)],
            out_specs=[whole(shape)] * 4,
            scratch_shapes=[pltpu.VMEM((full // 2, 4 * width), F32)],
        ),
        out_shape=[jax.ShapeDtypeStruct(shape, BF16)] * 4,
        name="attention_this",
        compiler_params=pltpu.CompilerParams(vmem_limit_bytes=48 << 20),
        cost_estimate=LIGHT,
    )(device.reshape(1), *normed, branch, *grads, attended, got)


def reduce_flow(send, add, layers, device):
    (send,) = yield (send,)
    (got,) = yield (swap(send, "dp", 1),)
    send_a, keep_a, send_b, keep_b = add(got)
    along_x, along_y = chip_masks(lax.axis_size("dp"))
    orders = (along_x + along_y, along_y + along_x)
    bits = len(orders[0])
    sends, keeps = [send_a, send_b], [keep_a, keep_b]
    lefts = []
    for side, order in enumerate(orders):
        left = list(range(bits - 1, -1, -1))
        left.remove(order[0].bit_length() - 2)
        lefts.append(left)
        keeps[side] = keeps[side].reshape((2,) * (bits - 1) + keeps[side].shape[1:])
    for step in range(bits):
        sends = yield tuple(sends)
        gots = yield tuple(swap(value, "dp", order[step]) for value, order in zip(sends, orders))
        gots = [got.reshape(keep.shape) for got, keep in zip(gots, keeps)]
        if step + 1 == bits:
            break
        sends, next_keeps = [], []
        for side, order in enumerate(orders):
            which = order[step + 1].bit_length() - 2
            axis = lefts[side].index(which)
            lefts[side].remove(which)
            bit = (device >> (which + 1)) & 1

            def part(value):
                summed = [
                    lax.dynamic_index_in_dim(item, value, axis, keepdims=False).astype(F32)
                    for item in (keeps[side], gots[side])
                ]
                return (summed[0] + summed[1]).astype(BF16)

            sends.append(part(1 - bit))
            next_keeps.append(part(bit))
        keeps = next_keeps
    each = len(layers) // 2
    size = keeps[0].shape[-1] // each
    pieces = []
    for side in range(2):
        for local in range(each):
            columns = slice(local * size, (local + 1) * size)
            pieces.append(
                keeps[side][..., columns].astype(F32) + gots[side][..., columns].astype(F32)
            )
    away = [(r, piece.astype(BF16)) for r, piece in zip(layers, pieces) if r]
    sent = yield tuple(piece for _, piece in away)
    found = yield tuple(swap(piece, "mp", r) for (r, _), piece in zip(away, sent))
    return [piece for r, piece in zip(layers, pieces) if r == 0] + [
        piece.astype(F32) for piece in found
    ]


def fill_kernel(plan, rows, dp, scal, *refs):
    ins, (qkv_ref, out_ref, turned) = refs[:-3], refs[-3:]
    width = turned.shape[1]
    for ref, (side, masks) in zip(ins, plan):
        for index, mask in enumerate(masks):
            place = pl.ds(pl.multiple_of(position(scal[0], mask, dp) * rows, rows), rows)
            for inner in range(2):
                value = ref[index, :, inner * width : (inner + 1) * width].astype(F32)
                if side * 2 + inner < 3:
                    qkv_ref[side * 2 + inner, place, :] = value
                else:
                    turned[place, :] = value
    out_ref[...] = turned[...].T


def fill_attention(arrays, full, width, device):
    dp = lax.axis_size("dp")
    inputs = [value for _, _, value in arrays]
    vmem = pl.BlockSpec(memory_space=pltpu.VMEM)
    return pl.pallas_call(
        functools.partial(fill_kernel, [(side, m) for side, m, _ in arrays], full // dp, dp),
        grid_spec=pltpu.PrefetchScalarGridSpec(
            num_scalar_prefetch=1,
            grid=(),
            in_specs=[vmem] * len(inputs),
            out_specs=[vmem, vmem],
            scratch_shapes=[pltpu.VMEM((full, width), F32)],
        ),
        out_shape=[
            jax.ShapeDtypeStruct((3, full, width), F32),
            jax.ShapeDtypeStruct((width, full), F32),
        ],
        name="fill_attention",
        compiler_params=pltpu.CompilerParams(vmem_limit_bytes=32 << 20),
        cost_estimate=LIGHT,
    )(device.reshape(1), *inputs)


def fill_ffn_kernel(turn, in_ref, out_ref):
    group, _, rows, hidden = in_ref.shape
    value = in_ref[...].astype(F32).reshape(group * rows, hidden)
    out_ref[...] = value.T if turn else value


def fill_ffn(gathered, turn):
    dp, rows, hidden = gathered.shape
    quarters = dp // 2
    group = quarters
    count = quarters // group
    full = dp * rows
    block = (hidden, group * rows) if turn else (group * rows, hidden)
    shape = (hidden, full) if turn else (full, hidden)
    where = (lambda c, j: (0, c * count + j)) if turn else (lambda c, j: (c * count + j, 0))
    return pl.pallas_call(
        functools.partial(fill_ffn_kernel, turn),
        grid=(2, count),
        in_specs=[pl.BlockSpec((group, 1, rows, hidden), lambda c, j: (j, c, 0, 0))],
        out_specs=pl.BlockSpec(block, where),
        out_shape=jax.ShapeDtypeStruct(shape, F32),
        name="fill_ffn",
        compiler_params=pltpu.CompilerParams(vmem_limit_bytes=24 << 20),
        cost_estimate=LIGHT,
    )(gathered.reshape(quarters, 2, rows, hidden))


def small_flow(value):
    for axis in ("dp", "mp"):
        for bit in range(lax.axis_size(axis).bit_length() - 1):
            (value,) = yield (value,)
            (got,) = yield (swap(value, axis, 1 << bit),)
            value = value + got
    return value


def spread_flow(sides):
    return (yield from spread_steps(sides))


def finish(flows, *values):
    while any(not flow.over for flow in flows):
        out = meet(flows, *values)
        values = out if len(values) > 1 else (out,)
    return values


def drain(*flows):
    for flow in flows:
        while not flow.over:
            flow.move(flow.held)


def eight_rows(*rows):
    stacked = jnp.stack([row.astype(F32) for row in rows])
    return jnp.pad(stacked, ((0, 8 - stacked.shape[0]), (0, 0)))


def on_device(
    tokens,
    groups,
    lengths,
    qkv_weight,
    qv_bias,
    out_weight,
    out_bias,
    up_weight,
    up_bias,
    down_weight,
    down_bias,
    norm_gain,
    norm_bias,
    group_table,
    cotangent,
):
    dp, mp = lax.axis_size("dp"), lax.axis_size("mp")
    device, layer = lax.axis_index("dp"), lax.axis_index("mp")
    core = device & 1
    rows, full = tokens.shape
    width = qkv_weight.shape[2]
    hidden = up_weight.shape[1]
    blocks = SEQ_LEN // rows
    place_in_seq = layer % blocks
    length = lax.dynamic_index_in_dim(lengths, layer // blocks, keepdims=False)
    along_x, along_y = chip_masks(dp)
    stages = len(along_x + along_y)
    gains = norm_gain.astype(F32)
    shifts = norm_bias.astype(F32)
    part, half = full // 2, full // 2

    shard_a = [(qkv_weight, 0, False), (out_weight, 3, True)]
    shard_u, shard_d = [(up_weight[None], 0, False)], [(down_weight, 0, True)]
    small_here = jnp.concatenate([qv_bias[0], qv_bias[1], up_bias]).reshape(-1, width)
    n_small = small_here.shape[0]
    small_here = jnp.pad(small_here, ((0, -n_small % 16), (0, 0)))
    slice_a = jnp.concatenate(
        [
            own_slice(qkv_weight, False, device, width),
            own_slice(out_weight, True, device, width),
        ]
    )
    flow_a = Flow(gather_flow(slice_a, small_here))
    tokens = begin([flow_a], tokens)

    order_of = layer ^ jnp.arange(mp)
    onehot = (
        groups[:, None] == lax.broadcasted_iota(jnp.int32, (1, group_table.shape[0]), 1)
    ).astype(BF16)
    residual = tokens.astype(F32) + jnp.dot(onehot, group_table, preferred_element_type=F32)
    normed, norm_one, inv_one = norm_forward(residual, gains[0], shifts[0])
    normed_low = normed.astype(BF16)

    def rows_flow(value):
        (value,) = yield (value,)
        return (yield tuple(swap(value, "mp", m) for m in range(1, blocks)))

    key_ids = lax.broadcasted_iota(jnp.int32, (blocks, rows, 1), 1)
    block_ids = place_in_seq ^ lax.broadcasted_iota(jnp.int32, (blocks, rows, 1), 0)
    shown = (block_ids <= place_in_seq) & (block_ids * rows + key_ids < length)
    spot = lax.broadcasted_iota(jnp.int32, (blocks, rows, LANES), 2) % HEAD_DIM
    key_const = jnp.where(
        spot == 0,
        jnp.where(shown, 0.0, MASKED_SCORE),
        jnp.where(spot <= 3, 1.0, 0.0),
    )
    key_const = key_const.astype(BF16).reshape(blocks * rows, LANES)

    slice_u = own_slice(up_weight[None], False, device, hidden)
    slice_d = own_slice(down_weight, True, device, hidden)
    flow_r = Flow(rows_flow(normed_low))
    slice_u, slice_d = begin([flow_r], slice_u, slice_d)
    normed_low, slice_u, slice_d = meet([flow_a], normed_low, slice_u, slice_d)
    flow_u, flow_d = Flow(gather_flow(slice_u)), Flow(gather_flow(slice_d))
    layer_stages = mp.bit_length() - 1
    for _ in range(layer_stages - 1):
        normed_low = meet([flow_a], normed_low)
    normed_low = begin([flow_u], normed_low)
    for _ in range(stages - 1):
        normed_low = meet([flow_a], normed_low)
    normed_low = meet([flow_a, flow_r, flow_u], normed_low)
    normed_low = meet([flow_a], normed_low)
    for _ in range(layer_stages - 1):
        normed_low = meet([flow_u], normed_low)
    normed_low = begin([flow_d], normed_low)
    arrays_a, small_all = flow_a.result
    group_a = Weights(shard_a, arrays_a)
    small_all = jnp.stack(small_all)[:, :n_small].reshape(mp, -1).astype(F32)
    qv_rows = small_all[:, : 2 * width].reshape(mp, 2, width).transpose(1, 0, 2).reshape(2, full)
    u_rows = small_all[:, 2 * width :].reshape(1, -1)
    qv_rows = jnp.pad(qv_rows, ((0, 6), (0, 0)))
    u_rows = jnp.pad(u_rows, ((0, 7), (0, 0)))
    seq_normed = (normed_low,) + tuple(flow_r.result)
    queries, keys, values = project(seq_normed, qv_rows, group_a, device)
    for _ in range(stages - 1):
        queries, keys, values = meet([flow_u, flow_d], queries, keys, values)
    attended_a, aug_a = attend(queries, keys, values, key_const, 0, part)
    attended_a, queries = meet([flow_d], attended_a, queries)
    for _ in range(layer_stages - 2):
        attended_a, queries = meet([flow_d], attended_a, queries)
    attended_b, aug_b = attend(queries, keys, values, key_const, part, part)
    attended_b = meet([flow_u], attended_b)
    for _ in range(stages - 1):
        attended_b = meet([flow_d], attended_b)
    (attended_b,) = finish([flow_u], attended_b)
    group_u = Weights(shard_u, flow_u.result[0])
    branch, middle, mid_low, act, slope = feed_up(
        attended_a,
        attended_b,
        residual,
        eight_rows(out_bias, gains[1], shifts[1], gains[2], shifts[2]),
        u_rows,
        group_a,
        group_u,
        device,
    )
    (act,) = finish([flow_d], act)
    group_d = Weights(shard_d, flow_d.result[0])
    output, grad_ffn, sums_ffn = feed_down(
        act, middle, cotangent, eight_rows(down_bias, gains[3], shifts[3]), group_d, device
    )

    everyone = list(range(mp))

    def weight_flow(left, right):
        return Flow(
            reduce_flow(
                other_half(left, right, device),
                lambda got: this_half(left, right, got, device),
                everyone,
                device,
            )
        )

    flow_d = weight_flow(grad_ffn, act)
    grad_ffn = begin([flow_d], grad_ffn)
    grad_ffn = meet([flow_d], grad_ffn)
    grad_pre, grad_middle, grad_branch, grad_attended, sums_back, sums_up = feed_back(
        grad_ffn,
        slope,
        branch,
        middle,
        cotangent,
        eight_rows(gains[2], gains[1]),
        group_a,
        group_u,
        group_d,
        device,
    )
    grad_pre, grad_branch, grad_attended = meet([flow_d], grad_pre, grad_branch, grad_attended)
    flow_u = weight_flow(mid_low, grad_pre)
    grad_branch, grad_attended = begin([flow_u], grad_branch, grad_attended)
    grad_branch, grad_attended = meet([flow_u], grad_branch, grad_attended)

    def attention_flow(grads, attended, layers):
        return Flow(
            reduce_flow(
                attention_other(seq_normed, grad_branch, grads, attended, width, device),
                lambda got: attention_this(
                    seq_normed, grad_branch, grads, attended, got, width, device
                ),
                layers,
                device,
            )
        )

    layers_b, layers_a = everyone[: mp // 2], everyone[mp // 2 :]
    grads_a = attend_back(queries, keys, values, key_const, aug_b, grad_attended, attended_b, part)
    grads_a = meet([flow_d], *grads_a)
    flow_qa = attention_flow(grads_a, attended_b, layers_a)
    grads_a = meet([flow_u], *grads_a)
    queries, *grads_a = begin([flow_qa], queries, *grads_a)
    near_a, far_a = unproject(grads_a, group_a, mp // 2, device)
    queries, near_a, far_a = meet([flow_qa], queries, near_a, far_a)
    queries, near_a, far_a = meet([flow_u], queries, near_a, far_a)
    grads_b = attend_back(queries, keys, values, key_const, aug_a, grad_attended, attended_a, 0)
    grads_b = meet([flow_d, flow_u, flow_qa], *grads_b)
    flow_qb = attention_flow(grads_b, attended_a, layers_b)
    grads_b = begin([flow_qb], *grads_b)
    near_b, far_b = unproject(grads_b, group_a, 0, device)
    flow_f = Flow(rows_back(far_a, far_b, rows, blocks))
    near_b = begin([flow_f], near_b)
    near_b = meet([flow_qb], near_b)
    near_b = meet([flow_f, flow_qa], near_b)
    grad_normed = near_a + near_b
    for value in flow_f.result:
        grad_normed = grad_normed + value.astype(F32)
    back_one, gain_one, shift_one = norm_backward(grad_normed, norm_one, inv_one, gains[0])
    input_grad = grad_middle + back_one
    table_part = jnp.dot(
        onehot.astype(F32).T, input_grad, precision=PRECISE, preferred_element_type=F32
    )
    grad_q_sum = jnp.concatenate([jnp.sum(g[0].astype(F32), axis=0) for g in (grads_b, grads_a)])
    grad_v_sum = jnp.concatenate([jnp.sum(g[2].astype(F32), axis=0) for g in (grads_b, grads_a)])
    ffn_sums = jnp.sum(sums_ffn.reshape(3, 8, full), axis=1)
    back_sums = jnp.sum(sums_back.reshape(5, 8, full), axis=1)
    up_bias_part = jnp.sum(sums_up, axis=0)
    by_layer = jnp.concatenate(
        [grad_q_sum.reshape(mp, -1), grad_v_sum.reshape(mp, -1), up_bias_part.reshape(mp, -1)],
        axis=1,
    )
    by_layer = jnp.take(by_layer, order_of, axis=0)
    wide = by_layer.shape[1]
    by_layer = jnp.pad(by_layer, ((0, 0), (0, -wide % full))).reshape(-1, full)
    parts = jnp.concatenate(
        [
            jnp.stack([gain_one, back_sums[2], back_sums[0], ffn_sums[0]]),
            jnp.stack([shift_one, back_sums[3], back_sums[1], ffn_sums[1]]),
            jnp.stack([back_sums[4], ffn_sums[2]]),
            table_part,
            by_layer,
        ]
    )
    flow_s = Flow(small_flow(parts))
    drain(flow_s, flow_u, flow_d, flow_qa, flow_qb)
    down_mine = sum(flow_d.result).astype(BF16)
    down_grad = fill_ffn(lax.all_gather(down_mine, "dp", axis=0), True)
    up_mine = sum(flow_u.result).astype(BF16)
    up_grad = fill_ffn(lax.all_gather(up_mine, "dp", axis=0), False)
    mine = sum(flow_qa.result + flow_qb.result).astype(BF16)
    flow_o = Flow(spread_flow((mine[:, : 2 * width], mine[:, 2 * width :])))
    drain(flow_o)
    qkv_grad, out_grad = fill_attention(flow_o.result, full, width, device)

    parts = flow_s.result
    gain_grad, shift_grad = parts[:4], parts[4:8]
    out_bias_grad, down_bias_grad = parts[8], parts[9]
    n_groups = group_table.shape[0]
    table_grad = parts[10 : 10 + n_groups]
    by_layer = parts[10 + n_groups :].reshape(mp, -1)
    mine = lax.dynamic_index_in_dim(by_layer, layer, keepdims=False)
    qv_bias_grad = mine[: 2 * width].reshape(2, width)
    up_bias_grad = mine[2 * width : 2 * width + hidden]
    return (
        output,
        input_grad,
        qkv_grad,
        qv_bias_grad,
        out_grad,
        out_bias_grad,
        up_grad,
        up_bias_grad,
        down_grad,
        down_bias_grad,
        gain_grad,
        shift_grad,
        table_grad,
    )


def rows_back(far_a, far_b, rows, blocks):
    value = (far_a.astype(F32) + far_b.astype(F32)).astype(BF16)
    (value,) = yield (value,)
    return (
        yield tuple(swap(value[(m - 1) * rows : m * rows], "mp", m) for m in range(1, blocks))
    )


def solution(mesh):
    placed = (
        P(("dp", "mp"), None),
        P(("dp", "mp")),
        P("dp"),
        P(None, None, "mp"),
        P(None, "mp"),
        P("mp", None),
        P(),
        P(None, "mp"),
        P("mp"),
        P("mp", None),
        P(),
        P(),
        P(),
        P(),
        P(("dp", "mp"), None),
    )
    return jax.shard_map(
        on_device,
        mesh=mesh,
        in_specs=placed,
        out_specs=(
            P(("dp", "mp"), None),
            P(("dp", "mp"), None),
            P(None, None, "mp"),
            P(None, "mp"),
            P("mp", None),
            P(),
            P(None, "mp"),
            P("mp"),
            P("mp", None),
            P(),
            P(),
            P(),
            P(),
        ),
        check_vma=False,
    )
```

```python
import functools
import math

import jax
import jax.numpy as jnp
from jax import lax
from jax.experimental import pallas as pl
from jax.experimental.pallas import tpu as pltpu
from jax.sharding import PartitionSpec as P

HEAD_DIM = 64
SEQ_LEN = 1088
RELAX_ALPHA = 32.0
NORM_EPSILON = 1e-05
MASKED_SCORE = -1000000000.0
PRECISE = lax.Precision.HIGHEST
BF16 = jnp.bfloat16
F32 = jnp.float32
LANES = 128
LIGHT = pl.CostEstimate(flops=1000, bytes_accessed=1000, transcendentals=0)


def swap(value, axis, mask):
    count = lax.axis_size(axis)
    return lax.ppermute(value, axis, [(i, i ^ mask) for i in range(count)])


def normalize(inputs):
    centred = inputs - jnp.mean(inputs, axis=-1, keepdims=True)
    factor = lax.rsqrt(jnp.mean(centred * centred, axis=-1, keepdims=True) + NORM_EPSILON)
    return centred * factor, factor


def norm_forward(inputs, gain_row, shift_row):
    centred = inputs - jnp.mean(inputs, axis=-1, keepdims=True)
    factor = lax.rsqrt(jnp.mean(centred * centred, axis=-1, keepdims=True) + NORM_EPSILON)
    normal = centred * factor
    return (normal * gain_row + shift_row, normal, factor)


def norm_backward(upstream, normal, factor, gain_row):
    scaled = upstream * gain_row
    adjusted = (
        scaled
        - jnp.mean(scaled, axis=-1, keepdims=True)
        - normal * jnp.mean(scaled * normal, axis=-1, keepdims=True)
    )
    return (adjusted * factor, jnp.sum(upstream * normal, axis=0), jnp.sum(upstream, axis=0))


def dot_nn(a, b):
    return lax.dot_general(a, b, (((1,), (0,)), ((), ())), preferred_element_type=F32)


def dot_nt(a, b):
    return lax.dot_general(a, b, (((1,), (1,)), ((), ())), preferred_element_type=F32)


def dot_tn(a, b):
    return lax.dot_general(a, b, (((0,), (0,)), ((), ())), preferred_element_type=F32)


def query_tile(rows):
    return rows // 2 if (rows // 2) % 16 == 0 else rows


def padded(rows):
    return -(-rows // LANES) * LANES


def three_parts(value):
    high = value.astype(BF16)
    rest = value - high.astype(F32)
    mid = rest.astype(BF16)
    return high, mid, (rest - mid.astype(F32)).astype(BF16)


def attend_kernel(blocks, rows, q_ref, k_ref, v_ref, kc_ref, out_ref, aug_ref):
    tile = query_tile(rows)
    far = (blocks - 1) * rows
    lane = lax.broadcasted_iota(jnp.int32, (1, LANES), 1)
    first = lane < HEAD_DIM
    mine = [first, jnp.logical_not(first)]
    keys = jnp.concatenate([k_ref[...], kc_ref[...]], axis=1)
    special = jnp.where(lane == 0, 1.0, 0.0).astype(BF16)
    special = jnp.broadcast_to(special, (tile, LANES))
    starts = list(range(0, rows, tile))

    def scores_of(start):
        q = q_ref[start : start + tile, :]
        zero = jnp.zeros_like(q)
        both = jnp.concatenate(
            [jnp.concatenate([jnp.where(m, q, zero), special], axis=1) for m in mine], axis=0
        )
        return dot_nt(both, keys[: far + start + tile])

    scores = [scores_of(start) for start in starts]
    for start, score in zip(starts, scores):
        limit = far + start + tile
        cut = (far + start) // LANES * LANES
        row_ids = lax.broadcasted_iota(jnp.int32, (2 * tile, limit - cut), 0)
        row_ids = start + far - cut + jnp.where(row_ids >= tile, row_ids - tile, row_ids)
        columns = lax.broadcasted_iota(jnp.int32, (2 * tile, limit - cut), 1)
        last = jnp.where(columns <= row_ids, score[:, cut:], MASKED_SCORE)
        score = jnp.concatenate([score[:, :cut], last], axis=1) if cut else last
        top = jnp.max(score, axis=-1, keepdims=True)
        exponent = jnp.exp(score - top)
        total = jnp.sum(exponent, axis=-1, keepdims=True)
        gathered = dot_nn(exponent.astype(BF16), v_ref[0:limit, :]) / total
        out_ref[start : start + tile, :] = jnp.where(
            first, gathered[:tile], gathered[tile:]
        ).astype(BF16)
        parts = three_parts(-(top + jnp.log(total)))
        spot = lane % HEAD_DIM
        augs = []
        for head in range(2):
            aug = jnp.where(spot == 0, 1.0, jnp.zeros((tile, LANES), F32)).astype(BF16)
            for index, value in enumerate(parts):
                aug = jnp.where(spot == index + 1, value[head * tile : (head + 1) * tile], aug)
            augs.append(aug)
        aug_ref[start : start + tile, :] = jnp.where(first, augs[0], augs[1])


def attend(queries, keys, values, key_const, begin, count):
    rows = queries.shape[0]
    span = keys.shape[0]
    first = begin // LANES
    pair = lambda height: pl.BlockSpec((height, LANES), lambda i: (0, first + i))
    made = lambda height: pl.BlockSpec((height, LANES), lambda i: (0, i))
    return pl.pallas_call(
        functools.partial(attend_kernel, span // rows, rows),
        grid=(count // LANES,),
        in_specs=[
            pair(rows),
            pair(span),
            pair(span),
            pl.BlockSpec((span, LANES), lambda i: (0, 0)),
        ],
        out_specs=[made(rows), made(rows)],
        out_shape=[
            jax.ShapeDtypeStruct((rows, count), BF16),
            jax.ShapeDtypeStruct((rows, count), BF16),
        ],
        name="attend",
        compiler_params=pltpu.CompilerParams(vmem_limit_bytes=48 << 20),
        cost_estimate=LIGHT,
    )(queries, keys, values, key_const)


def attend_back_kernel(
    causal, q_ref, k_ref, v_ref, kc_ref, aug_ref, go_ref, out_ref, *refs
):
    before, refs = (refs[0], refs[1:]) if causal else (None, refs)
    dq_ref, dk_ref, dv_ref, q_both, g_both, ds_ref = refs
    rows = q_ref.shape[0]
    span = k_ref.shape[0]
    key_tile = query_tile(rows)
    wide = padded(rows)
    lane = lax.broadcasted_iota(jnp.int32, (1, LANES), 1)
    first = lane < HEAD_DIM
    mine = [first, jnp.logical_not(first)]
    q_pair, aug, go = q_ref[...], aug_ref[...], go_ref[...]
    zero = jnp.zeros_like(q_pair)
    weighed = go.astype(F32) * out_ref[...].astype(F32)
    pad = jnp.zeros((wide - rows, 2 * LANES), BF16)
    for head in range(2):
        m = mine[head]
        place = head * wide
        q_both[place : place + rows, 0:LANES] = jnp.where(m, q_pair, zero)
        q_both[place : place + rows, LANES:] = jnp.where(m, aug, zero)
        parts = three_parts(-jnp.sum(jnp.where(m, weighed, 0.0), axis=-1, keepdims=True))
        g_aug = zero
        for index, value in enumerate(parts):
            g_aug = jnp.where(lane == index + 1, value, g_aug)
        g_both[place : place + rows, 0:LANES] = jnp.where(m, go, zero)
        g_both[place : place + rows, LANES:] = g_aug
        if wide > rows:
            q_both[place + rows : place + wide, :] = pad
            g_both[place + rows : place + wide, :] = pad
    keys = jnp.concatenate([k_ref[...], kc_ref[...]], axis=1)
    v_const = jnp.where((lane >= 1) & (lane <= 3), 1.0, 0.0).astype(BF16)
    values = jnp.concatenate([v_ref[...], jnp.broadcast_to(v_const, k_ref.shape)], axis=1)

    def dots_of(start):
        stop = start + key_tile
        return dot_nt(keys[start:stop], q_both[...]), dot_nt(values[start:stop], g_both[...])

    starts = list(range(0, span, key_tile))
    ahead = dots_of(starts[0])
    for index, start in enumerate(starts):
        stop = start + key_tile
        scores, centred = ahead
        if index + 1 < len(starts):
            ahead = dots_of(starts[index + 1])
        exact = jnp.exp(scores)
        if causal:
            key_ids = start + lax.broadcasted_iota(jnp.int32, (key_tile, 2 * wide), 0)
            query_ids = lax.broadcasted_iota(jnp.int32, (key_tile, 2 * wide), 1)
            query_ids = jnp.where(query_ids >= wide, query_ids - wide, query_ids)
            exact = jnp.where(key_ids <= query_ids, exact, 0.0)
        grad_scores = (exact * centred).astype(BF16)
        ds_ref[start:stop, :] = grad_scores
        dv_ref[start:stop, :] = dot_nn(exact.astype(BF16), g_both[:, 0:LANES]).astype(BF16)
        dk_ref[start:stop, :] = dot_nn(grad_scores, q_both[:, 0:LANES]).astype(BF16)
    grad_q = dot_tn(k_ref[...], ds_ref[...]).T
    grad_q = jnp.where(first, grad_q[0:rows], grad_q[wide : wide + rows])
    if causal:
        dq_ref[...] = ((grad_q + before[...]) * 0.125).astype(BF16)
    else:
        dq_ref[...] = grad_q


def attend_back(queries, keys, values, key_const, aug, grad_out, out, begin, count, before=None):
    rows = queries.shape[0]
    far = keys.shape[0] - rows
    causal = before is not None
    span, block = (rows, far // rows) if causal else (far, 0)
    first = begin // LANES
    wide = padded(rows)
    pair = pl.BlockSpec((rows, LANES), lambda i: (0, first + i))
    keys_of = pl.BlockSpec((span, LANES), lambda i: (block, first + i))
    made = lambda height: pl.BlockSpec((height, LANES), lambda i: (0, i))
    return pl.pallas_call(
        functools.partial(attend_back_kernel, causal),
        grid=(count // LANES,),
        in_specs=[
            pair,
            keys_of,
            keys_of,
            pl.BlockSpec((span, LANES), lambda i: (block, 0)),
            pair,
            pair,
            pair,
        ]
        + [pair] * causal,
        out_specs=[made(rows), made(span), made(span)],
        out_shape=[
            jax.ShapeDtypeStruct((rows, count), BF16 if causal else F32),
            jax.ShapeDtypeStruct((span, count), BF16),
            jax.ShapeDtypeStruct((span, count), BF16),
        ],
        scratch_shapes=[
            pltpu.VMEM((2 * wide, 2 * LANES), BF16),
            pltpu.VMEM((2 * wide, 2 * LANES), BF16),
            pltpu.VMEM((span, 2 * wide), BF16),
        ],
        name="attend_back",
        compiler_params=pltpu.CompilerParams(vmem_limit_bytes=52 << 20),
        cost_estimate=LIGHT,
    )(queries, keys, values, key_const, aug, grad_out, out, *([before] if causal else []))


def chip_masks(dp):
    bits = dp.bit_length() - 2
    low = bits // 2
    along_x = [2 << i for i in range(low)]
    along_y = [2 << i for i in range(low, bits)]
    return along_x, along_y


def position(device, mask, dp):
    other = device ^ mask
    return (other & 1) * (dp // 2) + (other >> 1)


def own_slice(weight, by_rows, device, width):
    dp = lax.axis_size("dp")
    if by_rows:
        full = weight.shape[1]
        start = position(device, 0, dp) * (full // dp)
        piece = lax.dynamic_slice(weight, (start % width, start // width * width), (full // dp, width))
        return piece[None]
    rows = weight.shape[1] // dp
    return lax.dynamic_slice_in_dim(weight, position(device, 0, dp) * rows, rows, axis=1)


class Flow:
    def __init__(self, steps):
        self.steps = steps
        self.result = None
        self.over = False
        self.held = None
        self.move(None)

    def move(self, value):
        try:
            self.held = self.steps.send(value)
        except StopIteration as stop:
            self.result, self.over, self.held = stop.value, True, None


def ordered(flows, values):
    live = [flow for flow in flows if not flow.over]
    values, held = lax.optimization_barrier((values, [flow.held for flow in live]))
    for flow, item in zip(live, held):
        flow.move(item)
    return values


def begin(flows, *values):
    values = ordered(flows, values)
    return values if len(values) > 1 else values[0]


def meet(flows, *values):
    values = ordered(flows, values)
    return begin(flows, *values)


def layer_steps(value):
    mp = lax.axis_size("mp")
    got = {0: value}
    for count in range(1, mp.bit_length()):
        ranks = [r for r in range(mp) if r.bit_count() == count]
        sent = [got[r & (r - 1)] for r in ranks]
        if count > 1:
            sent = yield tuple(sent)
        found = yield tuple(swap(item, "mp", r & -r) for r, item in zip(ranks, sent))
        got.update(zip(ranks, found))
    return [got[r] for r in range(mp)]


def spread_steps(sides):
    along_x, along_y = chip_masks(lax.axis_size("dp"))
    orders = (along_x + along_y, along_y + along_x)
    masks = [[0], [0]]
    held = [side[None] for side in sides]
    arrays = []
    for step in range(len(along_x + along_y)):
        held = yield tuple(held)
        got = yield tuple(swap(value, "dp", order[step]) for value, order in zip(held, orders))
        for side, order in enumerate(orders):
            moved = [m ^ order[step] for m in masks[side]]
            if step + 1 < len(order):
                masks[side] = masks[side] + moved
            else:
                arrays += [(side, masks[side], held[side]), (side, moved, got[side])]
        held = [jnp.concatenate([one, two], axis=0) for one, two in zip(held, got)]
    own = yield tuple(value for _, _, value in arrays)
    other = yield tuple(swap(value, "dp", 1) for value in own)
    return [(side, m, value) for (side, m, _), value in zip(arrays, own)] + [
        (side, [k ^ 1 for k in m], value) for (side, m, _), value in zip(arrays, other)
    ]


def gather_flow(stacked, extra=None):
    count, rows, width = stacked.shape
    flat = stacked.reshape(count * rows, width)
    if extra is not None:
        flat = jnp.concatenate([flat, extra], axis=0)
    (flat,) = yield (flat,)
    found = yield from layer_steps(flat)
    across = jnp.stack([item[: count * rows].reshape(count, rows, width) for item in found[1:]])
    half = rows // 2
    arrays = yield from spread_steps((across[:, :, :half], across[:, :, half:]))
    return arrays, [item[count * rows :] for item in found]


class Weights:
    def __init__(self, own, arrays):
        self.own, self.arrays = own, arrays
        sample = arrays[0][2]
        self.full, self.width = sample.shape[3] * 2 * lax.axis_size("dp"), sample.shape[4]
        self.inputs = [shard for shard, _, _ in own] + [value for _, _, value in arrays]
        self.n_own = len(own)

    def specs(self):
        return [pl.BlockSpec(memory_space=pl.ANY)] * len(self.inputs)

    def scratch(self, mp, which):
        count = self.full // self.width + sum(len(m) for _, m, _ in self.arrays)
        return [
            pltpu.VMEM((mp, len(which), self.full, self.width), BF16),
            pltpu.SemaphoreType.DMA((count + 4,)),
        ]

    def copies(self, refs, held, sems, device, mp, dp, which):
        made = [[], []]
        spot = 0

        def add(r, source, target):
            nonlocal spot
            made[r].append((source, target, sems.at[spot]))
            spot += 1

        first, last = which[0], which[-1] + 1
        for ref, (_, index, by_rows) in zip(refs, self.own):
            if by_rows and first <= index < last:
                for block in range(self.full // self.width):
                    columns = pl.ds(block * self.width, self.width)
                    add(0, ref.at[:, columns], held.at[0, index - first, columns, :])
            elif not by_rows and first == index:
                add(0, ref, held.at[0, 0 : ref.shape[0]])
        half = self.full // dp // 2
        for ref, (side, masks, _) in zip(refs[self.n_own :], self.arrays):
            for index, mask in enumerate(masks):
                start = pl.multiple_of((position(device, mask, dp) * 2 + side) * half, half)
                add(
                    1,
                    ref.at[index, :, first:last],
                    held.at[1:, :, pl.ds(start, half), :],
                )
        return made


def start_all(copies):
    for copy in copies:
        pltpu.make_async_copy(*copy).start()


def wait_all(copies):
    for copy in copies:
        pltpu.make_async_copy(*copy).wait()


def wait_step(step, copies, begin=0):
    for r in range(begin, len(copies)):

        @pl.when(step == r)
        def _():
            wait_all(copies[r])


def tiles(count, size, body):
    if count == size:
        body(0)
    else:

        for i in range(count // size):
            body(i * size)


def row_tile(rows):
    return 272 if rows % 272 == 0 else 16


COLUMNS = 256


def column_tile(width):
    return min(COLUMNS, width)


def whole(shape):
    return pl.BlockSpec(shape, lambda i, *_: (0,) * len(shape))


def project_kernel(group, blocks, scale, scal, *refs):
    n_in = len(group.inputs)
    x_refs, bias_ref = refs[:blocks], refs[blocks]
    w_refs = refs[blocks + 1 : blocks + 1 + n_in]
    q_ref, k_ref, v_ref, held, sems = refs[blocks + 1 + n_in :]
    r = pl.program_id(0)
    mp, dp = lax.axis_size("mp"), lax.axis_size("dp")
    copies = group.copies(w_refs, held, sems, scal[0], mp, dp, [0, 1, 2])
    rows = q_ref.shape[0]

    @pl.when(r == 0)
    def _():
        start_all(sum(copies, []))

    wait_step(r, copies)

    size = column_tile(group.width)
    for begin in range(0, group.width, size):
        columns = slice(begin, begin + size)
        q = dot_nn(x_refs[-1][...], held[r, 0, :, columns]) + bias_ref[0:1, columns].astype(F32)
        q_ref[:, columns] = ((q * scale).astype(BF16) * RELAX_ALPHA).astype(BF16)
        for block in range(blocks):
            x = x_refs[block][...]
            place = slice(block * rows, (block + 1) * rows)
            k_ref[place, columns] = dot_nn(x, held[r, 1, :, columns]).astype(BF16)
            v = dot_nn(x, held[r, 2, :, columns]) + bias_ref[1:2, columns].astype(F32)
            v_ref[place, columns] = v.astype(BF16)


def project(normed, biases, group, device):
    mp = lax.axis_size("mp")
    rows, full = normed[0].shape
    blocks = len(normed)
    width = group.width
    made = lambda height: pl.BlockSpec((height, width), lambda i, *_: (0, i))
    return pl.pallas_call(
        functools.partial(project_kernel, group, blocks, 1.0 / math.sqrt(HEAD_DIM) / RELAX_ALPHA),
        grid_spec=pltpu.PrefetchScalarGridSpec(
            num_scalar_prefetch=1,
            grid=(mp,),
            in_specs=[whole((rows, full))] * blocks
            + [pl.BlockSpec((8, width), lambda i, *_: (0, i))]
            + group.specs(),
            out_specs=[made(rows), made(blocks * rows), made(blocks * rows)],
            scratch_shapes=group.scratch(mp, [0, 1, 2]),
        ),
        out_shape=[
            jax.ShapeDtypeStruct((rows, full), BF16),
            jax.ShapeDtypeStruct((blocks * rows, full), BF16),
            jax.ShapeDtypeStruct((blocks * rows, full), BF16),
        ],
        name="project",
        compiler_params=pltpu.CompilerParams(vmem_limit_bytes=48 << 20),
        cost_estimate=LIGHT,
    )(device.reshape(1), *normed, biases, *group.inputs)


def up_kernel(group_a, group_u, scal, *refs):
    (att_a, att_b, residual_ref, rows_ref, bias_ref), refs = refs[:5], refs[5:]
    wa, refs = refs[: len(group_a.inputs)], refs[len(group_a.inputs) :]
    wu, refs = refs[: len(group_u.inputs)], refs[len(group_u.inputs) :]
    branch_ref, middle_ref, mid_ref, act_ref, slope_ref, held_o, sem_o, held_u, sem_u = refs
    r = pl.program_id(0)
    mp, dp = lax.axis_size("mp"), lax.axis_size("dp")
    copies_o = sum(group_a.copies(wa, held_o, sem_o, scal[0], mp, dp, [3]), [])
    copies_u = group_u.copies(wu, held_u, sem_u, scal[0], mp, dp, [0])
    rows, full = middle_ref.shape
    width = group_a.width
    part = att_a.shape[1]

    @pl.when(r == 0)
    def _():
        start_all(copies_o)
        start_all(sum(copies_u, []))
        wait_all(copies_o)
        for block in range(full // width):
            columns = slice(block * width, (block + 1) * width)
            total = jnp.zeros((rows, width), F32)
            for layer in range(mp):
                source = att_a if layer * width < part else att_b
                first = layer * width % part
                total = total + dot_nn(source[:, first : first + width], held_o[layer, 0, columns, :])
            branch_ref[:, columns] = total + rows_ref[0:1, columns]

        def norm_rows(start):
            place = pl.ds(start, row_tile(rows))
            normal, _ = normalize(branch_ref[place, :])
            middle = residual_ref[place, :] + normal * rows_ref[1:2, :] + rows_ref[2:3, :]
            middle_ref[place, :] = middle
            normal, _ = normalize(middle)
            mid_ref[place, :] = (normal * rows_ref[3:4, :] + rows_ref[4:5, :]).astype(BF16)

        tiles(rows, row_tile(rows), norm_rows)

    wait_step(r, copies_u)

    size = column_tile(group_u.width)

    def activate(start):
        columns = pl.ds(start, size)
        u = dot_nn(mid_ref[...], held_u[r, 0, :, columns]) + bias_ref[0:1, columns]
        scale = math.sqrt(2.0 / math.pi)
        square = u * u
        bent = jnp.tanh(scale * u * (1.0 + 0.044715 * square))
        lifted = 0.5 + 0.5 * bent
        act_ref[:, columns] = (u * lifted).astype(BF16)
        slope = lifted + (0.5 * scale) * u * (1.0 - bent * bent) * (
            1.0 + (3.0 * 0.044715) * square
        )
        slope_ref[:, columns] = slope.astype(BF16)

    tiles(group_u.width, size, activate)


def feed_up(att_a, att_b, residual, vectors, u_bias, group_a, group_u, device):
    mp = lax.axis_size("mp")
    rows, full = residual.shape
    hidden = group_u.width
    made = pl.BlockSpec((rows, hidden), lambda i, *_: (0, i))
    return pl.pallas_call(
        functools.partial(up_kernel, group_a, group_u),
        grid_spec=pltpu.PrefetchScalarGridSpec(
            num_scalar_prefetch=1,
            grid=(mp,),
            in_specs=[whole(att_a.shape), whole(att_b.shape), whole((rows, full)), whole((8, full))]
            + [pl.BlockSpec((8, hidden), lambda i, *_: (0, i))]
            + group_a.specs()
            + group_u.specs(),
            out_specs=[whole((rows, full)), whole((rows, full)), whole((rows, full)), made, made],
            scratch_shapes=group_a.scratch(mp, [3]) + group_u.scratch(mp, [0]),
        ),
        out_shape=[
            jax.ShapeDtypeStruct((rows, full), F32),
            jax.ShapeDtypeStruct((rows, full), F32),
            jax.ShapeDtypeStruct((rows, full), BF16),
            jax.ShapeDtypeStruct((rows, mp * hidden), BF16),
            jax.ShapeDtypeStruct((rows, mp * hidden), BF16),
        ],
        name="feed_up",
        compiler_params=pltpu.CompilerParams(vmem_limit_bytes=56 << 20),
        cost_estimate=LIGHT,
    )(
        device.reshape(1), att_a, att_b, residual, vectors, u_bias, *group_a.inputs, *group_u.inputs
    )


def down_kernel(group_d, scal, *refs):
    (act_ref, middle_ref, cot_ref, rows_ref), refs = refs[:4], refs[4:]
    wd, refs = refs[: len(group_d.inputs)], refs[len(group_d.inputs) :]
    out_ref, grad_ref, sums_ref, held, sems, total = refs
    r = pl.program_id(0)
    mp, dp = lax.axis_size("mp"), lax.axis_size("dp")
    copies = group_d.copies(wd, held, sems, scal[0], mp, dp, [0])
    rows, full = middle_ref.shape
    width = group_d.width

    @pl.when(r == 0)
    def _():
        start_all(sum(copies, []))
        total[...] = jnp.zeros_like(total)

    wait_step(r, copies)

    size = column_tile(width)
    for block in range(full // width):

        def add(start):
            columns = pl.ds(block * width + start, size)
            total[:, columns] += dot_nn(
                act_ref[...], held[r, 0, block * width : (block + 1) * width, pl.ds(start, size)]
            )

        tiles(width, size, add)

    @pl.when(r == mp - 1)
    def _():
        sums_ref[...] = jnp.zeros_like(sums_ref)

        def norm_rows(start):
            place = pl.ds(start, row_tile(rows))
            normal, factor = normalize(total[place, :] + rows_ref[0:1, :])
            gain = rows_ref[1:2, :]
            out_ref[place, :] = (
                middle_ref[place, :] + (normal * gain + rows_ref[2:3, :])
            ).astype(BF16)
            upstream = cot_ref[place, :].astype(F32)
            scaled = upstream * gain
            grad = (
                scaled
                - jnp.mean(scaled, axis=-1, keepdims=True)
                - normal * jnp.mean(scaled * normal, axis=-1, keepdims=True)
            ) * factor
            grad = grad.astype(BF16)
            grad_ref[place, :] = grad
            sums_ref[0:8, :] += fold(upstream * normal)
            sums_ref[8:16, :] += fold(upstream)
            sums_ref[16:24, :] += fold(grad.astype(F32))

        tiles(rows, row_tile(rows), norm_rows)


def fold(value):
    return functools.reduce(jnp.add, [value[i : i + 8] for i in range(0, value.shape[0], 8)])


def feed_down(act, middle, cotangent, vectors, group_d, device):
    mp = lax.axis_size("mp")
    rows, full = middle.shape
    hidden = group_d.width
    return pl.pallas_call(
        functools.partial(down_kernel, group_d),
        grid_spec=pltpu.PrefetchScalarGridSpec(
            num_scalar_prefetch=1,
            grid=(mp,),
            in_specs=[pl.BlockSpec((rows, hidden), lambda i, *_: (0, i))]
            + [whole((rows, full)), whole((rows, full)), whole((8, full))]
            + group_d.specs(),
            out_specs=[whole((rows, full)), whole((rows, full)), whole((24, full))],
            scratch_shapes=group_d.scratch(mp, [0]) + [pltpu.VMEM((rows, full), F32)],
        ),
        out_shape=[
            jax.ShapeDtypeStruct((rows, full), BF16),
            jax.ShapeDtypeStruct((rows, full), BF16),
            jax.ShapeDtypeStruct((24, full), F32),
        ],
        name="feed_down",
        compiler_params=pltpu.CompilerParams(vmem_limit_bytes=48 << 20),
        cost_estimate=LIGHT,
    )(device.reshape(1), act, middle, cotangent, vectors, *group_d.inputs)


def back_kernel(group_a, group_u, group_d, scal, *refs):
    (grad_ref, slope_ref, branch_ref, middle_ref, cot_ref, rows_ref), refs = refs[:6], refs[6:]
    wa, refs = refs[: len(group_a.inputs)], refs[len(group_a.inputs) :]
    wu, refs = refs[: len(group_u.inputs)], refs[len(group_u.inputs) :]
    wd, refs = refs[: len(group_d.inputs)], refs[len(group_d.inputs) :]
    (pre_ref, mid_ref, low_ref, att_ref, sums_ref, u_sum_ref), refs = refs[:6], refs[6:]
    held_o, sem_o, held_u, sem_u, held_d, sem_d, total = refs
    r = pl.program_id(0)
    mp, dp = lax.axis_size("mp"), lax.axis_size("dp")
    copies_o = sum(group_a.copies(wa, held_o, sem_o, scal[0], mp, dp, [3]), [])
    copies_u = group_u.copies(wu, held_u, sem_u, scal[0], mp, dp, [0])
    copies_d = group_d.copies(wd, held_d, sem_d, scal[0], mp, dp, [0])
    copies = [one + two for one, two in zip(copies_d, copies_u)]
    rows, full = middle_ref.shape
    hidden = group_d.width
    size = column_tile(hidden)

    @pl.when(r == 0)
    def _():
        start_all(sum(copies, []) + copies_o)
        total[...] = jnp.zeros_like(total)

    wait_step(r, copies)

    def slopes(start):
        columns = pl.ds(start, size)
        grad = jnp.zeros((rows, size), F32)
        for block in range(full // hidden):
            grad = grad + dot_nt(
                grad_ref[:, block * hidden : (block + 1) * hidden],
                held_d[r, 0, pl.ds(block * hidden + start, size), :],
            )
        pre = (grad * slope_ref[:, columns].astype(F32)).astype(BF16)
        pre_ref[:, columns] = pre
        u_sum_ref[:, columns] = fold(pre.astype(F32))

    tiles(hidden, size, slopes)
    wide = column_tile(full)

    def add(start):
        columns = pl.ds(start, wide)
        total[:, columns] += dot_nt(pre_ref[...], held_u[r, 0, columns, :])

    tiles(full, wide, add)

    @pl.when(r == mp - 1)
    def _():
        sums_ref[...] = jnp.zeros_like(sums_ref)

        def norm_rows(start):
            place = pl.ds(start, row_tile(rows))

            def backward(upstream, inputs, gain):
                normal, factor = normalize(inputs)
                scaled = upstream * gain
                grad = (
                    scaled
                    - jnp.mean(scaled, axis=-1, keepdims=True)
                    - normal * jnp.mean(scaled * normal, axis=-1, keepdims=True)
                ) * factor
                return grad, fold(upstream * normal), fold(upstream)

            grad_mid, gain_sum, shift_sum = backward(
                total[place, :], middle_ref[place, :], rows_ref[0:1, :]
            )
            sums_ref[0:8, :] += gain_sum
            sums_ref[8:16, :] += shift_sum
            grad_middle = cot_ref[place, :].astype(F32) + grad_mid
            mid_ref[place, :] = grad_middle
            grad_branch, gain_sum, shift_sum = backward(
                grad_middle, branch_ref[place, :], rows_ref[1:2, :]
            )
            sums_ref[16:24, :] += gain_sum
            sums_ref[24:32, :] += shift_sum
            low = grad_branch.astype(BF16)
            low_ref[place, :] = low
            sums_ref[32:40, :] += fold(low.astype(F32))

        tiles(rows, row_tile(rows), norm_rows)
        wait_all(copies_o)
        width = group_a.width
        for layer in range(mp):
            grad = jnp.zeros((rows, width), F32)
            for block in range(full // width):
                columns = slice(block * width, (block + 1) * width)
                grad = grad + dot_nt(low_ref[:, columns], held_o[layer, 0, columns, :])
            att_ref[:, layer * width : (layer + 1) * width] = grad.astype(BF16)


def feed_back(grad, slope, branch, middle, cotangent, vectors, group_a, group_u, group_d, device):
    mp = lax.axis_size("mp")
    rows, full = middle.shape
    hidden = group_d.width
    step = pl.BlockSpec((rows, hidden), lambda i, *_: (0, i))
    return pl.pallas_call(
        functools.partial(back_kernel, group_a, group_u, group_d),
        grid_spec=pltpu.PrefetchScalarGridSpec(
            num_scalar_prefetch=1,
            grid=(mp,),
            in_specs=[whole((rows, full)), step]
            + [whole((rows, full))] * 3
            + [whole((8, full))]
            + group_a.specs()
            + group_u.specs()
            + group_d.specs(),
            out_specs=[step]
            + [whole((rows, full))] * 3
            + [whole((40, full)), pl.BlockSpec((8, hidden), lambda i, *_: (0, i))],
            scratch_shapes=group_a.scratch(mp, [3])
            + group_u.scratch(mp, [0])
            + group_d.scratch(mp, [0])
            + [pltpu.VMEM((rows, full), F32)],
        ),
        out_shape=[
            jax.ShapeDtypeStruct((rows, mp * hidden), BF16),
            jax.ShapeDtypeStruct((rows, full), F32),
            jax.ShapeDtypeStruct((rows, full), BF16),
            jax.ShapeDtypeStruct((rows, full), BF16),
            jax.ShapeDtypeStruct((40, full), F32),
            jax.ShapeDtypeStruct((8, mp * hidden), F32),
        ],
        name="feed_back",
        compiler_params=pltpu.CompilerParams(vmem_limit_bytes=58 << 20),
        cost_estimate=LIGHT,
    )(
        device.reshape(1),
        grad,
        slope,
        branch,
        middle,
        cotangent,
        vectors,
        *group_a.inputs,
        *group_u.inputs,
        *group_d.inputs,
    )


def unproject_kernel(group, which, begin, steps, added, scal, *refs):
    grads, refs = refs[: len(which)], refs[len(which) :]
    before, refs = (refs[0], refs[1:]) if added else (None, refs)
    w_refs, refs = refs[: len(group.inputs)], refs[len(group.inputs) :]
    out_ref, held, sems, total = refs
    step = pl.program_id(0)
    mp, dp = lax.axis_size("mp"), lax.axis_size("dp")
    copies = group.copies(w_refs, held, sems, scal[0], mp, dp, [0, 1, 2])
    if begin:
        copies = copies[1:]
    elif steps == 1:
        copies = copies[:1]
    full = out_ref.shape[1]

    @pl.when(step == 0)
    def _():
        start_all(sum(copies, []))
        total[...] = before[...] if added else jnp.zeros_like(total)

    wait_step(step, copies)
    r = begin + step
    size = column_tile(full)

    def add(start):
        columns = pl.ds(start, size)
        total[:, columns] += functools.reduce(
            jnp.add,
            [dot_nt(g[...], held[r, index, columns, :]) for index, g in zip(which, grads)],
        )

    tiles(full, size, add)

    @pl.when(step == pl.num_programs(0) - 1)
    def _():
        out_ref[...] = total[...].astype(out_ref.dtype)


def unproject(grads, which, group, begin, before, dtype, device):
    mp = lax.axis_size("mp")
    rows, count = grads[0].shape
    full, width = group.full, group.width
    return pl.pallas_call(
        functools.partial(
            unproject_kernel, group, which, begin, count // width, before is not None
        ),
        grid_spec=pltpu.PrefetchScalarGridSpec(
            num_scalar_prefetch=1,
            grid=(count // width,),
            in_specs=[pl.BlockSpec((rows, width), lambda i, *_: (0, i))] * len(grads)
            + ([] if before is None else [whole((rows, full))])
            + group.specs(),
            out_specs=whole((rows, full)),
            scratch_shapes=group.scratch(mp, [0, 1, 2]) + [pltpu.VMEM((rows, full), F32)],
        ),
        out_shape=jax.ShapeDtypeStruct((rows, full), dtype),
        name="unproject",
        compiler_params=pltpu.CompilerParams(vmem_limit_bytes=48 << 20),
        cost_estimate=LIGHT,
    )(device.reshape(1), *grads, *([] if before is None else [before]), *group.inputs)


def other_half_kernel(scal, left_ref, right_ref, out_ref):
    out_ref[...] = dot_tn(left_ref[...], right_ref[...]).astype(BF16)


def split_rows(total, bit_at, bit, outs):
    send_ref, keep_ref = outs
    count, rows, _ = send_ref.shape
    for j in range(count):
        base = ((j >> bit_at) << (bit_at + 1)) | (j & ((1 << bit_at) - 1))
        for ref, value in ((send_ref, 1 - bit), (keep_ref, bit)):
            start = pl.multiple_of((base + (value << bit_at)) * rows, rows)
            ref[j] = total[pl.ds(start, rows), :].astype(BF16)


def this_half_kernel(bits_at, scal, left_ref, right_ref, got_ref, *refs):
    outs, total = refs[:-1], refs[-1]
    total[...] = dot_tn(left_ref[...], right_ref[...]) + got_ref[...].astype(F32)
    step = pl.program_id(0)
    count = pl.num_programs(0) // 2
    for side in range(2):

        @pl.when(step // count == side)
        def _():
            split_rows(
                total,
                bits_at[side],
                (scal[0] >> (bits_at[side] + 1)) & 1,
                outs[2 * side : 2 * side + 2],
            )


def first_bits():
    along_x, along_y = chip_masks(lax.axis_size("dp"))
    return [order[0].bit_length() - 2 for order in (along_x + along_y, along_y + along_x)]


def other_half(left, right, device):
    rows, full = left.shape
    size = right.shape[1] // lax.axis_size("mp")
    return pl.pallas_call(
        other_half_kernel,
        grid_spec=pltpu.PrefetchScalarGridSpec(
            num_scalar_prefetch=1,
            grid=(right.shape[1] // size,),
            in_specs=[
                pl.BlockSpec((rows, full // 2), lambda i, scal: (0, 1 - scal[0] % 2)),
                pl.BlockSpec((rows, size), lambda i, scal: (0, i)),
            ],
            out_specs=pl.BlockSpec((full // 2, size), lambda i, scal: (0, i)),
        ),
        out_shape=jax.ShapeDtypeStruct((full // 2, right.shape[1]), BF16),
        name="other_half",
        compiler_params=pltpu.CompilerParams(vmem_limit_bytes=32 << 20),
        cost_estimate=LIGHT,
    )(device.reshape(1), left, right)


def this_half(left, right, got, device):
    rows, full = left.shape
    mp = lax.axis_size("mp")
    size = right.shape[1] // mp
    quarters = lax.axis_size("dp") // 2
    shape = (quarters // 2, full // 2 // quarters, mp // 2 * size)
    block = (quarters // 2, full // 2 // quarters, size)
    last = mp // 2 - 1
    sides = [lambda i, scal: (0, 0, jnp.minimum(i, last))] * 2 + [
        lambda i, scal: (0, 0, jnp.maximum(i - last - 1, 0))
    ] * 2
    return pl.pallas_call(
        functools.partial(this_half_kernel, first_bits()),
        grid_spec=pltpu.PrefetchScalarGridSpec(
            num_scalar_prefetch=1,
            grid=(mp,),
            in_specs=[
                pl.BlockSpec((rows, full // 2), lambda i, scal: (0, scal[0] % 2)),
                pl.BlockSpec((rows, size), lambda i, scal: (0, i)),
                pl.BlockSpec((full // 2, size), lambda i, scal: (0, i)),
            ],
            out_specs=[pl.BlockSpec(block, index) for index in sides],
            scratch_shapes=[pltpu.VMEM((full // 2, size), F32)],
        ),
        out_shape=[jax.ShapeDtypeStruct(shape, BF16)] * 4,
        name="this_half",
        compiler_params=pltpu.CompilerParams(vmem_limit_bytes=40 << 20),
        cost_estimate=LIGHT,
    )(device.reshape(1), left, right, got)


def attention_dots(width, lefts, branch, grads, attended, layer, put):
    grad_q, near_k, near_v, far_k, far_v = grads
    rows = grad_q.shape[0]
    columns = slice(layer * width, (layer + 1) * width)
    put(0, dot_tn(lefts[-1][...], grad_q[:, columns]))
    for index, near, far in ((1, near_k, far_k), (2, near_v, far_v)):
        total = dot_tn(lefts[-1][...], near[:, columns])
        for block in range(len(lefts) - 1):
            total = total + dot_tn(lefts[block][...], far[block * rows : (block + 1) * rows, columns])
        put(index, total)
    put(3, dot_tn(branch[...], attended[:, columns]))


def attention_other_kernel(width, blocks, scal, *refs):
    lefts, (branch, *grads, attended, out_ref) = refs[:blocks], refs[blocks:]
    for layer in range(attended.shape[1] // width):

        def put(index, value):
            place = (layer * 4 + index) * width
            out_ref[:, place : place + width] = value.astype(BF16)

        attention_dots(width, lefts, branch, grads, attended, layer, put)


def attention_this_kernel(width, blocks, bits_at, scal, *refs):
    lefts, (branch, *grads, attended, got_ref) = refs[:blocks], refs[blocks : blocks + 8]
    outs, total = refs[blocks + 8 : -1], refs[-1]
    layers = attended.shape[1] // width
    for side in range(2):
        for local in range(layers // 2):
            layer = side * (layers // 2) + local

            def put(index, value):
                place = (layer * 4 + index) * width
                total[:, index * width : (index + 1) * width] = value + got_ref[
                    :, place : place + width
                ].astype(F32)

            attention_dots(width, lefts, branch, grads, attended, layer, put)
            columns = pl.ds(local * 4 * width, 4 * width)
            split_rows(
                total,
                bits_at[side],
                (scal[0] >> (bits_at[side] + 1)) & 1,
                [ref.at[:, :, columns] for ref in outs[2 * side : 2 * side + 2]],
            )


def attention_specs(normed, branch, grads, part, core_of):
    rows, full = branch.shape
    left = pl.BlockSpec((rows, full // 2), lambda i, scal: (0, core_of(scal)))
    wide = grads[0].shape[1]
    some = lambda height: pl.BlockSpec((height, wide), lambda i, scal: (0, part))
    return (
        [left] * (len(normed) + 1)
        + [whole(g.shape) for g in grads[:3]]
        + [some(g.shape[0]) for g in grads[3:]]
        + [some(rows)]
    )


def attention_other(normed, branch, grads, attended, part, width, device):
    full = branch.shape[1]
    out = (full // 2, 4 * grads[0].shape[1])
    return pl.pallas_call(
        functools.partial(attention_other_kernel, width, len(normed)),
        grid_spec=pltpu.PrefetchScalarGridSpec(
            num_scalar_prefetch=1,
            grid=(1,),
            in_specs=attention_specs(normed, branch, grads, part, lambda s: 1 - s[0] % 2),
            out_specs=whole(out),
        ),
        out_shape=jax.ShapeDtypeStruct(out, BF16),
        name="attention_other",
        compiler_params=pltpu.CompilerParams(vmem_limit_bytes=40 << 20),
        cost_estimate=LIGHT,
    )(device.reshape(1), *normed, branch, *grads, attended)


def attention_this(normed, branch, grads, attended, got, part, width, device):
    full = branch.shape[1]
    quarters = lax.axis_size("dp") // 2
    shape = (quarters // 2, full // 2 // quarters, 2 * grads[0].shape[1])
    return pl.pallas_call(
        functools.partial(attention_this_kernel, width, len(normed), first_bits()),
        grid_spec=pltpu.PrefetchScalarGridSpec(
            num_scalar_prefetch=1,
            grid=(1,),
            in_specs=attention_specs(normed, branch, grads, part, lambda s: s[0] % 2)
            + [whole(got.shape)],
            out_specs=[whole(shape)] * 4,
            scratch_shapes=[pltpu.VMEM((full // 2, 4 * width), F32)],
        ),
        out_shape=[jax.ShapeDtypeStruct(shape, BF16)] * 4,
        name="attention_this",
        compiler_params=pltpu.CompilerParams(vmem_limit_bytes=48 << 20),
        cost_estimate=LIGHT,
    )(device.reshape(1), *normed, branch, *grads, attended, got)


def next_stage_kernel(scal, *refs):
    ins, outs = refs[:8], refs[8:]
    for index, out in enumerate(outs):
        one, two = ins[2 * index], ins[2 * index + 1]
        out[...] = (one[0].astype(F32) + two[0].astype(F32)).astype(BF16)


def next_stage(keeps, gots, bits, device):
    _, rows, columns = keeps[0].shape
    specs, inputs = [], []
    for side in range(2):
        for flip in (1, 0):
            where = lambda i, scal, side=side, flip=flip: (
                ((scal[0] >> (bits[side] + 1)) & 1) ^ flip,
                0,
                0,
            )
            specs += [pl.BlockSpec((1, rows, columns), where)] * 2
            inputs += [keeps[side], gots[side]]
    return pl.pallas_call(
        next_stage_kernel,
        grid_spec=pltpu.PrefetchScalarGridSpec(
            num_scalar_prefetch=1,
            grid=(1,),
            in_specs=specs,
            out_specs=[whole((rows, columns))] * 4,
        ),
        out_shape=[jax.ShapeDtypeStruct((rows, columns), BF16)] * 4,
        name="next_stage",
        compiler_params=pltpu.CompilerParams(vmem_limit_bytes=32 << 20),
        cost_estimate=LIGHT,
    )(device.reshape(1), *inputs)


def by_layer_kernel(places, keep_a, got_a, keep_b, got_b, send_ref, rest_ref):
    width = send_ref.shape[2]
    each = len(places) // 2
    for index, (sent, spot) in enumerate(places):
        keep, got = ((keep_a, got_a), (keep_b, got_b))[index // each]
        columns = slice(index % each * width, (index % each + 1) * width)
        value = keep[:, columns].astype(F32) + got[:, columns].astype(F32)
        if sent:
            send_ref[spot] = value.astype(BF16)
        else:
            rest_ref[spot] = value


def by_layer_pieces(keeps, gots, layers):
    rows = keeps[0].shape[0]
    width = keeps[0].shape[1] * 2 // len(layers)
    odd = [r for r in layers if r & 1]
    even = [r for r in layers if not r & 1]
    places = [(r & 1, (odd if r & 1 else even).index(r)) for r in layers]
    send, rest = pl.pallas_call(
        functools.partial(by_layer_kernel, places),
        out_shape=[
            jax.ShapeDtypeStruct((len(odd), rows, width), BF16),
            jax.ShapeDtypeStruct((len(even), rows, width), F32),
        ],
        in_specs=[pl.BlockSpec(memory_space=pltpu.VMEM)] * 4,
        out_specs=[pl.BlockSpec(memory_space=pltpu.VMEM)] * 2,
        name="by_layer_pieces",
        compiler_params=pltpu.CompilerParams(vmem_limit_bytes=32 << 20),
        cost_estimate=LIGHT,
    )(keeps[0], gots[0], keeps[1], gots[1])
    return send, rest, odd, even


def reduce_flow(send, add, layers, device):
    (send,) = yield (send,)
    (got,) = yield (swap(send, "dp", 1),)
    send_a, keep_a, send_b, keep_b = add(got)
    along_x, along_y = chip_masks(lax.axis_size("dp"))
    orders = (along_x + along_y, along_y + along_x)
    bits = len(orders[0])
    sends, keeps = [send_a, send_b], [keep_a, keep_b]
    lefts = []
    for side, order in enumerate(orders):
        left = list(range(bits - 1, -1, -1))
        left.remove(order[0].bit_length() - 2)
        lefts.append(left)
        keeps[side] = keeps[side].reshape((2,) * (bits - 1) + keeps[side].shape[1:])
    for step in range(bits):
        sends = yield tuple(sends)
        gots = yield tuple(swap(value, "dp", order[step]) for value, order in zip(sends, orders))
        gots = [got.reshape(keep.shape) for got, keep in zip(gots, keeps)]
        if step + 1 == bits:
            break
        picks = [order[step + 1].bit_length() - 2 for order in orders]
        if keeps[0].ndim == 3:
            send_a, keep_a, send_b, keep_b = next_stage(keeps, gots, picks, device)
            sends, keeps = [send_a, send_b], [keep_a, keep_b]
            continue
        sends, next_keeps = [], []
        for side, which in enumerate(picks):
            axis = lefts[side].index(which)
            lefts[side].remove(which)
            bit = (device >> (which + 1)) & 1

            def part(value):
                summed = [
                    lax.dynamic_index_in_dim(item, value, axis, keepdims=False).astype(F32)
                    for item in (keeps[side], gots[side])
                ]
                return (summed[0] + summed[1]).astype(BF16)

            sends.append(part(1 - bit))
            next_keeps.append(part(bit))
        keeps = next_keeps
    send, rest, odd, even = by_layer_pieces(keeps, gots, layers)
    (send,) = yield (send,)
    (got,) = yield (swap(send, "mp", 1),)
    held = {r: rest[i] for i, r in enumerate(even)}
    for i, r in enumerate(odd):
        value = got[i].astype(F32)
        held[r ^ 1] = held[r ^ 1] + value if r ^ 1 in held else value
    for bit in range(1, lax.axis_size("mp").bit_length() - 1):
        mask = 1 << bit
        away = [r for r in sorted(held) if r & mask]
        if away:
            send = held[away[0]] if len(away) == 1 else jnp.stack([held[r] for r in away])
            (send,) = yield (send.astype(BF16),)
            (got,) = yield (swap(send, "mp", mask),)
            got = [got] if len(away) == 1 else list(got)
            for r, value in zip(away, got):
                del held[r]
                value = value.astype(F32)
                held[r ^ mask] = held[r ^ mask] + value if r ^ mask in held else value
    return held[0]


def fill_kernel(plan, rows, dp, scal, *refs):
    ins, (qkv_ref, out_ref, turned) = refs[:-3], refs[-3:]
    width = turned.shape[1]
    for ref, (side, masks) in zip(ins, plan):
        for index, mask in enumerate(masks):
            place = pl.ds(pl.multiple_of(position(scal[0], mask, dp) * rows, rows), rows)
            for inner in range(2):
                value = ref[index, :, inner * width : (inner + 1) * width].astype(F32)
                if side * 2 + inner < 3:
                    qkv_ref[side * 2 + inner, place, :] = value
                else:
                    turned[place, :] = value
    out_ref[...] = turned[...].T


def fill_attention(arrays, full, width, device):
    dp = lax.axis_size("dp")
    inputs = [value for _, _, value in arrays]
    vmem = pl.BlockSpec(memory_space=pltpu.VMEM)
    return pl.pallas_call(
        functools.partial(fill_kernel, [(side, m) for side, m, _ in arrays], full // dp, dp),
        grid_spec=pltpu.PrefetchScalarGridSpec(
            num_scalar_prefetch=1,
            grid=(),
            in_specs=[vmem] * len(inputs),
            out_specs=[vmem, vmem],
            scratch_shapes=[pltpu.VMEM((full, width), F32)],
        ),
        out_shape=[
            jax.ShapeDtypeStruct((3, full, width), F32),
            jax.ShapeDtypeStruct((width, full), F32),
        ],
        name="fill_attention",
        compiler_params=pltpu.CompilerParams(vmem_limit_bytes=32 << 20),
        cost_estimate=LIGHT,
    )(device.reshape(1), *inputs)


def fill_ffn_kernel(turn, in_ref, out_ref):
    group, _, rows, hidden = in_ref.shape
    value = in_ref[...].astype(F32).reshape(group * rows, hidden)
    out_ref[...] = value.T if turn else value


def fill_ffn(gathered, turn):
    dp, rows, hidden = gathered.shape
    quarters = dp // 2
    group = quarters
    count = quarters // group
    full = dp * rows
    block = (hidden, group * rows) if turn else (group * rows, hidden)
    shape = (hidden, full) if turn else (full, hidden)
    where = (lambda c, j: (0, c * count + j)) if turn else (lambda c, j: (c * count + j, 0))
    return pl.pallas_call(
        functools.partial(fill_ffn_kernel, turn),
        grid=(2, count),
        in_specs=[pl.BlockSpec((group, 1, rows, hidden), lambda c, j: (j, c, 0, 0))],
        out_specs=pl.BlockSpec(block, where),
        out_shape=jax.ShapeDtypeStruct(shape, F32),
        name="fill_ffn",
        compiler_params=pltpu.CompilerParams(vmem_limit_bytes=24 << 20),
        cost_estimate=LIGHT,
    )(gathered.reshape(quarters, 2, rows, hidden))


def small_flow(value):
    for axis in ("dp", "mp"):
        for bit in range(lax.axis_size(axis).bit_length() - 1):
            (value,) = yield (value,)
            (got,) = yield (swap(value, axis, 1 << bit),)
            value = value + got
    return value


def spread_flow(sides):
    return (yield from spread_steps(sides))


def finish(flows, *values):
    while any(not flow.over for flow in flows):
        out = meet(flows, *values)
        values = out if len(values) > 1 else (out,)
    return values


def drain(*flows):
    for flow in flows:
        while not flow.over:
            flow.move(flow.held)


def eight_rows(*rows):
    stacked = jnp.stack([row.astype(F32) for row in rows])
    return jnp.pad(stacked, ((0, 8 - stacked.shape[0]), (0, 0)))


def on_device(
    tokens,
    groups,
    lengths,
    qkv_weight,
    qv_bias,
    out_weight,
    out_bias,
    up_weight,
    up_bias,
    down_weight,
    down_bias,
    norm_gain,
    norm_bias,
    group_table,
    cotangent,
):
    dp, mp = lax.axis_size("dp"), lax.axis_size("mp")
    device, layer = lax.axis_index("dp"), lax.axis_index("mp")
    core = device & 1
    rows, full = tokens.shape
    width = qkv_weight.shape[2]
    hidden = up_weight.shape[1]
    blocks = SEQ_LEN // rows
    place_in_seq = layer % blocks
    length = lax.dynamic_index_in_dim(lengths, layer // blocks, keepdims=False)
    along_x, along_y = chip_masks(dp)
    stages = len(along_x + along_y)
    gains = norm_gain.astype(F32)
    shifts = norm_bias.astype(F32)
    part, half = full // 2, full // 2

    shard_a = [(qkv_weight, 0, False), (out_weight, 3, True)]
    shard_u, shard_d = [(up_weight[None], 0, False)], [(down_weight, 0, True)]
    small_here = jnp.concatenate([qv_bias[0], qv_bias[1], up_bias]).reshape(-1, width)
    n_small = small_here.shape[0]
    small_here = jnp.pad(small_here, ((0, -n_small % 16), (0, 0)))
    slice_a = jnp.concatenate(
        [
            own_slice(qkv_weight, False, device, width),
            own_slice(out_weight, True, device, width),
        ]
    )
    flow_a = Flow(gather_flow(slice_a, small_here))
    tokens = begin([flow_a], tokens)

    order_of = layer ^ jnp.arange(mp)
    onehot = (
        groups[:, None] == lax.broadcasted_iota(jnp.int32, (1, group_table.shape[0]), 1)
    ).astype(BF16)
    residual = tokens.astype(F32) + jnp.dot(onehot, group_table, preferred_element_type=F32)
    normed, norm_one, inv_one = norm_forward(residual, gains[0], shifts[0])
    normed_low = normed.astype(BF16)

    def rows_flow(value):
        (value,) = yield (value,)
        return (yield tuple(swap(value, "mp", m) for m in range(1, blocks)))

    key_ids = lax.broadcasted_iota(jnp.int32, (blocks, rows, 1), 1)
    block_ids = lax.broadcasted_iota(jnp.int32, (blocks, rows, 1), 0)
    block_ids = place_in_seq ^ ((block_ids + 1) % blocks)
    shown = (block_ids <= place_in_seq) & (block_ids * rows + key_ids < length)
    spot = lax.broadcasted_iota(jnp.int32, (blocks, rows, LANES), 2) % HEAD_DIM
    key_const = jnp.where(
        spot == 0,
        jnp.where(shown, 0.0, MASKED_SCORE),
        jnp.where(spot <= 3, 1.0, 0.0),
    )
    key_const = key_const.astype(BF16).reshape(blocks * rows, LANES)

    slice_u = own_slice(up_weight[None], False, device, hidden)
    slice_d = own_slice(down_weight, True, device, hidden)
    flow_r = Flow(rows_flow(normed_low))
    normed_low, slice_u, slice_d = meet([flow_a], normed_low, slice_u, slice_d)
    flow_u, flow_d = Flow(gather_flow(slice_u)), Flow(gather_flow(slice_d))
    layer_stages = mp.bit_length() - 1
    for _ in range(layer_stages - 1):
        normed_low = meet([flow_a], normed_low)
    normed_low = begin([flow_r, flow_u], normed_low)
    for _ in range(stages - 1):
        normed_low = meet([flow_a], normed_low)
    normed_low = meet([flow_a, flow_u, flow_r], normed_low)
    for _ in range(layer_stages - 2):
        normed_low = meet([flow_u], normed_low)
    normed_low = meet([flow_a, flow_u], normed_low)
    normed_low = begin([flow_d], normed_low)
    arrays_a, small_all = flow_a.result
    group_a = Weights(shard_a, arrays_a)
    small_all = jnp.stack(small_all)[:, :n_small].reshape(mp, -1).astype(F32)
    qv_rows = small_all[:, : 2 * width].reshape(mp, 2, width).transpose(1, 0, 2).reshape(2, full)
    u_rows = small_all[:, 2 * width :].reshape(1, -1)
    qv_rows = jnp.pad(qv_rows, ((0, 6), (0, 0)))
    u_rows = jnp.pad(u_rows, ((0, 7), (0, 0)))
    seq_normed = tuple(flow_r.result) + (normed_low,)
    queries, keys, values = project(seq_normed, qv_rows, group_a, device)
    queries, keys, values = meet([flow_d, flow_u], queries, keys, values)
    attended_a, aug_a = attend(queries, keys, values, key_const, 0, part)
    for _ in range(layer_stages - 1):
        attended_a, queries = meet([flow_d], attended_a, queries)
    attended_b, aug_b = attend(queries, keys, values, key_const, part, part)
    attended = jnp.concatenate([attended_a, attended_b], axis=1)
    aug = jnp.concatenate([aug_a, aug_b], axis=1)
    attended_b = meet([flow_u, flow_d], attended_b)
    for _ in range(stages - 2):
        attended_b = meet([flow_d], attended_b)
    (attended_b,) = finish([flow_u], attended_b)
    group_u = Weights(shard_u, flow_u.result[0])
    branch, middle, mid_low, act, slope = feed_up(
        attended_a,
        attended_b,
        residual,
        eight_rows(out_bias, gains[1], shifts[1], gains[2], shifts[2]),
        u_rows,
        group_a,
        group_u,
        device,
    )
    (act,) = finish([flow_d], act)
    group_d = Weights(shard_d, flow_d.result[0])
    output, grad_ffn, sums_ffn = feed_down(
        act, middle, cotangent, eight_rows(down_bias, gains[3], shifts[3]), group_d, device
    )

    everyone = list(range(mp))

    def weight_flow(left, right):
        return Flow(
            reduce_flow(
                other_half(left, right, device),
                lambda got: this_half(left, right, got, device),
                everyone,
                device,
            )
        )

    flow_d = weight_flow(grad_ffn, act)
    grad_ffn = begin([flow_d], grad_ffn)
    grad_ffn = meet([flow_d], grad_ffn)
    grad_pre, grad_middle, grad_branch, grad_attended, sums_back, sums_up = feed_back(
        grad_ffn,
        slope,
        branch,
        middle,
        cotangent,
        eight_rows(gains[2], gains[1]),
        group_a,
        group_u,
        group_d,
        device,
    )
    grad_pre, grad_branch, grad_attended = meet([flow_d], grad_pre, grad_branch, grad_attended)
    flow_u = weight_flow(mid_low, grad_pre)
    grad_branch, grad_attended = begin([flow_u], grad_branch, grad_attended)

    def attention_flow(grads, layers):
        index = layers[0] * width // part
        return Flow(
            reduce_flow(
                attention_other(seq_normed, grad_branch, grads, attended, index, width, device),
                lambda got: attention_this(
                    seq_normed, grad_branch, grads, attended, got, index, width, device
                ),
                layers,
                device,
            )
        )

    layers_b, layers_a = everyone[: mp // 2], everyone[mp // 2 :]
    back = functools.partial(
        attend_back, queries, keys, values, key_const, aug, grad_attended, attended
    )
    far_q, far_k, far_v = back(0, full)
    far_grad = unproject((far_k, far_v), (1, 2), group_a, 0, None, BF16, device)
    far_grad, far_q, far_k, far_v = ordered([flow_d, flow_u], (far_grad, far_q, far_k, far_v))
    flow_f = Flow(rows_back(far_grad, rows, blocks))
    far_q, far_k, far_v = begin([flow_f, flow_u], far_q, far_k, far_v)
    grads_a = back(part, part, far_q)
    flow_qa = attention_flow((*grads_a, far_k, far_v), layers_a)
    far_q, *grads_a = meet([flow_u, flow_f], far_q, *grads_a)
    far_q, *grads_a = begin([flow_qa], far_q, *grads_a)
    near_a = unproject(grads_a, (0, 1, 2), group_a, mp // 2, None, F32, device)
    far_q, near_a = meet([flow_qa], far_q, near_a)
    far_q, near_a = begin([flow_d], far_q, near_a)
    grads_b = back(0, part, far_q)
    grads_b = ordered([flow_u, flow_qa, flow_d], grads_b)
    flow_qb = attention_flow((*grads_b, far_k, far_v), layers_b)
    grads_b = begin([flow_qb], *grads_b)
    grads_b = begin([flow_u, flow_qa, flow_d], *grads_b)
    near_b = unproject(grads_b, (0, 1, 2), group_a, 0, near_a, F32, device)
    near_b, *grads_a, sums_ffn, sums_back, sums_up = meet(
        [flow_qb, flow_qa, flow_u, flow_d], near_b, *grads_a, sums_ffn, sums_back, sums_up
    )
    drain(flow_d)
    down_mine = flow_d.result.astype(BF16)
    down_all = lax.all_gather(down_mine, "dp", axis=0)
    grad_normed = near_b
    for value in flow_f.result:
        grad_normed = grad_normed + value.astype(F32)
    back_one, gain_one, shift_one = norm_backward(grad_normed, norm_one, inv_one, gains[0])
    input_grad = grad_middle + back_one
    table_part = jnp.dot(
        onehot.astype(F32).T, input_grad, precision=PRECISE, preferred_element_type=F32
    )
    grad_q_sum = jnp.concatenate([jnp.sum(g[0].astype(F32), axis=0) for g in (grads_b, grads_a)])
    grad_v_sum = jnp.concatenate([jnp.sum(g[2].astype(F32), axis=0) for g in (grads_b, grads_a)])
    grad_v_sum = grad_v_sum + jnp.sum(far_v.astype(F32), axis=0)
    ffn_sums = jnp.sum(sums_ffn.reshape(3, 8, full), axis=1)
    back_sums = jnp.sum(sums_back.reshape(5, 8, full), axis=1)
    up_bias_part = jnp.sum(sums_up, axis=0)
    by_layer = jnp.concatenate(
        [grad_q_sum.reshape(mp, -1), grad_v_sum.reshape(mp, -1), up_bias_part.reshape(mp, -1)],
        axis=1,
    )
    by_layer = jnp.take(by_layer, order_of, axis=0)
    wide = by_layer.shape[1]
    by_layer = jnp.pad(by_layer, ((0, 0), (0, -wide % full))).reshape(-1, full)
    input_grad, table_part, gain_one, shift_one = meet(
        [flow_qb, flow_qa, flow_u], input_grad, table_part, gain_one, shift_one
    )
    drain(flow_u)
    up_mine = flow_u.result.astype(BF16)
    up_all = lax.all_gather(up_mine, "dp", axis=0)
    parts = jnp.concatenate(
        [
            jnp.stack([gain_one, back_sums[2], back_sums[0], ffn_sums[0]]),
            jnp.stack([shift_one, back_sums[3], back_sums[1], ffn_sums[1]]),
            jnp.stack([back_sums[4], ffn_sums[2]]),
            table_part,
            by_layer,
        ]
    )
    flow_s = Flow(small_flow(parts))
    drain(flow_qa, flow_qb)
    mine = (flow_qa.result + flow_qb.result).astype(BF16)
    flow_o = Flow(spread_flow((mine[:, : 2 * width], mine[:, 2 * width :])))
    for _ in range(2 * stages):
        flow_o.move(flow_o.held)
    down_grad = fill_ffn(down_all, True)
    up_grad = fill_ffn(up_all, False)
    down_grad, up_grad = begin([flow_o], down_grad, up_grad)
    drain(flow_o, flow_s)
    qkv_grad, out_grad = fill_attention(flow_o.result, full, width, device)

    parts = flow_s.result
    gain_grad, shift_grad = parts[:4], parts[4:8]
    out_bias_grad, down_bias_grad = parts[8], parts[9]
    n_groups = group_table.shape[0]
    table_grad = parts[10 : 10 + n_groups]
    by_layer = parts[10 + n_groups :].reshape(mp, -1)
    mine = lax.dynamic_index_in_dim(by_layer, layer, keepdims=False)
    qv_bias_grad = mine[: 2 * width].reshape(2, width)
    up_bias_grad = mine[2 * width : 2 * width + hidden]
    return (
        output,
        input_grad,
        qkv_grad,
        qv_bias_grad,
        out_grad,
        out_bias_grad,
        up_grad,
        up_bias_grad,
        down_grad,
        down_bias_grad,
        gain_grad,
        shift_grad,
        table_grad,
    )


def rows_back(value, rows, blocks):
    (value,) = yield (value,)
    return (
        yield tuple(swap(value[(m - 1) * rows : m * rows], "mp", m) for m in range(1, blocks))
    )


def solution(mesh):
    placed = (
        P(("dp", "mp"), None),
        P(("dp", "mp")),
        P("dp"),
        P(None, None, "mp"),
        P(None, "mp"),
        P("mp", None),
        P(),
        P(None, "mp"),
        P("mp"),
        P("mp", None),
        P(),
        P(),
        P(),
        P(),
        P(("dp", "mp"), None),
    )
    return jax.shard_map(
        on_device,
        mesh=mesh,
        in_specs=placed,
        out_specs=(
            P(("dp", "mp"), None),
            P(("dp", "mp"), None),
            P(None, None, "mp"),
            P(None, "mp"),
            P("mp", None),
            P(),
            P(None, "mp"),
            P("mp"),
            P("mp", None),
            P(),
            P(),
            P(),
            P(),
        ),
        check_vma=False,
    )
```

```python
import functools
import math

import jax
import jax.numpy as jnp
from jax import lax
from jax.experimental import pallas as pl
from jax.experimental.pallas import tpu as pltpu
from jax.sharding import PartitionSpec as P

HEAD_DIM = 64
SEQ_LEN = 1088
RELAX_ALPHA = 32.0
NORM_EPSILON = 1e-05
MASKED_SCORE = -1000000000.0
PRECISE = lax.Precision.HIGHEST
BF16 = jnp.bfloat16
F32 = jnp.float32
LANES = 128
LIGHT = pl.CostEstimate(flops=1000, bytes_accessed=1000, transcendentals=0)


def swap(value, axis, mask):
    count = lax.axis_size(axis)
    return lax.ppermute(value, axis, [(i, i ^ mask) for i in range(count)])


def normalize(inputs):
    centred = inputs - jnp.mean(inputs, axis=-1, keepdims=True)
    factor = lax.rsqrt(jnp.mean(centred * centred, axis=-1, keepdims=True) + NORM_EPSILON)
    return centred * factor, factor


def norm_forward(inputs, gain_row, shift_row):
    centred = inputs - jnp.mean(inputs, axis=-1, keepdims=True)
    factor = lax.rsqrt(jnp.mean(centred * centred, axis=-1, keepdims=True) + NORM_EPSILON)
    normal = centred * factor
    return (normal * gain_row + shift_row, normal, factor)


def norm_backward(upstream, normal, factor, gain_row):
    scaled = upstream * gain_row
    adjusted = (
        scaled
        - jnp.mean(scaled, axis=-1, keepdims=True)
        - normal * jnp.mean(scaled * normal, axis=-1, keepdims=True)
    )
    return (adjusted * factor, jnp.sum(upstream * normal, axis=0), jnp.sum(upstream, axis=0))


def dot_nn(a, b):
    return lax.dot_general(a, b, (((1,), (0,)), ((), ())), preferred_element_type=F32)


def dot_nt(a, b):
    return lax.dot_general(a, b, (((1,), (1,)), ((), ())), preferred_element_type=F32)


def dot_tn(a, b):
    return lax.dot_general(a, b, (((0,), (0,)), ((), ())), preferred_element_type=F32)


def query_tile(rows):
    return rows // 2 if (rows // 2) % 16 == 0 else rows


def padded(rows):
    return -(-rows // LANES) * LANES


def three_parts(value):
    high = value.astype(BF16)
    rest = value - high.astype(F32)
    mid = rest.astype(BF16)
    return high, mid, (rest - mid.astype(F32)).astype(BF16)


def attend_kernel(blocks, rows, q_ref, k_ref, v_ref, kc_ref, out_ref, aug_ref):
    tile = query_tile(rows)
    far = (blocks - 1) * rows
    lane = lax.broadcasted_iota(jnp.int32, (1, LANES), 1)
    first = lane < HEAD_DIM
    mine = [first, jnp.logical_not(first)]
    keys = jnp.concatenate([k_ref[...], kc_ref[...]], axis=1)
    special = jnp.where(lane == 0, 1.0, 0.0).astype(BF16)
    special = jnp.broadcast_to(special, (tile, LANES))
    starts = list(range(0, rows, tile))

    def scores_of(start):
        q = q_ref[start : start + tile, :]
        zero = jnp.zeros_like(q)
        both = jnp.concatenate(
            [jnp.concatenate([jnp.where(m, q, zero), special], axis=1) for m in mine], axis=0
        )
        return dot_nt(both, keys[: far + start + tile])

    scores = [scores_of(start) for start in starts]
    for start, score in zip(starts, scores):
        limit = far + start + tile
        cut = (far + start) // LANES * LANES
        row_ids = lax.broadcasted_iota(jnp.int32, (2 * tile, limit - cut), 0)
        row_ids = start + far - cut + jnp.where(row_ids >= tile, row_ids - tile, row_ids)
        columns = lax.broadcasted_iota(jnp.int32, (2 * tile, limit - cut), 1)
        last = jnp.where(columns <= row_ids, score[:, cut:], MASKED_SCORE)
        score = jnp.concatenate([score[:, :cut], last], axis=1) if cut else last
        top = jnp.max(score, axis=-1, keepdims=True)
        exponent = jnp.exp(score - top)
        total = jnp.sum(exponent, axis=-1, keepdims=True)
        gathered = dot_nn(exponent.astype(BF16), v_ref[0:limit, :]) / total
        out_ref[start : start + tile, :] = jnp.where(
            first, gathered[:tile], gathered[tile:]
        ).astype(BF16)
        parts = three_parts(-(top + jnp.log(total)))
        spot = lane % HEAD_DIM
        augs = []
        for head in range(2):
            aug = jnp.where(spot == 0, 1.0, jnp.zeros((tile, LANES), F32)).astype(BF16)
            for index, value in enumerate(parts):
                aug = jnp.where(spot == index + 1, value[head * tile : (head + 1) * tile], aug)
            augs.append(aug)
        aug_ref[start : start + tile, :] = jnp.where(first, augs[0], augs[1])


def attend(queries, keys, values, key_const, begin, count):
    rows = queries.shape[0]
    span = keys.shape[0]
    first = begin // LANES
    pair = lambda height: pl.BlockSpec((height, LANES), lambda i: (0, first + i))
    made = lambda height: pl.BlockSpec((height, LANES), lambda i: (0, i))
    return pl.pallas_call(
        functools.partial(attend_kernel, span // rows, rows),
        grid=(count // LANES,),
        in_specs=[
            pair(rows),
            pair(span),
            pair(span),
            pl.BlockSpec((span, LANES), lambda i: (0, 0)),
        ],
        out_specs=[made(rows), made(rows)],
        out_shape=[
            jax.ShapeDtypeStruct((rows, count), BF16),
            jax.ShapeDtypeStruct((rows, count), BF16),
        ],
        name="attend",
        compiler_params=pltpu.CompilerParams(vmem_limit_bytes=24 << 20),
        cost_estimate=LIGHT,
    )(queries, keys, values, key_const)


def attend_back_kernel(
    causal, q_ref, k_ref, v_ref, kc_ref, aug_ref, go_ref, out_ref, *refs
):
    before, refs = (refs[0], refs[1:]) if causal else (None, refs)
    dq_ref, dk_ref, dv_ref, q_both, g_both, ds_ref = refs
    rows = q_ref.shape[0]
    span = k_ref.shape[0]
    key_tile = query_tile(rows)
    wide = padded(rows)
    lane = lax.broadcasted_iota(jnp.int32, (1, LANES), 1)
    first = lane < HEAD_DIM
    mine = [first, jnp.logical_not(first)]
    q_pair, aug, go = q_ref[...], aug_ref[...], go_ref[...]
    zero = jnp.zeros_like(q_pair)
    weighed = go.astype(F32) * out_ref[...].astype(F32)
    pad = jnp.zeros((wide - rows, 2 * LANES), BF16)
    for head in range(2):
        m = mine[head]
        place = head * wide
        q_both[place : place + rows, 0:LANES] = jnp.where(m, q_pair, zero)
        q_both[place : place + rows, LANES:] = jnp.where(m, aug, zero)
        parts = three_parts(-jnp.sum(jnp.where(m, weighed, 0.0), axis=-1, keepdims=True))
        g_aug = zero
        for index, value in enumerate(parts):
            g_aug = jnp.where(lane == index + 1, value, g_aug)
        g_both[place : place + rows, 0:LANES] = jnp.where(m, go, zero)
        g_both[place : place + rows, LANES:] = g_aug
        if wide > rows:
            q_both[place + rows : place + wide, :] = pad
            g_both[place + rows : place + wide, :] = pad
    keys = jnp.concatenate([k_ref[...], kc_ref[...]], axis=1)
    v_const = jnp.where((lane >= 1) & (lane <= 3), 1.0, 0.0).astype(BF16)
    values = jnp.concatenate([v_ref[...], jnp.broadcast_to(v_const, k_ref.shape)], axis=1)

    def dots_of(start):
        stop = start + key_tile
        return dot_nt(keys[start:stop], q_both[...]), dot_nt(values[start:stop], g_both[...])

    starts = list(range(0, span, key_tile))
    ahead = dots_of(starts[0])
    for index, start in enumerate(starts):
        stop = start + key_tile
        scores, centred = ahead
        if index + 1 < len(starts):
            ahead = dots_of(starts[index + 1])
        exact = jnp.exp(scores)
        if causal:
            key_ids = start + lax.broadcasted_iota(jnp.int32, (key_tile, 2 * wide), 0)
            query_ids = lax.broadcasted_iota(jnp.int32, (key_tile, 2 * wide), 1)
            query_ids = jnp.where(query_ids >= wide, query_ids - wide, query_ids)
            exact = jnp.where(key_ids <= query_ids, exact, 0.0)
        grad_scores = (exact * centred).astype(BF16)
        ds_ref[start:stop, :] = grad_scores
        dv_ref[start:stop, :] = dot_nn(exact.astype(BF16), g_both[:, 0:LANES]).astype(BF16)
        dk_ref[start:stop, :] = dot_nn(grad_scores, q_both[:, 0:LANES]).astype(BF16)
    grad_q = dot_tn(k_ref[...], ds_ref[...]).T
    grad_q = jnp.where(first, grad_q[0:rows], grad_q[wide : wide + rows])
    if causal:
        dq_ref[...] = ((grad_q + before[...]) * 0.125).astype(BF16)
    else:
        dq_ref[...] = grad_q


def attend_back(queries, keys, values, key_const, aug, grad_out, out, begin, count, before=None):
    rows = queries.shape[0]
    far = keys.shape[0] - rows
    causal = before is not None
    span, block = (rows, far // rows) if causal else (far, 0)
    first = begin // LANES
    wide = padded(rows)
    pair = pl.BlockSpec((rows, LANES), lambda i: (0, first + i))
    keys_of = pl.BlockSpec((span, LANES), lambda i: (block, first + i))
    made = lambda height: pl.BlockSpec((height, LANES), lambda i: (0, i))
    return pl.pallas_call(
        functools.partial(attend_back_kernel, causal),
        grid=(count // LANES,),
        in_specs=[
            pair,
            keys_of,
            keys_of,
            pl.BlockSpec((span, LANES), lambda i: (block, 0)),
            pair,
            pair,
            pair,
        ]
        + [pair] * causal,
        out_specs=[made(rows), made(span), made(span)],
        out_shape=[
            jax.ShapeDtypeStruct((rows, count), BF16 if causal else F32),
            jax.ShapeDtypeStruct((span, count), BF16),
            jax.ShapeDtypeStruct((span, count), BF16),
        ],
        scratch_shapes=[
            pltpu.VMEM((2 * wide, 2 * LANES), BF16),
            pltpu.VMEM((2 * wide, 2 * LANES), BF16),
            pltpu.VMEM((span, 2 * wide), BF16),
        ],
        name="attend_back",
        compiler_params=pltpu.CompilerParams(vmem_limit_bytes=24 << 20),
        cost_estimate=LIGHT,
    )(queries, keys, values, key_const, aug, grad_out, out, *([before] if causal else []))


def chip_masks(dp):
    bits = dp.bit_length() - 2
    low = bits // 2
    along_x = [2 << i for i in range(low)]
    along_y = [2 << i for i in range(low, bits)]
    return along_x, along_y


def position(device, mask, dp):
    other = device ^ mask
    return (other & 1) * (dp // 2) + (other >> 1)


def own_slice(weight, by_rows, device, width):
    dp = lax.axis_size("dp")
    if by_rows:
        full = weight.shape[1]
        start = position(device, 0, dp) * (full // dp)
        piece = lax.dynamic_slice(weight, (start % width, start // width * width), (full // dp, width))
        return piece[None]
    rows = weight.shape[1] // dp
    return lax.dynamic_slice_in_dim(weight, position(device, 0, dp) * rows, rows, axis=1)


class Flow:
    def __init__(self, steps):
        self.steps = steps
        self.result = None
        self.over = False
        self.held = None
        self.move(None)

    def move(self, value):
        try:
            self.held = self.steps.send(value)
        except StopIteration as stop:
            self.result, self.over, self.held = stop.value, True, None


def ordered(flows, values):
    live = [flow for flow in flows if not flow.over]
    values, held = lax.optimization_barrier((values, [flow.held for flow in live]))
    for flow, item in zip(live, held):
        flow.move(item)
    return values


def begin(flows, *values):
    values = ordered(flows, values)
    return values if len(values) > 1 else values[0]


def meet(flows, *values):
    values = ordered(flows, values)
    return begin(flows, *values)


def layer_steps(value):
    mp = lax.axis_size("mp")
    got = {0: value}
    for count in range(1, mp.bit_length()):
        ranks = [r for r in range(mp) if r.bit_count() == count]
        sent = [got[r & (r - 1)] for r in ranks]
        if count > 1:
            sent = yield tuple(sent)
        found = yield tuple(swap(item, "mp", r & -r) for r, item in zip(ranks, sent))
        got.update(zip(ranks, found))
    return [got[r] for r in range(mp)]


def spread_steps(sides):
    along_x, along_y = chip_masks(lax.axis_size("dp"))
    orders = (along_x + along_y, along_y + along_x)
    masks = [[0], [0]]
    held = [side[None] for side in sides]
    arrays = []
    for step in range(len(along_x + along_y)):
        held = yield tuple(held)
        got = yield tuple(swap(value, "dp", order[step]) for value, order in zip(held, orders))
        for side, order in enumerate(orders):
            moved = [m ^ order[step] for m in masks[side]]
            if step + 1 < len(order):
                masks[side] = masks[side] + moved
            else:
                arrays += [(side, masks[side], held[side]), (side, moved, got[side])]
        held = [jnp.concatenate([one, two], axis=0) for one, two in zip(held, got)]
    own = yield tuple(value for _, _, value in arrays)
    other = yield tuple(swap(value, "dp", 1) for value in own)
    return [(side, m, value) for (side, m, _), value in zip(arrays, own)] + [
        (side, [k ^ 1 for k in m], value) for (side, m, _), value in zip(arrays, other)
    ]


def gather_flow(stacked, extra=None):
    count, rows, width = stacked.shape
    flat = stacked.reshape(count * rows, width)
    if extra is not None:
        flat = jnp.concatenate([flat, extra], axis=0)
    (flat,) = yield (flat,)
    found = yield from layer_steps(flat)
    across = jnp.stack([item[: count * rows].reshape(count, rows, width) for item in found[1:]])
    half = rows // 2
    arrays = yield from spread_steps((across[:, :, :half], across[:, :, half:]))
    return arrays, [item[count * rows :] for item in found]


class Weights:
    def __init__(self, own, arrays):
        self.own, self.arrays = own, arrays
        sample = arrays[0][2]
        self.full, self.width = sample.shape[3] * 2 * lax.axis_size("dp"), sample.shape[4]
        self.inputs = [shard for shard, _, _ in own] + [value for _, _, value in arrays]
        self.n_own = len(own)

    def specs(self):
        return [pl.BlockSpec(memory_space=pl.ANY)] * len(self.inputs)

    def scratch(self, mp, which):
        count = self.full // self.width + sum(len(m) for _, m, _ in self.arrays)
        return [
            pltpu.VMEM((mp, len(which), self.full, self.width), BF16),
            pltpu.SemaphoreType.DMA((count + 4,)),
        ]

    def copies(self, refs, held, sems, device, mp, dp, which):
        made = [[], []]
        spot = 0

        def add(r, source, target):
            nonlocal spot
            made[r].append((source, target, sems.at[spot]))
            spot += 1

        first, last = which[0], which[-1] + 1
        for ref, (_, index, by_rows) in zip(refs, self.own):
            if by_rows and first <= index < last:
                for block in range(self.full // self.width):
                    columns = pl.ds(block * self.width, self.width)
                    add(0, ref.at[:, columns], held.at[0, index - first, columns, :])
            elif not by_rows and first == index:
                add(0, ref, held.at[0, 0 : ref.shape[0]])
        half = self.full // dp // 2
        for ref, (side, masks, _) in zip(refs[self.n_own :], self.arrays):
            for index, mask in enumerate(masks):
                start = pl.multiple_of((position(device, mask, dp) * 2 + side) * half, half)
                add(
                    1,
                    ref.at[index, :, first:last],
                    held.at[1:, :, pl.ds(start, half), :],
                )
        return made


def start_all(copies):
    for copy in copies:
        pltpu.make_async_copy(*copy).start()


def wait_all(copies):
    for copy in copies:
        pltpu.make_async_copy(*copy).wait()


def wait_step(step, copies, begin=0):
    for r in range(begin, len(copies)):

        @pl.when(step == r)
        def _():
            wait_all(copies[r])


def tiles(count, size, body):
    if count == size:
        body(0)
    else:

        for i in range(count // size):
            body(i * size)


def row_tile(rows):
    return 272 if rows % 272 == 0 else 16


COLUMNS = 256


def column_tile(width):
    return min(COLUMNS, width)


def whole(shape):
    return pl.BlockSpec(shape, lambda i, *_: (0,) * len(shape))


def project_kernel(group, blocks, scale, scal, *refs):
    n_in = len(group.inputs)
    x_refs, bias_ref = refs[:blocks], refs[blocks]
    w_refs = refs[blocks + 1 : blocks + 1 + n_in]
    q_ref, k_ref, v_ref, held, sems = refs[blocks + 1 + n_in :]
    r = pl.program_id(0)
    mp, dp = lax.axis_size("mp"), lax.axis_size("dp")
    copies = group.copies(w_refs, held, sems, scal[0], mp, dp, [0, 1, 2])
    rows = q_ref.shape[0]

    @pl.when(r == 0)
    def _():
        start_all(sum(copies, []))

    wait_step(r, copies)

    size = column_tile(group.width)
    for begin in range(0, group.width, size):
        columns = slice(begin, begin + size)
        q = dot_nn(x_refs[-1][...], held[r, 0, :, columns]) + bias_ref[0:1, columns].astype(F32)
        q_ref[:, columns] = ((q * scale).astype(BF16) * RELAX_ALPHA).astype(BF16)
        for block in range(blocks):
            x = x_refs[block][...]
            place = slice(block * rows, (block + 1) * rows)
            k_ref[place, columns] = dot_nn(x, held[r, 1, :, columns]).astype(BF16)
            v = dot_nn(x, held[r, 2, :, columns]) + bias_ref[1:2, columns].astype(F32)
            v_ref[place, columns] = v.astype(BF16)


def project(normed, biases, group, device):
    mp = lax.axis_size("mp")
    rows, full = normed[0].shape
    blocks = len(normed)
    width = group.width
    made = lambda height: pl.BlockSpec((height, width), lambda i, *_: (0, i))
    return pl.pallas_call(
        functools.partial(project_kernel, group, blocks, 1.0 / math.sqrt(HEAD_DIM) / RELAX_ALPHA),
        grid_spec=pltpu.PrefetchScalarGridSpec(
            num_scalar_prefetch=1,
            grid=(mp,),
            in_specs=[whole((rows, full))] * blocks
            + [pl.BlockSpec((8, width), lambda i, *_: (0, i))]
            + group.specs(),
            out_specs=[made(rows), made(blocks * rows), made(blocks * rows)],
            scratch_shapes=group.scratch(mp, [0, 1, 2]),
        ),
        out_shape=[
            jax.ShapeDtypeStruct((rows, full), BF16),
            jax.ShapeDtypeStruct((blocks * rows, full), BF16),
            jax.ShapeDtypeStruct((blocks * rows, full), BF16),
        ],
        name="project",
        compiler_params=pltpu.CompilerParams(vmem_limit_bytes=28 << 20),
        cost_estimate=LIGHT,
    )(device.reshape(1), *normed, biases, *group.inputs)


def up_kernel(group_a, group_u, scal, *refs):
    (att_a, att_b, residual_ref, rows_ref, bias_ref), refs = refs[:5], refs[5:]
    wa, refs = refs[: len(group_a.inputs)], refs[len(group_a.inputs) :]
    wu, refs = refs[: len(group_u.inputs)], refs[len(group_u.inputs) :]
    branch_ref, middle_ref, mid_ref, act_ref, slope_ref, held_o, sem_o, held_u, sem_u = refs
    r = pl.program_id(0)
    mp, dp = lax.axis_size("mp"), lax.axis_size("dp")
    copies_o = sum(group_a.copies(wa, held_o, sem_o, scal[0], mp, dp, [3]), [])
    copies_u = group_u.copies(wu, held_u, sem_u, scal[0], mp, dp, [0])
    rows, full = middle_ref.shape
    width = group_a.width
    part = att_a.shape[1]

    @pl.when(r == 0)
    def _():
        start_all(copies_o)
        start_all(sum(copies_u, []))
        wait_all(copies_o)
        for block in range(full // width):
            columns = slice(block * width, (block + 1) * width)
            total = jnp.zeros((rows, width), F32)
            for layer in range(mp):
                source = att_a if layer * width < part else att_b
                first = layer * width % part
                total = total + dot_nn(source[:, first : first + width], held_o[layer, 0, columns, :])
            branch_ref[:, columns] = total + rows_ref[0:1, columns]

        def norm_rows(start):
            place = pl.ds(start, row_tile(rows))
            normal, _ = normalize(branch_ref[place, :])
            middle = residual_ref[place, :] + normal * rows_ref[1:2, :] + rows_ref[2:3, :]
            middle_ref[place, :] = middle
            normal, _ = normalize(middle)
            mid_ref[place, :] = (normal * rows_ref[3:4, :] + rows_ref[4:5, :]).astype(BF16)

        tiles(rows, row_tile(rows), norm_rows)

    wait_step(r, copies_u)

    size = column_tile(group_u.width)

    def activate(start):
        columns = pl.ds(start, size)
        u = dot_nn(mid_ref[...], held_u[r, 0, :, columns]) + bias_ref[0:1, columns]
        scale = math.sqrt(2.0 / math.pi)
        square = u * u
        bent = jnp.tanh(scale * u * (1.0 + 0.044715 * square))
        lifted = 0.5 + 0.5 * bent
        act_ref[:, columns] = (u * lifted).astype(BF16)
        slope = lifted + (0.5 * scale) * u * (1.0 - bent * bent) * (
            1.0 + (3.0 * 0.044715) * square
        )
        slope_ref[:, columns] = slope.astype(BF16)

    tiles(group_u.width, size, activate)


def feed_up(att_a, att_b, residual, vectors, u_bias, group_a, group_u, device):
    mp = lax.axis_size("mp")
    rows, full = residual.shape
    hidden = group_u.width
    made = pl.BlockSpec((rows, hidden), lambda i, *_: (0, i))
    return pl.pallas_call(
        functools.partial(up_kernel, group_a, group_u),
        grid_spec=pltpu.PrefetchScalarGridSpec(
            num_scalar_prefetch=1,
            grid=(mp,),
            in_specs=[whole(att_a.shape), whole(att_b.shape), whole((rows, full)), whole((8, full))]
            + [pl.BlockSpec((8, hidden), lambda i, *_: (0, i))]
            + group_a.specs()
            + group_u.specs(),
            out_specs=[whole((rows, full)), whole((rows, full)), whole((rows, full)), made, made],
            scratch_shapes=group_a.scratch(mp, [3]) + group_u.scratch(mp, [0]),
        ),
        out_shape=[
            jax.ShapeDtypeStruct((rows, full), F32),
            jax.ShapeDtypeStruct((rows, full), F32),
            jax.ShapeDtypeStruct((rows, full), BF16),
            jax.ShapeDtypeStruct((rows, mp * hidden), BF16),
            jax.ShapeDtypeStruct((rows, mp * hidden), BF16),
        ],
        name="feed_up",
        compiler_params=pltpu.CompilerParams(vmem_limit_bytes=44 << 20),
        cost_estimate=LIGHT,
    )(
        device.reshape(1), att_a, att_b, residual, vectors, u_bias, *group_a.inputs, *group_u.inputs
    )


def down_kernel(group_d, scal, *refs):
    (act_ref, middle_ref, cot_ref, rows_ref), refs = refs[:4], refs[4:]
    wd, refs = refs[: len(group_d.inputs)], refs[len(group_d.inputs) :]
    out_ref, grad_ref, sums_ref, held, sems, total = refs
    r = pl.program_id(0)
    mp, dp = lax.axis_size("mp"), lax.axis_size("dp")
    copies = group_d.copies(wd, held, sems, scal[0], mp, dp, [0])
    rows, full = middle_ref.shape
    width = group_d.width

    @pl.when(r == 0)
    def _():
        start_all(sum(copies, []))
        total[...] = jnp.zeros_like(total)

    wait_step(r, copies)

    size = column_tile(width)
    for block in range(full // width):

        def add(start):
            columns = pl.ds(block * width + start, size)
            total[:, columns] += dot_nn(
                act_ref[...], held[r, 0, block * width : (block + 1) * width, pl.ds(start, size)]
            )

        tiles(width, size, add)

    @pl.when(r == mp - 1)
    def _():
        sums_ref[...] = jnp.zeros_like(sums_ref)

        def norm_rows(start):
            place = pl.ds(start, row_tile(rows))
            normal, factor = normalize(total[place, :] + rows_ref[0:1, :])
            gain = rows_ref[1:2, :]
            out_ref[place, :] = (
                middle_ref[place, :] + (normal * gain + rows_ref[2:3, :])
            ).astype(BF16)
            upstream = cot_ref[place, :].astype(F32)
            scaled = upstream * gain
            grad = (
                scaled
                - jnp.mean(scaled, axis=-1, keepdims=True)
                - normal * jnp.mean(scaled * normal, axis=-1, keepdims=True)
            ) * factor
            grad = grad.astype(BF16)
            grad_ref[place, :] = grad
            sums_ref[0:8, :] += fold(upstream * normal)
            sums_ref[8:16, :] += fold(upstream)
            sums_ref[16:24, :] += fold(grad.astype(F32))

        tiles(rows, row_tile(rows), norm_rows)


def fold(value):
    return functools.reduce(jnp.add, [value[i : i + 8] for i in range(0, value.shape[0], 8)])


def feed_down(act, middle, cotangent, vectors, group_d, device):
    mp = lax.axis_size("mp")
    rows, full = middle.shape
    hidden = group_d.width
    return pl.pallas_call(
        functools.partial(down_kernel, group_d),
        grid_spec=pltpu.PrefetchScalarGridSpec(
            num_scalar_prefetch=1,
            grid=(mp,),
            in_specs=[pl.BlockSpec((rows, hidden), lambda i, *_: (0, i))]
            + [whole((rows, full)), whole((rows, full)), whole((8, full))]
            + group_d.specs(),
            out_specs=[whole((rows, full)), whole((rows, full)), whole((24, full))],
            scratch_shapes=group_d.scratch(mp, [0]) + [pltpu.VMEM((rows, full), F32)],
        ),
        out_shape=[
            jax.ShapeDtypeStruct((rows, full), BF16),
            jax.ShapeDtypeStruct((rows, full), BF16),
            jax.ShapeDtypeStruct((24, full), F32),
        ],
        name="feed_down",
        compiler_params=pltpu.CompilerParams(vmem_limit_bytes=30 << 20),
        cost_estimate=LIGHT,
    )(device.reshape(1), act, middle, cotangent, vectors, *group_d.inputs)


def back_kernel(group_a, group_u, group_d, scal, *refs):
    (grad_ref, slope_ref, branch_ref, middle_ref, cot_ref, rows_ref), refs = refs[:6], refs[6:]
    wa, refs = refs[: len(group_a.inputs)], refs[len(group_a.inputs) :]
    wu, refs = refs[: len(group_u.inputs)], refs[len(group_u.inputs) :]
    wd, refs = refs[: len(group_d.inputs)], refs[len(group_d.inputs) :]
    (pre_ref, mid_ref, low_ref, att_ref, sums_ref, u_sum_ref), refs = refs[:6], refs[6:]
    held_o, sem_o, held_u, sem_u, held_d, sem_d, total = refs
    r = pl.program_id(0)
    mp, dp = lax.axis_size("mp"), lax.axis_size("dp")
    copies_o = sum(group_a.copies(wa, held_o, sem_o, scal[0], mp, dp, [3]), [])
    copies_u = group_u.copies(wu, held_u, sem_u, scal[0], mp, dp, [0])
    copies_d = group_d.copies(wd, held_d, sem_d, scal[0], mp, dp, [0])
    copies = [one + two for one, two in zip(copies_d, copies_u)]
    rows, full = middle_ref.shape
    hidden = group_d.width
    size = column_tile(hidden)

    @pl.when(r == 0)
    def _():
        start_all(sum(copies, []) + copies_o)
        total[...] = jnp.zeros_like(total)

    wait_step(r, copies)

    def slopes(start):
        columns = pl.ds(start, size)
        grad = jnp.zeros((rows, size), F32)
        for block in range(full // hidden):
            grad = grad + dot_nt(
                grad_ref[:, block * hidden : (block + 1) * hidden],
                held_d[r, 0, pl.ds(block * hidden + start, size), :],
            )
        pre = (grad * slope_ref[:, columns].astype(F32)).astype(BF16)
        pre_ref[:, columns] = pre
        u_sum_ref[:, columns] = fold(pre.astype(F32))

    tiles(hidden, size, slopes)
    wide = column_tile(full)

    def add(start):
        columns = pl.ds(start, wide)
        total[:, columns] += dot_nt(pre_ref[...], held_u[r, 0, columns, :])

    tiles(full, wide, add)

    @pl.when(r == mp - 1)
    def _():
        sums_ref[...] = jnp.zeros_like(sums_ref)

        def norm_rows(start):
            place = pl.ds(start, row_tile(rows))

            def backward(upstream, inputs, gain):
                normal, factor = normalize(inputs)
                scaled = upstream * gain
                grad = (
                    scaled
                    - jnp.mean(scaled, axis=-1, keepdims=True)
                    - normal * jnp.mean(scaled * normal, axis=-1, keepdims=True)
                ) * factor
                return grad, fold(upstream * normal), fold(upstream)

            grad_mid, gain_sum, shift_sum = backward(
                total[place, :], middle_ref[place, :], rows_ref[0:1, :]
            )
            sums_ref[0:8, :] += gain_sum
            sums_ref[8:16, :] += shift_sum
            grad_middle = cot_ref[place, :].astype(F32) + grad_mid
            mid_ref[place, :] = grad_middle
            grad_branch, gain_sum, shift_sum = backward(
                grad_middle, branch_ref[place, :], rows_ref[1:2, :]
            )
            sums_ref[16:24, :] += gain_sum
            sums_ref[24:32, :] += shift_sum
            low = grad_branch.astype(BF16)
            low_ref[place, :] = low
            sums_ref[32:40, :] += fold(low.astype(F32))

        tiles(rows, row_tile(rows), norm_rows)
        wait_all(copies_o)
        width = group_a.width
        for layer in range(mp):
            grad = jnp.zeros((rows, width), F32)
            for block in range(full // width):
                columns = slice(block * width, (block + 1) * width)
                grad = grad + dot_nt(low_ref[:, columns], held_o[layer, 0, columns, :])
            att_ref[:, layer * width : (layer + 1) * width] = grad.astype(BF16)


def feed_back(grad, slope, branch, middle, cotangent, vectors, group_a, group_u, group_d, device):
    mp = lax.axis_size("mp")
    rows, full = middle.shape
    hidden = group_d.width
    step = pl.BlockSpec((rows, hidden), lambda i, *_: (0, i))
    return pl.pallas_call(
        functools.partial(back_kernel, group_a, group_u, group_d),
        grid_spec=pltpu.PrefetchScalarGridSpec(
            num_scalar_prefetch=1,
            grid=(mp,),
            in_specs=[whole((rows, full)), step]
            + [whole((rows, full))] * 3
            + [whole((8, full))]
            + group_a.specs()
            + group_u.specs()
            + group_d.specs(),
            out_specs=[step]
            + [whole((rows, full))] * 3
            + [whole((40, full)), pl.BlockSpec((8, hidden), lambda i, *_: (0, i))],
            scratch_shapes=group_a.scratch(mp, [3])
            + group_u.scratch(mp, [0])
            + group_d.scratch(mp, [0])
            + [pltpu.VMEM((rows, full), F32)],
        ),
        out_shape=[
            jax.ShapeDtypeStruct((rows, mp * hidden), BF16),
            jax.ShapeDtypeStruct((rows, full), F32),
            jax.ShapeDtypeStruct((rows, full), BF16),
            jax.ShapeDtypeStruct((rows, full), BF16),
            jax.ShapeDtypeStruct((40, full), F32),
            jax.ShapeDtypeStruct((8, mp * hidden), F32),
        ],
        name="feed_back",
        compiler_params=pltpu.CompilerParams(vmem_limit_bytes=52 << 20),
        cost_estimate=LIGHT,
    )(
        device.reshape(1),
        grad,
        slope,
        branch,
        middle,
        cotangent,
        vectors,
        *group_a.inputs,
        *group_u.inputs,
        *group_d.inputs,
    )


def unproject_kernel(group, which, begin, steps, added, scal, *refs):
    grads, refs = refs[: len(which)], refs[len(which) :]
    before, refs = (refs[0], refs[1:]) if added else (None, refs)
    w_refs, refs = refs[: len(group.inputs)], refs[len(group.inputs) :]
    out_ref, held, sems, total = refs
    step = pl.program_id(0)
    mp, dp = lax.axis_size("mp"), lax.axis_size("dp")
    copies = group.copies(w_refs, held, sems, scal[0], mp, dp, [0, 1, 2])
    if begin:
        copies = copies[1:]
    elif steps == 1:
        copies = copies[:1]
    full = out_ref.shape[1]

    @pl.when(step == 0)
    def _():
        start_all(sum(copies, []))
        total[...] = before[...] if added else jnp.zeros_like(total)

    wait_step(step, copies)
    r = begin + step
    size = column_tile(full)

    def add(start):
        columns = pl.ds(start, size)
        total[:, columns] += functools.reduce(
            jnp.add,
            [dot_nt(g[...], held[r, index, columns, :]) for index, g in zip(which, grads)],
        )

    tiles(full, size, add)

    @pl.when(step == pl.num_programs(0) - 1)
    def _():
        out_ref[...] = total[...].astype(out_ref.dtype)


def unproject(grads, which, group, begin, before, dtype, device):
    mp = lax.axis_size("mp")
    rows, count = grads[0].shape
    full, width = group.full, group.width
    return pl.pallas_call(
        functools.partial(
            unproject_kernel, group, which, begin, count // width, before is not None
        ),
        grid_spec=pltpu.PrefetchScalarGridSpec(
            num_scalar_prefetch=1,
            grid=(count // width,),
            in_specs=[pl.BlockSpec((rows, width), lambda i, *_: (0, i))] * len(grads)
            + ([] if before is None else [whole((rows, full))])
            + group.specs(),
            out_specs=whole((rows, full)),
            scratch_shapes=group.scratch(mp, [0, 1, 2]) + [pltpu.VMEM((rows, full), F32)],
        ),
        out_shape=jax.ShapeDtypeStruct((rows, full), dtype),
        name="unproject",
        compiler_params=pltpu.CompilerParams(vmem_limit_bytes=22 << 20),
        cost_estimate=LIGHT,
    )(device.reshape(1), *grads, *([] if before is None else [before]), *group.inputs)


def other_half_kernel(scal, left_ref, right_ref, out_ref):
    out_ref[...] = dot_tn(left_ref[...], right_ref[...]).astype(BF16)


def split_rows(total, bit_at, bit, outs):
    send_ref, keep_ref = outs
    count, rows, _ = send_ref.shape
    for j in range(count):
        base = ((j >> bit_at) << (bit_at + 1)) | (j & ((1 << bit_at) - 1))
        for ref, value in ((send_ref, 1 - bit), (keep_ref, bit)):
            start = pl.multiple_of((base + (value << bit_at)) * rows, rows)
            ref[j] = total[pl.ds(start, rows), :].astype(BF16)


def this_half_kernel(bits_at, scal, left_ref, right_ref, got_ref, *refs):
    outs, total = refs[:-1], refs[-1]
    total[...] = dot_tn(left_ref[...], right_ref[...]) + got_ref[...].astype(F32)
    step = pl.program_id(0)
    count = pl.num_programs(0) // 2
    for side in range(2):

        @pl.when(step // count == side)
        def _():
            split_rows(
                total,
                bits_at[side],
                (scal[0] >> (bits_at[side] + 1)) & 1,
                outs[2 * side : 2 * side + 2],
            )


def first_bits():
    along_x, along_y = chip_masks(lax.axis_size("dp"))
    return [order[0].bit_length() - 2 for order in (along_x + along_y, along_y + along_x)]


def other_half(left, right, device):
    rows, full = left.shape
    size = right.shape[1] // lax.axis_size("mp")
    return pl.pallas_call(
        other_half_kernel,
        grid_spec=pltpu.PrefetchScalarGridSpec(
            num_scalar_prefetch=1,
            grid=(right.shape[1] // size,),
            in_specs=[
                pl.BlockSpec((rows, full // 2), lambda i, scal: (0, 1 - scal[0] % 2)),
                pl.BlockSpec((rows, size), lambda i, scal: (0, i)),
            ],
            out_specs=pl.BlockSpec((full // 2, size), lambda i, scal: (0, i)),
        ),
        out_shape=jax.ShapeDtypeStruct((full // 2, right.shape[1]), BF16),
        name="other_half",
        compiler_params=pltpu.CompilerParams(vmem_limit_bytes=16 << 20),
        cost_estimate=LIGHT,
    )(device.reshape(1), left, right)


def this_half(left, right, got, device):
    rows, full = left.shape
    mp = lax.axis_size("mp")
    size = right.shape[1] // mp
    quarters = lax.axis_size("dp") // 2
    shape = (quarters // 2, full // 2 // quarters, mp // 2 * size)
    block = (quarters // 2, full // 2 // quarters, size)
    last = mp // 2 - 1
    sides = [lambda i, scal: (0, 0, jnp.minimum(i, last))] * 2 + [
        lambda i, scal: (0, 0, jnp.maximum(i - last - 1, 0))
    ] * 2
    return pl.pallas_call(
        functools.partial(this_half_kernel, first_bits()),
        grid_spec=pltpu.PrefetchScalarGridSpec(
            num_scalar_prefetch=1,
            grid=(mp,),
            in_specs=[
                pl.BlockSpec((rows, full // 2), lambda i, scal: (0, scal[0] % 2)),
                pl.BlockSpec((rows, size), lambda i, scal: (0, i)),
                pl.BlockSpec((full // 2, size), lambda i, scal: (0, i)),
            ],
            out_specs=[pl.BlockSpec(block, index) for index in sides],
            scratch_shapes=[pltpu.VMEM((full // 2, size), F32)],
        ),
        out_shape=[jax.ShapeDtypeStruct(shape, BF16)] * 4,
        name="this_half",
        compiler_params=pltpu.CompilerParams(vmem_limit_bytes=24 << 20),
        cost_estimate=LIGHT,
    )(device.reshape(1), left, right, got)


def attention_dots(width, lefts, branch, grads, attended, layer, put):
    grad_q, near_k, near_v, far_k, far_v = grads
    rows = grad_q.shape[0]
    columns = slice(layer * width, (layer + 1) * width)
    put(0, dot_tn(lefts[-1][...], grad_q[:, columns]))
    for index, near, far in ((1, near_k, far_k), (2, near_v, far_v)):
        total = dot_tn(lefts[-1][...], near[:, columns])
        for block in range(len(lefts) - 1):
            total = total + dot_tn(lefts[block][...], far[block * rows : (block + 1) * rows, columns])
        put(index, total)
    put(3, dot_tn(branch[...], attended[:, columns]))


def attention_other_kernel(width, blocks, scal, *refs):
    lefts, (branch, *grads, attended, out_ref) = refs[:blocks], refs[blocks:]
    for layer in range(attended.shape[1] // width):

        def put(index, value):
            place = (layer * 4 + index) * width
            out_ref[:, place : place + width] = value.astype(BF16)

        attention_dots(width, lefts, branch, grads, attended, layer, put)


def attention_this_kernel(width, blocks, bits_at, scal, *refs):
    lefts, (branch, *grads, attended, got_ref) = refs[:blocks], refs[blocks : blocks + 8]
    outs, total = refs[blocks + 8 : -1], refs[-1]
    layers = attended.shape[1] // width
    for side in range(2):
        for local in range(layers // 2):
            layer = side * (layers // 2) + local

            def put(index, value):
                place = (layer * 4 + index) * width
                total[:, index * width : (index + 1) * width] = value + got_ref[
                    :, place : place + width
                ].astype(F32)

            attention_dots(width, lefts, branch, grads, attended, layer, put)
            columns = pl.ds(local * 4 * width, 4 * width)
            split_rows(
                total,
                bits_at[side],
                (scal[0] >> (bits_at[side] + 1)) & 1,
                [ref.at[:, :, columns] for ref in outs[2 * side : 2 * side + 2]],
            )


def attention_specs(normed, branch, grads, part, core_of):
    rows, full = branch.shape
    left = pl.BlockSpec((rows, full // 2), lambda i, scal: (0, core_of(scal)))
    wide = grads[0].shape[1]
    some = lambda height: pl.BlockSpec((height, wide), lambda i, scal: (0, part))
    return (
        [left] * (len(normed) + 1)
        + [whole(g.shape) for g in grads[:3]]
        + [some(g.shape[0]) for g in grads[3:]]
        + [some(rows)]
    )


def attention_other(normed, branch, grads, attended, part, width, device):
    full = branch.shape[1]
    out = (full // 2, 4 * grads[0].shape[1])
    return pl.pallas_call(
        functools.partial(attention_other_kernel, width, len(normed)),
        grid_spec=pltpu.PrefetchScalarGridSpec(
            num_scalar_prefetch=1,
            grid=(1,),
            in_specs=attention_specs(normed, branch, grads, part, lambda s: 1 - s[0] % 2),
            out_specs=whole(out),
        ),
        out_shape=jax.ShapeDtypeStruct(out, BF16),
        name="attention_other",
        compiler_params=pltpu.CompilerParams(vmem_limit_bytes=16 << 20),
        cost_estimate=LIGHT,
    )(device.reshape(1), *normed, branch, *grads, attended)


def attention_this(normed, branch, grads, attended, got, part, width, device):
    full = branch.shape[1]
    quarters = lax.axis_size("dp") // 2
    shape = (quarters // 2, full // 2 // quarters, 2 * grads[0].shape[1])
    return pl.pallas_call(
        functools.partial(attention_this_kernel, width, len(normed), first_bits()),
        grid_spec=pltpu.PrefetchScalarGridSpec(
            num_scalar_prefetch=1,
            grid=(1,),
            in_specs=attention_specs(normed, branch, grads, part, lambda s: s[0] % 2)
            + [whole(got.shape)],
            out_specs=[whole(shape)] * 4,
            scratch_shapes=[pltpu.VMEM((full // 2, 4 * width), F32)],
        ),
        out_shape=[jax.ShapeDtypeStruct(shape, BF16)] * 4,
        name="attention_this",
        compiler_params=pltpu.CompilerParams(vmem_limit_bytes=24 << 20),
        cost_estimate=LIGHT,
    )(device.reshape(1), *normed, branch, *grads, attended, got)


def next_stage_kernel(scal, *refs):
    ins, outs = refs[:8], refs[8:]
    for index, out in enumerate(outs):
        one, two = ins[2 * index], ins[2 * index + 1]
        out[...] = (one[0].astype(F32) + two[0].astype(F32)).astype(BF16)


def next_stage(keeps, gots, bits, device):
    _, rows, columns = keeps[0].shape
    specs, inputs = [], []
    for side in range(2):
        for flip in (1, 0):
            where = lambda i, scal, side=side, flip=flip: (
                ((scal[0] >> (bits[side] + 1)) & 1) ^ flip,
                0,
                0,
            )
            specs += [pl.BlockSpec((1, rows, columns), where)] * 2
            inputs += [keeps[side], gots[side]]
    return pl.pallas_call(
        next_stage_kernel,
        grid_spec=pltpu.PrefetchScalarGridSpec(
            num_scalar_prefetch=1,
            grid=(1,),
            in_specs=specs,
            out_specs=[whole((rows, columns))] * 4,
        ),
        out_shape=[jax.ShapeDtypeStruct((rows, columns), BF16)] * 4,
        name="next_stage",
        compiler_params=pltpu.CompilerParams(vmem_limit_bytes=16 << 20),
        cost_estimate=LIGHT,
    )(device.reshape(1), *inputs)


def by_layer_kernel(places, keep_a, got_a, keep_b, got_b, send_ref, rest_ref):
    width = send_ref.shape[2]
    each = len(places) // 2
    for index, (sent, spot) in enumerate(places):
        keep, got = ((keep_a, got_a), (keep_b, got_b))[index // each]
        columns = slice(index % each * width, (index % each + 1) * width)
        value = keep[:, columns].astype(F32) + got[:, columns].astype(F32)
        if sent:
            send_ref[spot] = value.astype(BF16)
        else:
            rest_ref[spot] = value


def by_layer_pieces(keeps, gots, layers):
    rows = keeps[0].shape[0]
    width = keeps[0].shape[1] * 2 // len(layers)
    odd = [r for r in layers if r & 1]
    even = [r for r in layers if not r & 1]
    places = [(r & 1, (odd if r & 1 else even).index(r)) for r in layers]
    send, rest = pl.pallas_call(
        functools.partial(by_layer_kernel, places),
        out_shape=[
            jax.ShapeDtypeStruct((len(odd), rows, width), BF16),
            jax.ShapeDtypeStruct((len(even), rows, width), F32),
        ],
        in_specs=[pl.BlockSpec(memory_space=pltpu.VMEM)] * 4,
        out_specs=[pl.BlockSpec(memory_space=pltpu.VMEM)] * 2,
        name="by_layer_pieces",
        compiler_params=pltpu.CompilerParams(vmem_limit_bytes=12 << 20),
        cost_estimate=LIGHT,
    )(keeps[0], gots[0], keeps[1], gots[1])
    return send, rest, odd, even


def reduce_flow(send, add, layers, device):
    (send,) = yield (send,)
    (got,) = yield (swap(send, "dp", 1),)
    send_a, keep_a, send_b, keep_b = add(got)
    along_x, along_y = chip_masks(lax.axis_size("dp"))
    orders = (along_x + along_y, along_y + along_x)
    bits = len(orders[0])
    sends, keeps = [send_a, send_b], [keep_a, keep_b]
    lefts = []
    for side, order in enumerate(orders):
        left = list(range(bits - 1, -1, -1))
        left.remove(order[0].bit_length() - 2)
        lefts.append(left)
        keeps[side] = keeps[side].reshape((2,) * (bits - 1) + keeps[side].shape[1:])
    for step in range(bits):
        sends = yield tuple(sends)
        gots = yield tuple(swap(value, "dp", order[step]) for value, order in zip(sends, orders))
        gots = [got.reshape(keep.shape) for got, keep in zip(gots, keeps)]
        if step + 1 == bits:
            break
        picks = [order[step + 1].bit_length() - 2 for order in orders]
        if keeps[0].ndim == 3:
            send_a, keep_a, send_b, keep_b = next_stage(keeps, gots, picks, device)
            sends, keeps = [send_a, send_b], [keep_a, keep_b]
            continue
        sends, next_keeps = [], []
        for side, which in enumerate(picks):
            axis = lefts[side].index(which)
            lefts[side].remove(which)
            bit = (device >> (which + 1)) & 1

            def part(value):
                summed = [
                    lax.dynamic_index_in_dim(item, value, axis, keepdims=False).astype(F32)
                    for item in (keeps[side], gots[side])
                ]
                return (summed[0] + summed[1]).astype(BF16)

            sends.append(part(1 - bit))
            next_keeps.append(part(bit))
        keeps = next_keeps
    send, rest, odd, even = by_layer_pieces(keeps, gots, layers)
    (send,) = yield (send,)
    (got,) = yield (swap(send, "mp", 1),)
    held = {r: rest[i] for i, r in enumerate(even)}
    for i, r in enumerate(odd):
        value = got[i].astype(F32)
        held[r ^ 1] = held[r ^ 1] + value if r ^ 1 in held else value
    for bit in range(1, lax.axis_size("mp").bit_length() - 1):
        mask = 1 << bit
        away = [r for r in sorted(held) if r & mask]
        if away:
            send = held[away[0]] if len(away) == 1 else jnp.stack([held[r] for r in away])
            (send,) = yield (send.astype(BF16),)
            (got,) = yield (swap(send, "mp", mask),)
            got = [got] if len(away) == 1 else list(got)
            for r, value in zip(away, got):
                del held[r]
                value = value.astype(F32)
                held[r ^ mask] = held[r ^ mask] + value if r ^ mask in held else value
    return held[0]


def fill_kernel(plan, rows, dp, scal, *refs):
    ins, (qkv_ref, out_ref, turned) = refs[:-3], refs[-3:]
    width = turned.shape[1]
    for ref, (side, masks) in zip(ins, plan):
        for index, mask in enumerate(masks):
            place = pl.ds(pl.multiple_of(position(scal[0], mask, dp) * rows, rows), rows)
            for inner in range(2):
                value = ref[index, :, inner * width : (inner + 1) * width].astype(F32)
                if side * 2 + inner < 3:
                    qkv_ref[side * 2 + inner, place, :] = value
                else:
                    turned[place, :] = value
    out_ref[...] = turned[...].T


def fill_attention(arrays, full, width, device):
    dp = lax.axis_size("dp")
    inputs = [value for _, _, value in arrays]
    vmem = pl.BlockSpec(memory_space=pltpu.VMEM)
    return pl.pallas_call(
        functools.partial(fill_kernel, [(side, m) for side, m, _ in arrays], full // dp, dp),
        grid_spec=pltpu.PrefetchScalarGridSpec(
            num_scalar_prefetch=1,
            grid=(),
            in_specs=[vmem] * len(inputs),
            out_specs=[vmem, vmem],
            scratch_shapes=[pltpu.VMEM((full, width), F32)],
        ),
        out_shape=[
            jax.ShapeDtypeStruct((3, full, width), F32),
            jax.ShapeDtypeStruct((width, full), F32),
        ],
        name="fill_attention",
        compiler_params=pltpu.CompilerParams(vmem_limit_bytes=32 << 20),
        cost_estimate=LIGHT,
    )(device.reshape(1), *inputs)


def fill_ffn_kernel(turn, in_ref, out_ref):
    group, _, rows, hidden = in_ref.shape
    value = in_ref[...].astype(F32).reshape(group * rows, hidden)
    out_ref[...] = value.T if turn else value


def fill_ffn(gathered, turn):
    dp, rows, hidden = gathered.shape
    quarters = dp // 2
    group = quarters
    count = quarters // group
    full = dp * rows
    block = (hidden, group * rows) if turn else (group * rows, hidden)
    shape = (hidden, full) if turn else (full, hidden)
    where = (lambda c, j: (0, c * count + j)) if turn else (lambda c, j: (c * count + j, 0))
    return pl.pallas_call(
        functools.partial(fill_ffn_kernel, turn),
        grid=(2, count),
        in_specs=[pl.BlockSpec((group, 1, rows, hidden), lambda c, j: (j, c, 0, 0))],
        out_specs=pl.BlockSpec(block, where),
        out_shape=jax.ShapeDtypeStruct(shape, F32),
        name="fill_ffn",
        compiler_params=pltpu.CompilerParams(vmem_limit_bytes=24 << 20),
        cost_estimate=LIGHT,
    )(gathered.reshape(quarters, 2, rows, hidden))


def small_flow(value):
    for axis in ("dp", "mp"):
        for bit in range(lax.axis_size(axis).bit_length() - 1):
            (value,) = yield (value,)
            (got,) = yield (swap(value, axis, 1 << bit),)
            value = value + got
    return value


def spread_flow(sides):
    return (yield from spread_steps(sides))


def finish(flows, *values):
    while any(not flow.over for flow in flows):
        out = meet(flows, *values)
        values = out if len(values) > 1 else (out,)
    return values


def drain(*flows):
    for flow in flows:
        while not flow.over:
            flow.move(flow.held)


def eight_rows(*rows):
    stacked = jnp.stack([row.astype(F32) for row in rows])
    return jnp.pad(stacked, ((0, 8 - stacked.shape[0]), (0, 0)))


def on_device(
    tokens,
    groups,
    lengths,
    qkv_weight,
    qv_bias,
    out_weight,
    out_bias,
    up_weight,
    up_bias,
    down_weight,
    down_bias,
    norm_gain,
    norm_bias,
    group_table,
    cotangent,
):
    dp, mp = lax.axis_size("dp"), lax.axis_size("mp")
    device, layer = lax.axis_index("dp"), lax.axis_index("mp")
    core = device & 1
    rows, full = tokens.shape
    width = qkv_weight.shape[2]
    hidden = up_weight.shape[1]
    blocks = SEQ_LEN // rows
    place_in_seq = layer % blocks
    length = lax.dynamic_index_in_dim(lengths, layer // blocks, keepdims=False)
    along_x, along_y = chip_masks(dp)
    stages = len(along_x + along_y)
    gains = norm_gain.astype(F32)
    shifts = norm_bias.astype(F32)
    part, half = full // 2, full // 2

    shard_a = [(qkv_weight, 0, False), (out_weight, 3, True)]
    shard_u, shard_d = [(up_weight[None], 0, False)], [(down_weight, 0, True)]
    small_here = jnp.concatenate([qv_bias[0], qv_bias[1], up_bias]).reshape(-1, width)
    n_small = small_here.shape[0]
    small_here = jnp.pad(small_here, ((0, -n_small % 16), (0, 0)))
    slice_a = jnp.concatenate(
        [
            own_slice(qkv_weight, False, device, width),
            own_slice(out_weight, True, device, width),
        ]
    )
    flow_a = Flow(gather_flow(slice_a, small_here))
    tokens = begin([flow_a], tokens)

    order_of = layer ^ jnp.arange(mp)
    onehot = (
        groups[:, None] == lax.broadcasted_iota(jnp.int32, (1, group_table.shape[0]), 1)
    ).astype(BF16)
    residual = tokens.astype(F32) + jnp.dot(onehot, group_table, preferred_element_type=F32)
    normed, norm_one, inv_one = norm_forward(residual, gains[0], shifts[0])
    normed_low = normed.astype(BF16)

    def rows_flow(value):
        (value,) = yield (value,)
        return (yield tuple(swap(value, "mp", m) for m in range(1, blocks)))

    key_ids = lax.broadcasted_iota(jnp.int32, (blocks, rows, 1), 1)
    block_ids = lax.broadcasted_iota(jnp.int32, (blocks, rows, 1), 0)
    block_ids = place_in_seq ^ ((block_ids + 1) % blocks)
    shown = (block_ids <= place_in_seq) & (block_ids * rows + key_ids < length)
    spot = lax.broadcasted_iota(jnp.int32, (blocks, rows, LANES), 2) % HEAD_DIM
    key_const = jnp.where(
        spot == 0,
        jnp.where(shown, 0.0, MASKED_SCORE),
        jnp.where(spot <= 3, 1.0, 0.0),
    )
    key_const = key_const.astype(BF16).reshape(blocks * rows, LANES)

    slice_u = own_slice(up_weight[None], False, device, hidden)
    slice_d = own_slice(down_weight, True, device, hidden)
    flow_r = Flow(rows_flow(normed_low))
    normed_low, slice_u, slice_d = meet([flow_a], normed_low, slice_u, slice_d)
    flow_u, flow_d = Flow(gather_flow(slice_u)), Flow(gather_flow(slice_d))
    layer_stages = mp.bit_length() - 1
    for _ in range(layer_stages - 1):
        normed_low = meet([flow_a], normed_low)
    normed_low = begin([flow_r, flow_u], normed_low)
    for _ in range(stages - 1):
        normed_low = meet([flow_a], normed_low)
    normed_low = meet([flow_a, flow_u, flow_r], normed_low)
    for _ in range(layer_stages - 2):
        normed_low = meet([flow_u], normed_low)
    normed_low = meet([flow_a, flow_u], normed_low)
    normed_low = begin([flow_d], normed_low)
    arrays_a, small_all = flow_a.result
    group_a = Weights(shard_a, arrays_a)
    small_all = jnp.stack(small_all)[:, :n_small].reshape(mp, -1).astype(F32)
    qv_rows = small_all[:, : 2 * width].reshape(mp, 2, width).transpose(1, 0, 2).reshape(2, full)
    u_rows = small_all[:, 2 * width :].reshape(1, -1)
    qv_rows = jnp.pad(qv_rows, ((0, 6), (0, 0)))
    u_rows = jnp.pad(u_rows, ((0, 7), (0, 0)))
    seq_normed = tuple(flow_r.result) + (normed_low,)
    queries, keys, values = project(seq_normed, qv_rows, group_a, device)
    queries, keys, values = meet([flow_d, flow_u], queries, keys, values)
    attended_a, aug_a = attend(queries, keys, values, key_const, 0, part)
    for _ in range(layer_stages - 1):
        attended_a, queries = meet([flow_d], attended_a, queries)
    attended_b, aug_b = attend(queries, keys, values, key_const, part, part)
    attended = jnp.concatenate([attended_a, attended_b], axis=1)
    aug = jnp.concatenate([aug_a, aug_b], axis=1)
    attended_b = meet([flow_u, flow_d], attended_b)
    for _ in range(stages - 2):
        attended_b = meet([flow_d], attended_b)
    (attended_b,) = finish([flow_u], attended_b)
    group_u = Weights(shard_u, flow_u.result[0])
    branch, middle, mid_low, act, slope = feed_up(
        attended_a,
        attended_b,
        residual,
        eight_rows(out_bias, gains[1], shifts[1], gains[2], shifts[2]),
        u_rows,
        group_a,
        group_u,
        device,
    )
    (act,) = finish([flow_d], act)
    group_d = Weights(shard_d, flow_d.result[0])
    output, grad_ffn, sums_ffn = feed_down(
        act, middle, cotangent, eight_rows(down_bias, gains[3], shifts[3]), group_d, device
    )

    everyone = list(range(mp))

    def weight_flow(left, right):
        return Flow(
            reduce_flow(
                other_half(left, right, device),
                lambda got: this_half(left, right, got, device),
                everyone,
                device,
            )
        )

    flow_d = weight_flow(grad_ffn, act)
    grad_ffn = begin([flow_d], grad_ffn)
    grad_ffn = meet([flow_d], grad_ffn)
    grad_pre, grad_middle, grad_branch, grad_attended, sums_back, sums_up = feed_back(
        grad_ffn,
        slope,
        branch,
        middle,
        cotangent,
        eight_rows(gains[2], gains[1]),
        group_a,
        group_u,
        group_d,
        device,
    )
    grad_pre, grad_branch, grad_attended = meet([flow_d], grad_pre, grad_branch, grad_attended)
    flow_u = weight_flow(mid_low, grad_pre)
    grad_branch, grad_attended = begin([flow_u], grad_branch, grad_attended)

    def attention_flow(grads, layers):
        index = layers[0] * width // part
        return Flow(
            reduce_flow(
                attention_other(seq_normed, grad_branch, grads, attended, index, width, device),
                lambda got: attention_this(
                    seq_normed, grad_branch, grads, attended, got, index, width, device
                ),
                layers,
                device,
            )
        )

    layers_b, layers_a = everyone[: mp // 2], everyone[mp // 2 :]
    back = functools.partial(
        attend_back, queries, keys, values, key_const, aug, grad_attended, attended
    )
    far_q, far_k, far_v = back(0, full)
    far_grad = unproject((far_k, far_v), (1, 2), group_a, 0, None, BF16, device)
    far_grad, far_q, far_k, far_v = ordered([flow_d, flow_u], (far_grad, far_q, far_k, far_v))
    flow_f = Flow(rows_back(far_grad, rows, blocks))
    far_q, far_k, far_v = begin([flow_f, flow_u], far_q, far_k, far_v)
    grads_a = back(part, part, far_q)
    flow_qa = attention_flow((*grads_a, far_k, far_v), layers_a)
    far_q, *grads_a = meet([flow_u, flow_f], far_q, *grads_a)
    far_q, *grads_a = begin([flow_qa], far_q, *grads_a)
    near_a = unproject(grads_a, (0, 1, 2), group_a, mp // 2, None, F32, device)
    far_q, near_a = meet([flow_qa], far_q, near_a)
    far_q, near_a = begin([flow_d], far_q, near_a)
    grads_b = back(0, part, far_q)
    grads_b = ordered([flow_u, flow_qa, flow_d], grads_b)
    flow_qb = attention_flow((*grads_b, far_k, far_v), layers_b)
    grads_b = begin([flow_qb], *grads_b)
    grads_b = begin([flow_u, flow_qa, flow_d], *grads_b)
    near_b = unproject(grads_b, (0, 1, 2), group_a, 0, near_a, F32, device)
    near_b, *grads_a, sums_ffn, sums_back, sums_up = meet(
        [flow_qb, flow_qa, flow_u, flow_d], near_b, *grads_a, sums_ffn, sums_back, sums_up
    )
    drain(flow_d)
    down_mine = flow_d.result.astype(BF16)
    down_all = lax.all_gather(down_mine, "dp", axis=0)
    grad_normed = near_b
    for value in flow_f.result:
        grad_normed = grad_normed + value.astype(F32)
    back_one, gain_one, shift_one = norm_backward(grad_normed, norm_one, inv_one, gains[0])
    input_grad = grad_middle + back_one
    table_part = jnp.dot(
        onehot.astype(F32).T, input_grad, precision=PRECISE, preferred_element_type=F32
    )
    grad_q_sum = jnp.concatenate([jnp.sum(g[0].astype(F32), axis=0) for g in (grads_b, grads_a)])
    grad_v_sum = jnp.concatenate([jnp.sum(g[2].astype(F32), axis=0) for g in (grads_b, grads_a)])
    grad_v_sum = grad_v_sum + jnp.sum(far_v.astype(F32), axis=0)
    ffn_sums = jnp.sum(sums_ffn.reshape(3, 8, full), axis=1)
    back_sums = jnp.sum(sums_back.reshape(5, 8, full), axis=1)
    up_bias_part = jnp.sum(sums_up, axis=0)
    by_layer = jnp.concatenate(
        [grad_q_sum.reshape(mp, -1), grad_v_sum.reshape(mp, -1), up_bias_part.reshape(mp, -1)],
        axis=1,
    )
    by_layer = jnp.take(by_layer, order_of, axis=0)
    wide = by_layer.shape[1]
    by_layer = jnp.pad(by_layer, ((0, 0), (0, -wide % full))).reshape(-1, full)
    input_grad, table_part, gain_one, shift_one = meet(
        [flow_qb, flow_qa, flow_u], input_grad, table_part, gain_one, shift_one
    )
    drain(flow_u)
    up_mine = flow_u.result.astype(BF16)
    up_all = lax.all_gather(up_mine, "dp", axis=0)
    parts = jnp.concatenate(
        [
            jnp.stack([gain_one, back_sums[2], back_sums[0], ffn_sums[0]]),
            jnp.stack([shift_one, back_sums[3], back_sums[1], ffn_sums[1]]),
            jnp.stack([back_sums[4], ffn_sums[2]]),
            table_part,
            by_layer,
        ]
    )
    flow_s = Flow(small_flow(parts))
    drain(flow_qa, flow_qb)
    mine = (flow_qa.result + flow_qb.result).astype(BF16)
    flow_o = Flow(spread_flow((mine[:, : 2 * width], mine[:, 2 * width :])))
    for _ in range(2 * stages):
        flow_o.move(flow_o.held)
    down_grad = fill_ffn(down_all, True)
    up_grad = fill_ffn(up_all, False)
    down_grad, up_grad = begin([flow_o], down_grad, up_grad)
    drain(flow_o, flow_s)
    qkv_grad, out_grad = fill_attention(flow_o.result, full, width, device)

    parts = flow_s.result
    gain_grad, shift_grad = parts[:4], parts[4:8]
    out_bias_grad, down_bias_grad = parts[8], parts[9]
    n_groups = group_table.shape[0]
    table_grad = parts[10 : 10 + n_groups]
    by_layer = parts[10 + n_groups :].reshape(mp, -1)
    mine = lax.dynamic_index_in_dim(by_layer, layer, keepdims=False)
    qv_bias_grad = mine[: 2 * width].reshape(2, width)
    up_bias_grad = mine[2 * width : 2 * width + hidden]
    return (
        output,
        input_grad,
        qkv_grad,
        qv_bias_grad,
        out_grad,
        out_bias_grad,
        up_grad,
        up_bias_grad,
        down_grad,
        down_bias_grad,
        gain_grad,
        shift_grad,
        table_grad,
    )


def rows_back(value, rows, blocks):
    (value,) = yield (value,)
    return (
        yield tuple(swap(value[(m - 1) * rows : m * rows], "mp", m) for m in range(1, blocks))
    )


def solution(mesh):
    placed = (
        P(("dp", "mp"), None),
        P(("dp", "mp")),
        P("dp"),
        P(None, None, "mp"),
        P(None, "mp"),
        P("mp", None),
        P(),
        P(None, "mp"),
        P("mp"),
        P("mp", None),
        P(),
        P(),
        P(),
        P(),
        P(("dp", "mp"), None),
    )
    return jax.shard_map(
        on_device,
        mesh=mesh,
        in_specs=placed,
        out_specs=(
            P(("dp", "mp"), None),
            P(("dp", "mp"), None),
            P(None, None, "mp"),
            P(None, "mp"),
            P("mp", None),
            P(),
            P(None, "mp"),
            P("mp"),
            P("mp", None),
            P(),
            P(),
            P(),
            P(),
        ),
        check_vma=False,
    )
```

```python
import functools
import math

import jax
import jax.numpy as jnp
from jax import lax
from jax.experimental import pallas as pl
from jax.experimental.pallas import tpu as pltpu
from jax.sharding import PartitionSpec as P

HEAD_DIM = 64
SEQ_LEN = 1088
RELAX_ALPHA = 32.0
NORM_EPSILON = 1e-05
MASKED_SCORE = -1000000000.0
PRECISE = lax.Precision.HIGHEST
BF16 = jnp.bfloat16
F32 = jnp.float32
LANES = 128
LIGHT = pl.CostEstimate(flops=1000, bytes_accessed=1000, transcendentals=0)


def swap(value, axis, mask):
    count = lax.axis_size(axis)
    return lax.ppermute(value, axis, [(i, i ^ mask) for i in range(count)])


def normalize(inputs):
    centred = inputs - jnp.mean(inputs, axis=-1, keepdims=True)
    factor = lax.rsqrt(jnp.mean(centred * centred, axis=-1, keepdims=True) + NORM_EPSILON)
    return centred * factor, factor


def norm_forward(inputs, gain_row, shift_row):
    centred = inputs - jnp.mean(inputs, axis=-1, keepdims=True)
    factor = lax.rsqrt(jnp.mean(centred * centred, axis=-1, keepdims=True) + NORM_EPSILON)
    normal = centred * factor
    return (normal * gain_row + shift_row, normal, factor)


def norm_backward(upstream, normal, factor, gain_row):
    scaled = upstream * gain_row
    adjusted = (
        scaled
        - jnp.mean(scaled, axis=-1, keepdims=True)
        - normal * jnp.mean(scaled * normal, axis=-1, keepdims=True)
    )
    return (adjusted * factor, jnp.sum(upstream * normal, axis=0), jnp.sum(upstream, axis=0))


def dot_nn(a, b):
    return lax.dot_general(a, b, (((1,), (0,)), ((), ())), preferred_element_type=F32)


def dot_nt(a, b):
    return lax.dot_general(a, b, (((1,), (1,)), ((), ())), preferred_element_type=F32)


def dot_tn(a, b):
    return lax.dot_general(a, b, (((0,), (0,)), ((), ())), preferred_element_type=F32)


def query_tile(rows):
    return rows // 2 if (rows // 2) % 16 == 0 else rows


def padded(rows):
    return -(-rows // LANES) * LANES


def three_parts(value):
    high = value.astype(BF16)
    rest = value - high.astype(F32)
    mid = rest.astype(BF16)
    return high, mid, (rest - mid.astype(F32)).astype(BF16)


def attend_kernel(blocks, rows, q_ref, k_ref, v_ref, kc_ref, out_ref, aug_ref):
    tile = query_tile(rows)
    far = (blocks - 1) * rows
    lane = lax.broadcasted_iota(jnp.int32, (1, LANES), 1)
    first = lane < HEAD_DIM
    mine = [first, jnp.logical_not(first)]
    keys = jnp.concatenate([k_ref[...], kc_ref[...]], axis=1)
    special = jnp.where(lane == 0, 1.0, 0.0).astype(BF16)
    special = jnp.broadcast_to(special, (tile, LANES))
    starts = list(range(0, rows, tile))

    def scores_of(start):
        q = q_ref[start : start + tile, :]
        zero = jnp.zeros_like(q)
        both = jnp.concatenate(
            [jnp.concatenate([jnp.where(m, q, zero), special], axis=1) for m in mine], axis=0
        )
        return dot_nt(both, keys[: far + start + tile])

    scores = [scores_of(start) for start in starts]
    for start, score in zip(starts, scores):
        limit = far + start + tile
        cut = (far + start) // LANES * LANES
        row_ids = lax.broadcasted_iota(jnp.int32, (2 * tile, limit - cut), 0)
        row_ids = start + far - cut + jnp.where(row_ids >= tile, row_ids - tile, row_ids)
        columns = lax.broadcasted_iota(jnp.int32, (2 * tile, limit - cut), 1)
        last = jnp.where(columns <= row_ids, score[:, cut:], MASKED_SCORE)
        score = jnp.concatenate([score[:, :cut], last], axis=1) if cut else last
        top = jnp.max(score, axis=-1, keepdims=True)
        exponent = jnp.exp(score - top)
        total = jnp.sum(exponent, axis=-1, keepdims=True)
        gathered = dot_nn(exponent.astype(BF16), v_ref[0:limit, :]) / total
        out_ref[start : start + tile, :] = jnp.where(
            first, gathered[:tile], gathered[tile:]
        ).astype(BF16)
        parts = three_parts(-(top + jnp.log(total)))
        spot = lane % HEAD_DIM
        augs = []
        for head in range(2):
            aug = jnp.where(spot == 0, 1.0, jnp.zeros((tile, LANES), F32)).astype(BF16)
            for index, value in enumerate(parts):
                aug = jnp.where(spot == index + 1, value[head * tile : (head + 1) * tile], aug)
            augs.append(aug)
        aug_ref[start : start + tile, :] = jnp.where(first, augs[0], augs[1])


def attend(queries, keys, values, key_const, begin, count):
    rows = queries.shape[0]
    span = keys.shape[0]
    first = begin // LANES
    pair = lambda height: pl.BlockSpec((height, LANES), lambda i: (0, first + i))
    made = lambda height: pl.BlockSpec((height, LANES), lambda i: (0, i))
    return pl.pallas_call(
        functools.partial(attend_kernel, span // rows, rows),
        grid=(count // LANES,),
        in_specs=[
            pair(rows),
            pair(span),
            pair(span),
            pl.BlockSpec((span, LANES), lambda i: (0, 0)),
        ],
        out_specs=[made(rows), made(rows)],
        out_shape=[
            jax.ShapeDtypeStruct((rows, count), BF16),
            jax.ShapeDtypeStruct((rows, count), BF16),
        ],
        name="attend",
        compiler_params=pltpu.CompilerParams(vmem_limit_bytes=16 << 20),
        cost_estimate=LIGHT,
    )(queries, keys, values, key_const)


def attend_back_kernel(
    causal, q_ref, k_ref, v_ref, kc_ref, aug_ref, go_ref, out_ref, *refs
):
    before, refs = (refs[0], refs[1:]) if causal else (None, refs)
    dq_ref, dk_ref, dv_ref, q_both, g_both, ds_ref = refs
    rows = q_ref.shape[0]
    span = k_ref.shape[0]
    key_tile = query_tile(rows)
    wide = padded(rows)
    lane = lax.broadcasted_iota(jnp.int32, (1, LANES), 1)
    first = lane < HEAD_DIM
    mine = [first, jnp.logical_not(first)]
    q_pair, aug, go = q_ref[...], aug_ref[...], go_ref[...]
    zero = jnp.zeros_like(q_pair)
    weighed = go.astype(F32) * out_ref[...].astype(F32)
    pad = jnp.zeros((wide - rows, 2 * LANES), BF16)
    for head in range(2):
        m = mine[head]
        place = head * wide
        q_both[place : place + rows, 0:LANES] = jnp.where(m, q_pair, zero)
        q_both[place : place + rows, LANES:] = jnp.where(m, aug, zero)
        parts = three_parts(-jnp.sum(jnp.where(m, weighed, 0.0), axis=-1, keepdims=True))
        g_aug = zero
        for index, value in enumerate(parts):
            g_aug = jnp.where(lane == index + 1, value, g_aug)
        g_both[place : place + rows, 0:LANES] = jnp.where(m, go, zero)
        g_both[place : place + rows, LANES:] = g_aug
        if wide > rows:
            q_both[place + rows : place + wide, :] = pad
            g_both[place + rows : place + wide, :] = pad
    keys = jnp.concatenate([k_ref[...], kc_ref[...]], axis=1)
    v_const = jnp.where((lane >= 1) & (lane <= 3), 1.0, 0.0).astype(BF16)
    values = jnp.concatenate([v_ref[...], jnp.broadcast_to(v_const, k_ref.shape)], axis=1)

    def dots_of(start):
        stop = start + key_tile
        return dot_nt(keys[start:stop], q_both[...]), dot_nt(values[start:stop], g_both[...])

    starts = list(range(0, span, key_tile))
    ahead = dots_of(starts[0])
    for index, start in enumerate(starts):
        stop = start + key_tile
        scores, centred = ahead
        if index + 1 < len(starts):
            ahead = dots_of(starts[index + 1])
        exact = jnp.exp(scores)
        if causal:
            key_ids = start + lax.broadcasted_iota(jnp.int32, (key_tile, 2 * wide), 0)
            query_ids = lax.broadcasted_iota(jnp.int32, (key_tile, 2 * wide), 1)
            query_ids = jnp.where(query_ids >= wide, query_ids - wide, query_ids)
            exact = jnp.where(key_ids <= query_ids, exact, 0.0)
        grad_scores = (exact * centred).astype(BF16)
        ds_ref[start:stop, :] = grad_scores
        dv_ref[start:stop, :] = dot_nn(exact.astype(BF16), g_both[:, 0:LANES]).astype(BF16)
        dk_ref[start:stop, :] = dot_nn(grad_scores, q_both[:, 0:LANES]).astype(BF16)
    grad_q = dot_tn(k_ref[...], ds_ref[...]).T
    grad_q = jnp.where(first, grad_q[0:rows], grad_q[wide : wide + rows])
    if causal:
        dq_ref[...] = ((grad_q + before[...]) * 0.125).astype(BF16)
    else:
        dq_ref[...] = grad_q


def attend_back(queries, keys, values, key_const, aug, grad_out, out, begin, count, before=None):
    rows = queries.shape[0]
    far = keys.shape[0] - rows
    causal = before is not None
    span, block = (rows, far // rows) if causal else (far, 0)
    first = begin // LANES
    wide = padded(rows)
    pair = pl.BlockSpec((rows, LANES), lambda i: (0, first + i))
    keys_of = pl.BlockSpec((span, LANES), lambda i: (block, first + i))
    made = lambda height: pl.BlockSpec((height, LANES), lambda i: (0, i))
    return pl.pallas_call(
        functools.partial(attend_back_kernel, causal),
        grid=(count // LANES,),
        in_specs=[
            pair,
            keys_of,
            keys_of,
            pl.BlockSpec((span, LANES), lambda i: (block, 0)),
            pair,
            pair,
            pair,
        ]
        + [pair] * causal,
        out_specs=[made(rows), made(span), made(span)],
        out_shape=[
            jax.ShapeDtypeStruct((rows, count), BF16 if causal else F32),
            jax.ShapeDtypeStruct((span, count), BF16),
            jax.ShapeDtypeStruct((span, count), BF16),
        ],
        scratch_shapes=[
            pltpu.VMEM((2 * wide, 2 * LANES), BF16),
            pltpu.VMEM((2 * wide, 2 * LANES), BF16),
            pltpu.VMEM((span, 2 * wide), BF16),
        ],
        name="attend_back",
        compiler_params=pltpu.CompilerParams(vmem_limit_bytes=16 << 20),
        cost_estimate=LIGHT,
    )(queries, keys, values, key_const, aug, grad_out, out, *([before] if causal else []))


def chip_masks(dp):
    bits = dp.bit_length() - 2
    low = bits // 2
    along_x = [2 << i for i in range(low)]
    along_y = [2 << i for i in range(low, bits)]
    return along_x, along_y


def position(device, mask, dp):
    other = device ^ mask
    return (other & 1) * (dp // 2) + (other >> 1)


def own_slice(weight, by_rows, device, width):
    dp = lax.axis_size("dp")
    if by_rows:
        full = weight.shape[1]
        start = position(device, 0, dp) * (full // dp)
        piece = lax.dynamic_slice(weight, (start % width, start // width * width), (full // dp, width))
        return piece[None]
    rows = weight.shape[1] // dp
    return lax.dynamic_slice_in_dim(weight, position(device, 0, dp) * rows, rows, axis=1)


class Flow:
    def __init__(self, steps):
        self.steps = steps
        self.result = None
        self.over = False
        self.held = None
        self.move(None)

    def move(self, value):
        try:
            self.held = self.steps.send(value)
        except StopIteration as stop:
            self.result, self.over, self.held = stop.value, True, None


def ordered(flows, values):
    live = [flow for flow in flows if not flow.over]
    values, held = lax.optimization_barrier((values, [flow.held for flow in live]))
    for flow, item in zip(live, held):
        flow.move(item)
    return values


def begin(flows, *values):
    values = ordered(flows, values)
    return values if len(values) > 1 else values[0]


def meet(flows, *values):
    values = ordered(flows, values)
    return begin(flows, *values)


def layer_steps(value):
    mp = lax.axis_size("mp")
    got = {0: value}
    for count in range(1, mp.bit_length()):
        ranks = [r for r in range(mp) if r.bit_count() == count]
        sent = [got[r & (r - 1)] for r in ranks]
        if count > 1:
            sent = yield tuple(sent)
        found = yield tuple(swap(item, "mp", r & -r) for r, item in zip(ranks, sent))
        got.update(zip(ranks, found))
    return [got[r] for r in range(mp)]


def spread_steps(sides):
    along_x, along_y = chip_masks(lax.axis_size("dp"))
    orders = (along_x + along_y, along_y + along_x)
    masks = [[0], [0]]
    held = [side[None] for side in sides]
    arrays = []
    for step in range(len(along_x + along_y)):
        held = yield tuple(held)
        got = yield tuple(swap(value, "dp", order[step]) for value, order in zip(held, orders))
        for side, order in enumerate(orders):
            moved = [m ^ order[step] for m in masks[side]]
            if step + 1 < len(order):
                masks[side] = masks[side] + moved
            else:
                arrays += [(side, masks[side], held[side]), (side, moved, got[side])]
        held = [jnp.concatenate([one, two], axis=0) for one, two in zip(held, got)]
    own = yield tuple(value for _, _, value in arrays)
    other = yield tuple(swap(value, "dp", 1) for value in own)
    return [(side, m, value) for (side, m, _), value in zip(arrays, own)] + [
        (side, [k ^ 1 for k in m], value) for (side, m, _), value in zip(arrays, other)
    ]


def gather_flow(stacked, extra=None):
    count, rows, width = stacked.shape
    flat = stacked.reshape(count * rows, width)
    if extra is not None:
        flat = jnp.concatenate([flat, extra], axis=0)
    (flat,) = yield (flat,)
    found = yield from layer_steps(flat)
    across = jnp.stack([item[: count * rows].reshape(count, rows, width) for item in found[1:]])
    half = rows // 2
    arrays = yield from spread_steps((across[:, :, :half], across[:, :, half:]))
    return arrays, [item[count * rows :] for item in found]


class Weights:
    def __init__(self, own, arrays):
        self.own, self.arrays = own, arrays
        sample = arrays[0][2]
        self.full, self.width = sample.shape[3] * 2 * lax.axis_size("dp"), sample.shape[4]
        self.inputs = [shard for shard, _, _ in own] + [value for _, _, value in arrays]
        self.n_own = len(own)

    def specs(self):
        return [pl.BlockSpec(memory_space=pl.ANY)] * len(self.inputs)

    def scratch(self, mp, which):
        count = self.full // self.width + sum(len(m) for _, m, _ in self.arrays)
        return [
            pltpu.VMEM((mp, len(which), self.full, self.width), BF16),
            pltpu.SemaphoreType.DMA((count + 4,)),
        ]

    def copies(self, refs, held, sems, device, mp, dp, which):
        made = [[], []]
        spot = 0

        def add(r, source, target):
            nonlocal spot
            made[r].append((source, target, sems.at[spot]))
            spot += 1

        first, last = which[0], which[-1] + 1
        for ref, (_, index, by_rows) in zip(refs, self.own):
            if by_rows and first <= index < last:
                for block in range(self.full // self.width):
                    columns = pl.ds(block * self.width, self.width)
                    add(0, ref.at[:, columns], held.at[0, index - first, columns, :])
            elif not by_rows and first == index:
                add(0, ref, held.at[0, 0 : ref.shape[0]])
        half = self.full // dp // 2
        for ref, (side, masks, _) in zip(refs[self.n_own :], self.arrays):
            for index, mask in enumerate(masks):
                start = pl.multiple_of((position(device, mask, dp) * 2 + side) * half, half)
                add(
                    1,
                    ref.at[index, :, first:last],
                    held.at[1:, :, pl.ds(start, half), :],
                )
        return made


def start_all(copies):
    for copy in copies:
        pltpu.make_async_copy(*copy).start()


def wait_all(copies):
    for copy in copies:
        pltpu.make_async_copy(*copy).wait()


def wait_step(step, copies, begin=0):
    for r in range(begin, len(copies)):

        @pl.when(step == r)
        def _():
            wait_all(copies[r])


def tiles(count, size, body):
    if count == size:
        body(0)
    else:

        for i in range(count // size):
            body(i * size)


def row_tile(rows):
    return 272 if rows % 272 == 0 else 16


COLUMNS = 256


def column_tile(width):
    return min(COLUMNS, width)


def whole(shape):
    return pl.BlockSpec(shape, lambda i, *_: (0,) * len(shape))


def project_kernel(group, blocks, scale, scal, *refs):
    n_in = len(group.inputs)
    x_refs, bias_ref = refs[:blocks], refs[blocks]
    w_refs = refs[blocks + 1 : blocks + 1 + n_in]
    q_ref, k_ref, v_ref, held, sems = refs[blocks + 1 + n_in :]
    r = pl.program_id(0)
    mp, dp = lax.axis_size("mp"), lax.axis_size("dp")
    copies = group.copies(w_refs, held, sems, scal[0], mp, dp, [0, 1, 2])
    rows = q_ref.shape[0]

    @pl.when(r == 0)
    def _():
        start_all(sum(copies, []))

    wait_step(r, copies)

    size = column_tile(group.width)
    for begin in range(0, group.width, size):
        columns = slice(begin, begin + size)
        q = dot_nn(x_refs[-1][...], held[r, 0, :, columns]) + bias_ref[0:1, columns].astype(F32)
        q_ref[:, columns] = ((q * scale).astype(BF16) * RELAX_ALPHA).astype(BF16)
        for block in range(blocks):
            x = x_refs[block][...]
            place = slice(block * rows, (block + 1) * rows)
            k_ref[place, columns] = dot_nn(x, held[r, 1, :, columns]).astype(BF16)
            v = dot_nn(x, held[r, 2, :, columns]) + bias_ref[1:2, columns].astype(F32)
            v_ref[place, columns] = v.astype(BF16)


def project(normed, biases, group, device):
    mp = lax.axis_size("mp")
    rows, full = normed[0].shape
    blocks = len(normed)
    width = group.width
    made = lambda height: pl.BlockSpec((height, width), lambda i, *_: (0, i))
    return pl.pallas_call(
        functools.partial(project_kernel, group, blocks, 1.0 / math.sqrt(HEAD_DIM) / RELAX_ALPHA),
        grid_spec=pltpu.PrefetchScalarGridSpec(
            num_scalar_prefetch=1,
            grid=(mp,),
            in_specs=[whole((rows, full))] * blocks
            + [pl.BlockSpec((8, width), lambda i, *_: (0, i))]
            + group.specs(),
            out_specs=[made(rows), made(blocks * rows), made(blocks * rows)],
            scratch_shapes=group.scratch(mp, [0, 1, 2]),
        ),
        out_shape=[
            jax.ShapeDtypeStruct((rows, full), BF16),
            jax.ShapeDtypeStruct((blocks * rows, full), BF16),
            jax.ShapeDtypeStruct((blocks * rows, full), BF16),
        ],
        name="project",
        compiler_params=pltpu.CompilerParams(vmem_limit_bytes=22 << 20),
        cost_estimate=LIGHT,
    )(device.reshape(1), *normed, biases, *group.inputs)


def up_kernel(group_a, group_u, scal, *refs):
    (att_a, att_b, residual_ref, rows_ref, bias_ref), refs = refs[:5], refs[5:]
    wa, refs = refs[: len(group_a.inputs)], refs[len(group_a.inputs) :]
    wu, refs = refs[: len(group_u.inputs)], refs[len(group_u.inputs) :]
    branch_ref, middle_ref, mid_ref, act_ref, slope_ref, held_o, sem_o, held_u, sem_u = refs
    r = pl.program_id(0)
    mp, dp = lax.axis_size("mp"), lax.axis_size("dp")
    copies_o = sum(group_a.copies(wa, held_o, sem_o, scal[0], mp, dp, [3]), [])
    copies_u = group_u.copies(wu, held_u, sem_u, scal[0], mp, dp, [0])
    rows, full = middle_ref.shape
    width = group_a.width
    part = att_a.shape[1]

    @pl.when(r == 0)
    def _():
        start_all(copies_o)
        start_all(sum(copies_u, []))
        wait_all(copies_o)
        for block in range(full // width):
            columns = slice(block * width, (block + 1) * width)
            total = jnp.zeros((rows, width), F32)
            for layer in range(mp):
                source = att_a if layer * width < part else att_b
                first = layer * width % part
                total = total + dot_nn(source[:, first : first + width], held_o[layer, 0, columns, :])
            branch_ref[:, columns] = total + rows_ref[0:1, columns]

        def norm_rows(start):
            place = pl.ds(start, row_tile(rows))
            normal, _ = normalize(branch_ref[place, :])
            middle = residual_ref[place, :] + normal * rows_ref[1:2, :] + rows_ref[2:3, :]
            middle_ref[place, :] = middle
            normal, _ = normalize(middle)
            mid_ref[place, :] = (normal * rows_ref[3:4, :] + rows_ref[4:5, :]).astype(BF16)

        tiles(rows, row_tile(rows), norm_rows)

    wait_step(r, copies_u)

    size = column_tile(group_u.width)

    def activate(start):
        columns = pl.ds(start, size)
        u = dot_nn(mid_ref[...], held_u[r, 0, :, columns]) + bias_ref[0:1, columns]
        scale = math.sqrt(2.0 / math.pi)
        square = u * u
        bent = jnp.tanh(scale * u * (1.0 + 0.044715 * square))
        lifted = 0.5 + 0.5 * bent
        act_ref[:, columns] = (u * lifted).astype(BF16)
        slope = lifted + (0.5 * scale) * u * (1.0 - bent * bent) * (
            1.0 + (3.0 * 0.044715) * square
        )
        slope_ref[:, columns] = slope.astype(BF16)

    tiles(group_u.width, size, activate)


def feed_up(att_a, att_b, residual, vectors, u_bias, group_a, group_u, device):
    mp = lax.axis_size("mp")
    rows, full = residual.shape
    hidden = group_u.width
    made = pl.BlockSpec((rows, hidden), lambda i, *_: (0, i))
    return pl.pallas_call(
        functools.partial(up_kernel, group_a, group_u),
        grid_spec=pltpu.PrefetchScalarGridSpec(
            num_scalar_prefetch=1,
            grid=(mp,),
            in_specs=[whole(att_a.shape), whole(att_b.shape), whole((rows, full)), whole((8, full))]
            + [pl.BlockSpec((8, hidden), lambda i, *_: (0, i))]
            + group_a.specs()
            + group_u.specs(),
            out_specs=[whole((rows, full)), whole((rows, full)), whole((rows, full)), made, made],
            scratch_shapes=group_a.scratch(mp, [3]) + group_u.scratch(mp, [0]),
        ),
        out_shape=[
            jax.ShapeDtypeStruct((rows, full), F32),
            jax.ShapeDtypeStruct((rows, full), F32),
            jax.ShapeDtypeStruct((rows, full), BF16),
            jax.ShapeDtypeStruct((rows, mp * hidden), BF16),
            jax.ShapeDtypeStruct((rows, mp * hidden), BF16),
        ],
        name="feed_up",
        compiler_params=pltpu.CompilerParams(vmem_limit_bytes=38 << 20),
        cost_estimate=LIGHT,
    )(
        device.reshape(1), att_a, att_b, residual, vectors, u_bias, *group_a.inputs, *group_u.inputs
    )


def down_kernel(group_d, scal, *refs):
    (act_ref, middle_ref, cot_ref, rows_ref), refs = refs[:4], refs[4:]
    wd, refs = refs[: len(group_d.inputs)], refs[len(group_d.inputs) :]
    out_ref, grad_ref, sums_ref, held, sems, total = refs
    r = pl.program_id(0)
    mp, dp = lax.axis_size("mp"), lax.axis_size("dp")
    copies = group_d.copies(wd, held, sems, scal[0], mp, dp, [0])
    rows, full = middle_ref.shape
    width = group_d.width

    @pl.when(r == 0)
    def _():
        start_all(sum(copies, []))
        total[...] = jnp.zeros_like(total)

    wait_step(r, copies)

    size = column_tile(width)
    for block in range(full // width):

        def add(start):
            columns = pl.ds(block * width + start, size)
            total[:, columns] += dot_nn(
                act_ref[...], held[r, 0, block * width : (block + 1) * width, pl.ds(start, size)]
            )

        tiles(width, size, add)

    @pl.when(r == mp - 1)
    def _():
        sums_ref[...] = jnp.zeros_like(sums_ref)

        def norm_rows(start):
            place = pl.ds(start, row_tile(rows))
            normal, factor = normalize(total[place, :] + rows_ref[0:1, :])
            gain = rows_ref[1:2, :]
            out_ref[place, :] = (
                middle_ref[place, :] + (normal * gain + rows_ref[2:3, :])
            ).astype(BF16)
            upstream = cot_ref[place, :].astype(F32)
            scaled = upstream * gain
            grad = (
                scaled
                - jnp.mean(scaled, axis=-1, keepdims=True)
                - normal * jnp.mean(scaled * normal, axis=-1, keepdims=True)
            ) * factor
            grad = grad.astype(BF16)
            grad_ref[place, :] = grad
            sums_ref[0:8, :] += fold(upstream * normal)
            sums_ref[8:16, :] += fold(upstream)
            sums_ref[16:24, :] += fold(grad.astype(F32))

        tiles(rows, row_tile(rows), norm_rows)


def fold(value):
    return functools.reduce(jnp.add, [value[i : i + 8] for i in range(0, value.shape[0], 8)])


def feed_down(act, middle, cotangent, vectors, group_d, device):
    mp = lax.axis_size("mp")
    rows, full = middle.shape
    hidden = group_d.width
    return pl.pallas_call(
        functools.partial(down_kernel, group_d),
        grid_spec=pltpu.PrefetchScalarGridSpec(
            num_scalar_prefetch=1,
            grid=(mp,),
            in_specs=[pl.BlockSpec((rows, hidden), lambda i, *_: (0, i))]
            + [whole((rows, full)), whole((rows, full)), whole((8, full))]
            + group_d.specs(),
            out_specs=[whole((rows, full)), whole((rows, full)), whole((24, full))],
            scratch_shapes=group_d.scratch(mp, [0]) + [pltpu.VMEM((rows, full), F32)],
        ),
        out_shape=[
            jax.ShapeDtypeStruct((rows, full), BF16),
            jax.ShapeDtypeStruct((rows, full), BF16),
            jax.ShapeDtypeStruct((24, full), F32),
        ],
        name="feed_down",
        compiler_params=pltpu.CompilerParams(vmem_limit_bytes=26 << 20),
        cost_estimate=LIGHT,
    )(device.reshape(1), act, middle, cotangent, vectors, *group_d.inputs)


def back_kernel(group_a, group_u, group_d, scal, *refs):
    (grad_ref, slope_ref, branch_ref, middle_ref, cot_ref, rows_ref), refs = refs[:6], refs[6:]
    wa, refs = refs[: len(group_a.inputs)], refs[len(group_a.inputs) :]
    wu, refs = refs[: len(group_u.inputs)], refs[len(group_u.inputs) :]
    wd, refs = refs[: len(group_d.inputs)], refs[len(group_d.inputs) :]
    (pre_ref, mid_ref, low_ref, att_ref, sums_ref, u_sum_ref), refs = refs[:6], refs[6:]
    held_o, sem_o, held_u, sem_u, held_d, sem_d, total = refs
    r = pl.program_id(0)
    mp, dp = lax.axis_size("mp"), lax.axis_size("dp")
    copies_o = sum(group_a.copies(wa, held_o, sem_o, scal[0], mp, dp, [3]), [])
    copies_u = group_u.copies(wu, held_u, sem_u, scal[0], mp, dp, [0])
    copies_d = group_d.copies(wd, held_d, sem_d, scal[0], mp, dp, [0])
    copies = [one + two for one, two in zip(copies_d, copies_u)]
    rows, full = middle_ref.shape
    hidden = group_d.width
    size = column_tile(hidden)

    @pl.when(r == 0)
    def _():
        start_all(sum(copies, []) + copies_o)
        total[...] = jnp.zeros_like(total)

    wait_step(r, copies)

    def slopes(start):
        columns = pl.ds(start, size)
        grad = jnp.zeros((rows, size), F32)
        for block in range(full // hidden):
            grad = grad + dot_nt(
                grad_ref[:, block * hidden : (block + 1) * hidden],
                held_d[r, 0, pl.ds(block * hidden + start, size), :],
            )
        pre = (grad * slope_ref[:, columns].astype(F32)).astype(BF16)
        pre_ref[:, columns] = pre
        u_sum_ref[:, columns] = fold(pre.astype(F32))

    tiles(hidden, size, slopes)
    wide = column_tile(full)

    def add(start):
        columns = pl.ds(start, wide)
        total[:, columns] += dot_nt(pre_ref[...], held_u[r, 0, columns, :])

    tiles(full, wide, add)

    @pl.when(r == mp - 1)
    def _():
        sums_ref[...] = jnp.zeros_like(sums_ref)

        def norm_rows(start):
            place = pl.ds(start, row_tile(rows))

            def backward(upstream, inputs, gain):
                normal, factor = normalize(inputs)
                scaled = upstream * gain
                grad = (
                    scaled
                    - jnp.mean(scaled, axis=-1, keepdims=True)
                    - normal * jnp.mean(scaled * normal, axis=-1, keepdims=True)
                ) * factor
                return grad, fold(upstream * normal), fold(upstream)

            grad_mid, gain_sum, shift_sum = backward(
                total[place, :], middle_ref[place, :], rows_ref[0:1, :]
            )
            sums_ref[0:8, :] += gain_sum
            sums_ref[8:16, :] += shift_sum
            grad_middle = cot_ref[place, :].astype(F32) + grad_mid
            mid_ref[place, :] = grad_middle
            grad_branch, gain_sum, shift_sum = backward(
                grad_middle, branch_ref[place, :], rows_ref[1:2, :]
            )
            sums_ref[16:24, :] += gain_sum
            sums_ref[24:32, :] += shift_sum
            low = grad_branch.astype(BF16)
            low_ref[place, :] = low
            sums_ref[32:40, :] += fold(low.astype(F32))

        tiles(rows, row_tile(rows), norm_rows)
        wait_all(copies_o)
        width = group_a.width
        for layer in range(mp):
            grad = jnp.zeros((rows, width), F32)
            for block in range(full // width):
                columns = slice(block * width, (block + 1) * width)
                grad = grad + dot_nt(low_ref[:, columns], held_o[layer, 0, columns, :])
            att_ref[:, layer * width : (layer + 1) * width] = grad.astype(BF16)


def feed_back(grad, slope, branch, middle, cotangent, vectors, group_a, group_u, group_d, device):
    mp = lax.axis_size("mp")
    rows, full = middle.shape
    hidden = group_d.width
    step = pl.BlockSpec((rows, hidden), lambda i, *_: (0, i))
    return pl.pallas_call(
        functools.partial(back_kernel, group_a, group_u, group_d),
        grid_spec=pltpu.PrefetchScalarGridSpec(
            num_scalar_prefetch=1,
            grid=(mp,),
            in_specs=[whole((rows, full)), step]
            + [whole((rows, full))] * 3
            + [whole((8, full))]
            + group_a.specs()
            + group_u.specs()
            + group_d.specs(),
            out_specs=[step]
            + [whole((rows, full))] * 3
            + [whole((40, full)), pl.BlockSpec((8, hidden), lambda i, *_: (0, i))],
            scratch_shapes=group_a.scratch(mp, [3])
            + group_u.scratch(mp, [0])
            + group_d.scratch(mp, [0])
            + [pltpu.VMEM((rows, full), F32)],
        ),
        out_shape=[
            jax.ShapeDtypeStruct((rows, mp * hidden), BF16),
            jax.ShapeDtypeStruct((rows, full), F32),
            jax.ShapeDtypeStruct((rows, full), BF16),
            jax.ShapeDtypeStruct((rows, full), BF16),
            jax.ShapeDtypeStruct((40, full), F32),
            jax.ShapeDtypeStruct((8, mp * hidden), F32),
        ],
        name="feed_back",
        compiler_params=pltpu.CompilerParams(vmem_limit_bytes=46 << 20),
        cost_estimate=LIGHT,
    )(
        device.reshape(1),
        grad,
        slope,
        branch,
        middle,
        cotangent,
        vectors,
        *group_a.inputs,
        *group_u.inputs,
        *group_d.inputs,
    )


def unproject_kernel(group, which, begin, steps, added, scal, *refs):
    grads, refs = refs[: len(which)], refs[len(which) :]
    before, refs = (refs[0], refs[1:]) if added else (None, refs)
    w_refs, refs = refs[: len(group.inputs)], refs[len(group.inputs) :]
    out_ref, held, sems, total = refs
    step = pl.program_id(0)
    mp, dp = lax.axis_size("mp"), lax.axis_size("dp")
    copies = group.copies(w_refs, held, sems, scal[0], mp, dp, [0, 1, 2])
    if begin:
        copies = copies[1:]
    elif steps == 1:
        copies = copies[:1]
    full = out_ref.shape[1]

    @pl.when(step == 0)
    def _():
        start_all(sum(copies, []))
        total[...] = before[...] if added else jnp.zeros_like(total)

    wait_step(step, copies)
    r = begin + step
    size = column_tile(full)

    def add(start):
        columns = pl.ds(start, size)
        total[:, columns] += functools.reduce(
            jnp.add,
            [dot_nt(g[...], held[r, index, columns, :]) for index, g in zip(which, grads)],
        )

    tiles(full, size, add)

    @pl.when(step == pl.num_programs(0) - 1)
    def _():
        out_ref[...] = total[...].astype(out_ref.dtype)


def unproject(grads, which, group, begin, before, dtype, device):
    mp = lax.axis_size("mp")
    rows, count = grads[0].shape
    full, width = group.full, group.width
    return pl.pallas_call(
        functools.partial(
            unproject_kernel, group, which, begin, count // width, before is not None
        ),
        grid_spec=pltpu.PrefetchScalarGridSpec(
            num_scalar_prefetch=1,
            grid=(count // width,),
            in_specs=[pl.BlockSpec((rows, width), lambda i, *_: (0, i))] * len(grads)
            + ([] if before is None else [whole((rows, full))])
            + group.specs(),
            out_specs=whole((rows, full)),
            scratch_shapes=group.scratch(mp, [0, 1, 2]) + [pltpu.VMEM((rows, full), F32)],
        ),
        out_shape=jax.ShapeDtypeStruct((rows, full), dtype),
        name="unproject",
        compiler_params=pltpu.CompilerParams(vmem_limit_bytes=18 << 20),
        cost_estimate=LIGHT,
    )(device.reshape(1), *grads, *([] if before is None else [before]), *group.inputs)


def other_half_kernel(scal, left_ref, right_ref, out_ref):
    out_ref[...] = dot_tn(left_ref[...], right_ref[...]).astype(BF16)


def split_rows(total, bit_at, bit, outs):
    send_ref, keep_ref = outs
    count, rows, _ = send_ref.shape
    for j in range(count):
        base = ((j >> bit_at) << (bit_at + 1)) | (j & ((1 << bit_at) - 1))
        for ref, value in ((send_ref, 1 - bit), (keep_ref, bit)):
            start = pl.multiple_of((base + (value << bit_at)) * rows, rows)
            ref[j] = total[pl.ds(start, rows), :].astype(BF16)


def this_half_kernel(bits_at, scal, left_ref, right_ref, got_ref, *refs):
    outs, total = refs[:-1], refs[-1]
    total[...] = dot_tn(left_ref[...], right_ref[...]) + got_ref[...].astype(F32)
    step = pl.program_id(0)
    count = pl.num_programs(0) // 2
    for side in range(2):

        @pl.when(step // count == side)
        def _():
            split_rows(
                total,
                bits_at[side],
                (scal[0] >> (bits_at[side] + 1)) & 1,
                outs[2 * side : 2 * side + 2],
            )


def first_bits():
    along_x, along_y = chip_masks(lax.axis_size("dp"))
    return [order[0].bit_length() - 2 for order in (along_x + along_y, along_y + along_x)]


def other_half(left, right, device):
    rows, full = left.shape
    size = right.shape[1] // lax.axis_size("mp")
    return pl.pallas_call(
        other_half_kernel,
        grid_spec=pltpu.PrefetchScalarGridSpec(
            num_scalar_prefetch=1,
            grid=(right.shape[1] // size,),
            in_specs=[
                pl.BlockSpec((rows, full // 2), lambda i, scal: (0, 1 - scal[0] % 2)),
                pl.BlockSpec((rows, size), lambda i, scal: (0, i)),
            ],
            out_specs=pl.BlockSpec((full // 2, size), lambda i, scal: (0, i)),
        ),
        out_shape=jax.ShapeDtypeStruct((full // 2, right.shape[1]), BF16),
        name="other_half",
        compiler_params=pltpu.CompilerParams(vmem_limit_bytes=12 << 20),
        cost_estimate=LIGHT,
    )(device.reshape(1), left, right)


def this_half(left, right, got, device):
    rows, full = left.shape
    mp = lax.axis_size("mp")
    size = right.shape[1] // mp
    quarters = lax.axis_size("dp") // 2
    shape = (quarters // 2, full // 2 // quarters, mp // 2 * size)
    block = (quarters // 2, full // 2 // quarters, size)
    last = mp // 2 - 1
    sides = [lambda i, scal: (0, 0, jnp.minimum(i, last))] * 2 + [
        lambda i, scal: (0, 0, jnp.maximum(i - last - 1, 0))
    ] * 2
    return pl.pallas_call(
        functools.partial(this_half_kernel, first_bits()),
        grid_spec=pltpu.PrefetchScalarGridSpec(
            num_scalar_prefetch=1,
            grid=(mp,),
            in_specs=[
                pl.BlockSpec((rows, full // 2), lambda i, scal: (0, scal[0] % 2)),
                pl.BlockSpec((rows, size), lambda i, scal: (0, i)),
                pl.BlockSpec((full // 2, size), lambda i, scal: (0, i)),
            ],
            out_specs=[pl.BlockSpec(block, index) for index in sides],
            scratch_shapes=[pltpu.VMEM((full // 2, size), F32)],
        ),
        out_shape=[jax.ShapeDtypeStruct(shape, BF16)] * 4,
        name="this_half",
        compiler_params=pltpu.CompilerParams(vmem_limit_bytes=18 << 20),
        cost_estimate=LIGHT,
    )(device.reshape(1), left, right, got)


def attention_dots(width, lefts, branch, grads, attended, layer, put):
    grad_q, near_k, near_v, far_k, far_v = grads
    rows = grad_q.shape[0]
    columns = slice(layer * width, (layer + 1) * width)
    put(0, dot_tn(lefts[-1][...], grad_q[:, columns]))
    for index, near, far in ((1, near_k, far_k), (2, near_v, far_v)):
        total = dot_tn(lefts[-1][...], near[:, columns])
        for block in range(len(lefts) - 1):
            total = total + dot_tn(lefts[block][...], far[block * rows : (block + 1) * rows, columns])
        put(index, total)
    put(3, dot_tn(branch[...], attended[:, columns]))


def attention_other_kernel(width, blocks, scal, *refs):
    lefts, (branch, *grads, attended, out_ref) = refs[:blocks], refs[blocks:]
    for layer in range(attended.shape[1] // width):

        def put(index, value):
            place = (layer * 4 + index) * width
            out_ref[:, place : place + width] = value.astype(BF16)

        attention_dots(width, lefts, branch, grads, attended, layer, put)


def attention_this_kernel(width, blocks, bits_at, scal, *refs):
    lefts, (branch, *grads, attended, got_ref) = refs[:blocks], refs[blocks : blocks + 8]
    outs, total = refs[blocks + 8 : -1], refs[-1]
    layers = attended.shape[1] // width
    for side in range(2):
        for local in range(layers // 2):
            layer = side * (layers // 2) + local

            def put(index, value):
                place = (layer * 4 + index) * width
                total[:, index * width : (index + 1) * width] = value + got_ref[
                    :, place : place + width
                ].astype(F32)

            attention_dots(width, lefts, branch, grads, attended, layer, put)
            columns = pl.ds(local * 4 * width, 4 * width)
            split_rows(
                total,
                bits_at[side],
                (scal[0] >> (bits_at[side] + 1)) & 1,
                [ref.at[:, :, columns] for ref in outs[2 * side : 2 * side + 2]],
            )


def attention_specs(normed, branch, grads, part, core_of):
    rows, full = branch.shape
    left = pl.BlockSpec((rows, full // 2), lambda i, scal: (0, core_of(scal)))
    wide = grads[0].shape[1]
    some = lambda height: pl.BlockSpec((height, wide), lambda i, scal: (0, part))
    return (
        [left] * (len(normed) + 1)
        + [whole(g.shape) for g in grads[:3]]
        + [some(g.shape[0]) for g in grads[3:]]
        + [some(rows)]
    )


def attention_other(normed, branch, grads, attended, part, width, device):
    full = branch.shape[1]
    out = (full // 2, 4 * grads[0].shape[1])
    return pl.pallas_call(
        functools.partial(attention_other_kernel, width, len(normed)),
        grid_spec=pltpu.PrefetchScalarGridSpec(
            num_scalar_prefetch=1,
            grid=(1,),
            in_specs=attention_specs(normed, branch, grads, part, lambda s: 1 - s[0] % 2),
            out_specs=whole(out),
        ),
        out_shape=jax.ShapeDtypeStruct(out, BF16),
        name="attention_other",
        compiler_params=pltpu.CompilerParams(vmem_limit_bytes=12 << 20),
        cost_estimate=LIGHT,
    )(device.reshape(1), *normed, branch, *grads, attended)


def attention_this(normed, branch, grads, attended, got, part, width, device):
    full = branch.shape[1]
    quarters = lax.axis_size("dp") // 2
    shape = (quarters // 2, full // 2 // quarters, 2 * grads[0].shape[1])
    return pl.pallas_call(
        functools.partial(attention_this_kernel, width, len(normed), first_bits()),
        grid_spec=pltpu.PrefetchScalarGridSpec(
            num_scalar_prefetch=1,
            grid=(1,),
            in_specs=attention_specs(normed, branch, grads, part, lambda s: s[0] % 2)
            + [whole(got.shape)],
            out_specs=[whole(shape)] * 4,
            scratch_shapes=[pltpu.VMEM((full // 2, 4 * width), F32)],
        ),
        out_shape=[jax.ShapeDtypeStruct(shape, BF16)] * 4,
        name="attention_this",
        compiler_params=pltpu.CompilerParams(vmem_limit_bytes=16 << 20),
        cost_estimate=LIGHT,
    )(device.reshape(1), *normed, branch, *grads, attended, got)


def next_stage_kernel(scal, *refs):
    ins, outs = refs[:8], refs[8:]
    for index, out in enumerate(outs):
        one, two = ins[2 * index], ins[2 * index + 1]
        out[...] = (one[0].astype(F32) + two[0].astype(F32)).astype(BF16)


def next_stage(keeps, gots, bits, device):
    _, rows, columns = keeps[0].shape
    specs, inputs = [], []
    for side in range(2):
        for flip in (1, 0):
            where = lambda i, scal, side=side, flip=flip: (
                ((scal[0] >> (bits[side] + 1)) & 1) ^ flip,
                0,
                0,
            )
            specs += [pl.BlockSpec((1, rows, columns), where)] * 2
            inputs += [keeps[side], gots[side]]
    return pl.pallas_call(
        next_stage_kernel,
        grid_spec=pltpu.PrefetchScalarGridSpec(
            num_scalar_prefetch=1,
            grid=(1,),
            in_specs=specs,
            out_specs=[whole((rows, columns))] * 4,
        ),
        out_shape=[jax.ShapeDtypeStruct((rows, columns), BF16)] * 4,
        name="next_stage",
        compiler_params=pltpu.CompilerParams(vmem_limit_bytes=10 << 20),
        cost_estimate=LIGHT,
    )(device.reshape(1), *inputs)


def by_layer_kernel(places, keep_a, got_a, keep_b, got_b, send_ref, rest_ref):
    width = send_ref.shape[2]
    each = len(places) // 2
    for index, (sent, spot) in enumerate(places):
        keep, got = ((keep_a, got_a), (keep_b, got_b))[index // each]
        columns = slice(index % each * width, (index % each + 1) * width)
        value = keep[:, columns].astype(F32) + got[:, columns].astype(F32)
        if sent:
            send_ref[spot] = value.astype(BF16)
        else:
            rest_ref[spot] = value


def by_layer_pieces(keeps, gots, layers):
    rows = keeps[0].shape[0]
    width = keeps[0].shape[1] * 2 // len(layers)
    odd = [r for r in layers if r & 1]
    even = [r for r in layers if not r & 1]
    places = [(r & 1, (odd if r & 1 else even).index(r)) for r in layers]
    send, rest = pl.pallas_call(
        functools.partial(by_layer_kernel, places),
        out_shape=[
            jax.ShapeDtypeStruct((len(odd), rows, width), BF16),
            jax.ShapeDtypeStruct((len(even), rows, width), F32),
        ],
        in_specs=[pl.BlockSpec(memory_space=pltpu.VMEM)] * 4,
        out_specs=[pl.BlockSpec(memory_space=pltpu.VMEM)] * 2,
        name="by_layer_pieces",
        compiler_params=pltpu.CompilerParams(vmem_limit_bytes=8 << 20),
        cost_estimate=LIGHT,
    )(keeps[0], gots[0], keeps[1], gots[1])
    return send, rest, odd, even


def reduce_flow(send, add, layers, device):
    (send,) = yield (send,)
    (got,) = yield (swap(send, "dp", 1),)
    send_a, keep_a, send_b, keep_b = add(got)
    along_x, along_y = chip_masks(lax.axis_size("dp"))
    orders = (along_x + along_y, along_y + along_x)
    bits = len(orders[0])
    sends, keeps = [send_a, send_b], [keep_a, keep_b]
    lefts = []
    for side, order in enumerate(orders):
        left = list(range(bits - 1, -1, -1))
        left.remove(order[0].bit_length() - 2)
        lefts.append(left)
        keeps[side] = keeps[side].reshape((2,) * (bits - 1) + keeps[side].shape[1:])
    for step in range(bits):
        sends = yield tuple(sends)
        gots = yield tuple(swap(value, "dp", order[step]) for value, order in zip(sends, orders))
        gots = [got.reshape(keep.shape) for got, keep in zip(gots, keeps)]
        if step + 1 == bits:
            break
        picks = [order[step + 1].bit_length() - 2 for order in orders]
        if keeps[0].ndim == 3:
            send_a, keep_a, send_b, keep_b = next_stage(keeps, gots, picks, device)
            sends, keeps = [send_a, send_b], [keep_a, keep_b]
            continue
        sends, next_keeps = [], []
        for side, which in enumerate(picks):
            axis = lefts[side].index(which)
            lefts[side].remove(which)
            bit = (device >> (which + 1)) & 1

            def part(value):
                summed = [
                    lax.dynamic_index_in_dim(item, value, axis, keepdims=False).astype(F32)
                    for item in (keeps[side], gots[side])
                ]
                return (summed[0] + summed[1]).astype(BF16)

            sends.append(part(1 - bit))
            next_keeps.append(part(bit))
        keeps = next_keeps
    send, rest, odd, even = by_layer_pieces(keeps, gots, layers)
    (send,) = yield (send,)
    (got,) = yield (swap(send, "mp", 1),)
    held = {r: rest[i] for i, r in enumerate(even)}
    for i, r in enumerate(odd):
        value = got[i].astype(F32)
        held[r ^ 1] = held[r ^ 1] + value if r ^ 1 in held else value
    for bit in range(1, lax.axis_size("mp").bit_length() - 1):
        mask = 1 << bit
        away = [r for r in sorted(held) if r & mask]
        if away:
            send = held[away[0]] if len(away) == 1 else jnp.stack([held[r] for r in away])
            (send,) = yield (send.astype(BF16),)
            (got,) = yield (swap(send, "mp", mask),)
            got = [got] if len(away) == 1 else list(got)
            for r, value in zip(away, got):
                del held[r]
                value = value.astype(F32)
                held[r ^ mask] = held[r ^ mask] + value if r ^ mask in held else value
    return held[0]


def fill_kernel(plan, rows, dp, scal, *refs):
    ins, (qkv_ref, out_ref, turned) = refs[:-3], refs[-3:]
    width = turned.shape[1]
    for ref, (side, masks) in zip(ins, plan):
        for index, mask in enumerate(masks):
            place = pl.ds(pl.multiple_of(position(scal[0], mask, dp) * rows, rows), rows)
            for inner in range(2):
                value = ref[index, :, inner * width : (inner + 1) * width].astype(F32)
                if side * 2 + inner < 3:
                    qkv_ref[side * 2 + inner, place, :] = value
                else:
                    turned[place, :] = value
    out_ref[...] = turned[...].T


def fill_attention(arrays, full, width, device):
    dp = lax.axis_size("dp")
    inputs = [value for _, _, value in arrays]
    vmem = pl.BlockSpec(memory_space=pltpu.VMEM)
    return pl.pallas_call(
        functools.partial(fill_kernel, [(side, m) for side, m, _ in arrays], full // dp, dp),
        grid_spec=pltpu.PrefetchScalarGridSpec(
            num_scalar_prefetch=1,
            grid=(),
            in_specs=[vmem] * len(inputs),
            out_specs=[vmem, vmem],
            scratch_shapes=[pltpu.VMEM((full, width), F32)],
        ),
        out_shape=[
            jax.ShapeDtypeStruct((3, full, width), F32),
            jax.ShapeDtypeStruct((width, full), F32),
        ],
        name="fill_attention",
        compiler_params=pltpu.CompilerParams(vmem_limit_bytes=32 << 20),
        cost_estimate=LIGHT,
    )(device.reshape(1), *inputs)


def fill_ffn_kernel(turn, in_ref, out_ref):
    group, _, rows, hidden = in_ref.shape
    value = in_ref[...].astype(F32).reshape(group * rows, hidden)
    out_ref[...] = value.T if turn else value


def fill_ffn(gathered, turn):
    dp, rows, hidden = gathered.shape
    quarters = dp // 2
    group = quarters
    count = quarters // group
    full = dp * rows
    block = (hidden, group * rows) if turn else (group * rows, hidden)
    shape = (hidden, full) if turn else (full, hidden)
    where = (lambda c, j: (0, c * count + j)) if turn else (lambda c, j: (c * count + j, 0))
    return pl.pallas_call(
        functools.partial(fill_ffn_kernel, turn),
        grid=(2, count),
        in_specs=[pl.BlockSpec((group, 1, rows, hidden), lambda c, j: (j, c, 0, 0))],
        out_specs=pl.BlockSpec(block, where),
        out_shape=jax.ShapeDtypeStruct(shape, F32),
        name="fill_ffn",
        compiler_params=pltpu.CompilerParams(vmem_limit_bytes=24 << 20),
        cost_estimate=LIGHT,
    )(gathered.reshape(quarters, 2, rows, hidden))


def small_flow(value):
    for axis in ("dp", "mp"):
        for bit in range(lax.axis_size(axis).bit_length() - 1):
            (value,) = yield (value,)
            (got,) = yield (swap(value, axis, 1 << bit),)
            value = value + got
    return value


def spread_flow(sides):
    return (yield from spread_steps(sides))


def finish(flows, *values):
    while any(not flow.over for flow in flows):
        out = meet(flows, *values)
        values = out if len(values) > 1 else (out,)
    return values


def drain(*flows):
    for flow in flows:
        while not flow.over:
            flow.move(flow.held)


def eight_rows(*rows):
    stacked = jnp.stack([row.astype(F32) for row in rows])
    return jnp.pad(stacked, ((0, 8 - stacked.shape[0]), (0, 0)))


def on_device(
    tokens,
    groups,
    lengths,
    qkv_weight,
    qv_bias,
    out_weight,
    out_bias,
    up_weight,
    up_bias,
    down_weight,
    down_bias,
    norm_gain,
    norm_bias,
    group_table,
    cotangent,
):
    dp, mp = lax.axis_size("dp"), lax.axis_size("mp")
    device, layer = lax.axis_index("dp"), lax.axis_index("mp")
    core = device & 1
    rows, full = tokens.shape
    width = qkv_weight.shape[2]
    hidden = up_weight.shape[1]
    blocks = SEQ_LEN // rows
    place_in_seq = layer % blocks
    length = lax.dynamic_index_in_dim(lengths, layer // blocks, keepdims=False)
    along_x, along_y = chip_masks(dp)
    stages = len(along_x + along_y)
    gains = norm_gain.astype(F32)
    shifts = norm_bias.astype(F32)
    part, half = full // 2, full // 2

    shard_a = [(qkv_weight, 0, False), (out_weight, 3, True)]
    shard_u, shard_d = [(up_weight[None], 0, False)], [(down_weight, 0, True)]
    small_here = jnp.concatenate([qv_bias[0], qv_bias[1], up_bias]).reshape(-1, width)
    n_small = small_here.shape[0]
    small_here = jnp.pad(small_here, ((0, -n_small % 16), (0, 0)))
    slice_a = jnp.concatenate(
        [
            own_slice(qkv_weight, False, device, width),
            own_slice(out_weight, True, device, width),
        ]
    )
    flow_a = Flow(gather_flow(slice_a, small_here))
    tokens = begin([flow_a], tokens)

    order_of = layer ^ jnp.arange(mp)
    onehot = (
        groups[:, None] == lax.broadcasted_iota(jnp.int32, (1, group_table.shape[0]), 1)
    ).astype(BF16)
    residual = tokens.astype(F32) + jnp.dot(onehot, group_table, preferred_element_type=F32)
    normed, norm_one, inv_one = norm_forward(residual, gains[0], shifts[0])
    normed_low = normed.astype(BF16)

    def rows_flow(value):
        (value,) = yield (value,)
        return (yield tuple(swap(value, "mp", m) for m in range(1, blocks)))

    key_ids = lax.broadcasted_iota(jnp.int32, (blocks, rows, 1), 1)
    block_ids = lax.broadcasted_iota(jnp.int32, (blocks, rows, 1), 0)
    block_ids = place_in_seq ^ ((block_ids + 1) % blocks)
    shown = (block_ids <= place_in_seq) & (block_ids * rows + key_ids < length)
    spot = lax.broadcasted_iota(jnp.int32, (blocks, rows, LANES), 2) % HEAD_DIM
    key_const = jnp.where(
        spot == 0,
        jnp.where(shown, 0.0, MASKED_SCORE),
        jnp.where(spot <= 3, 1.0, 0.0),
    )
    key_const = key_const.astype(BF16).reshape(blocks * rows, LANES)

    slice_u = own_slice(up_weight[None], False, device, hidden)
    slice_d = own_slice(down_weight, True, device, hidden)
    flow_r = Flow(rows_flow(normed_low))
    normed_low, slice_u, slice_d = meet([flow_a], normed_low, slice_u, slice_d)
    flow_u, flow_d = Flow(gather_flow(slice_u)), Flow(gather_flow(slice_d))
    layer_stages = mp.bit_length() - 1
    for _ in range(layer_stages - 1):
        normed_low = meet([flow_a], normed_low)
    normed_low = begin([flow_r, flow_u], normed_low)
    for _ in range(stages - 1):
        normed_low = meet([flow_a], normed_low)
    normed_low = meet([flow_a, flow_u, flow_r], normed_low)
    for _ in range(layer_stages - 2):
        normed_low = meet([flow_u], normed_low)
    normed_low = meet([flow_a, flow_u], normed_low)
    normed_low = begin([flow_d], normed_low)
    arrays_a, small_all = flow_a.result
    group_a = Weights(shard_a, arrays_a)
    small_all = jnp.stack(small_all)[:, :n_small].reshape(mp, -1).astype(F32)
    qv_rows = small_all[:, : 2 * width].reshape(mp, 2, width).transpose(1, 0, 2).reshape(2, full)
    u_rows = small_all[:, 2 * width :].reshape(1, -1)
    qv_rows = jnp.pad(qv_rows, ((0, 6), (0, 0)))
    u_rows = jnp.pad(u_rows, ((0, 7), (0, 0)))
    seq_normed = tuple(flow_r.result) + (normed_low,)
    queries, keys, values = project(seq_normed, qv_rows, group_a, device)
    queries, keys, values = meet([flow_d, flow_u], queries, keys, values)
    attended_a, aug_a = attend(queries, keys, values, key_const, 0, part)
    for _ in range(layer_stages - 1):
        attended_a, queries = meet([flow_d], attended_a, queries)
    attended_b, aug_b = attend(queries, keys, values, key_const, part, part)
    attended = jnp.concatenate([attended_a, attended_b], axis=1)
    aug = jnp.concatenate([aug_a, aug_b], axis=1)
    attended_b = meet([flow_u, flow_d], attended_b)
    for _ in range(stages - 2):
        attended_b = meet([flow_d], attended_b)
    (attended_b,) = finish([flow_u], attended_b)
    group_u = Weights(shard_u, flow_u.result[0])
    branch, middle, mid_low, act, slope = feed_up(
        attended_a,
        attended_b,
        residual,
        eight_rows(out_bias, gains[1], shifts[1], gains[2], shifts[2]),
        u_rows,
        group_a,
        group_u,
        device,
    )
    (act,) = finish([flow_d], act)
    group_d = Weights(shard_d, flow_d.result[0])
    output, grad_ffn, sums_ffn = feed_down(
        act, middle, cotangent, eight_rows(down_bias, gains[3], shifts[3]), group_d, device
    )

    everyone = list(range(mp))

    def weight_flow(left, right):
        return Flow(
            reduce_flow(
                other_half(left, right, device),
                lambda got: this_half(left, right, got, device),
                everyone,
                device,
            )
        )

    flow_d = weight_flow(grad_ffn, act)
    grad_ffn = begin([flow_d], grad_ffn)
    grad_ffn = meet([flow_d], grad_ffn)
    grad_pre, grad_middle, grad_branch, grad_attended, sums_back, sums_up = feed_back(
        grad_ffn,
        slope,
        branch,
        middle,
        cotangent,
        eight_rows(gains[2], gains[1]),
        group_a,
        group_u,
        group_d,
        device,
    )
    grad_pre, grad_branch, grad_attended = meet([flow_d], grad_pre, grad_branch, grad_attended)
    flow_u = weight_flow(mid_low, grad_pre)
    grad_branch, grad_attended = begin([flow_u], grad_branch, grad_attended)

    def attention_flow(grads, layers):
        index = layers[0] * width // part
        return Flow(
            reduce_flow(
                attention_other(seq_normed, grad_branch, grads, attended, index, width, device),
                lambda got: attention_this(
                    seq_normed, grad_branch, grads, attended, got, index, width, device
                ),
                layers,
                device,
            )
        )

    layers_b, layers_a = everyone[: mp // 2], everyone[mp // 2 :]
    back = functools.partial(
        attend_back, queries, keys, values, key_const, aug, grad_attended, attended
    )
    far_q, far_k, far_v = back(0, full)
    far_grad = unproject((far_k, far_v), (1, 2), group_a, 0, None, BF16, device)
    far_grad, far_q, far_k, far_v = ordered([flow_d, flow_u], (far_grad, far_q, far_k, far_v))
    flow_f = Flow(rows_back(far_grad, rows, blocks))
    far_q, far_k, far_v = begin([flow_f, flow_u], far_q, far_k, far_v)
    grads_a = back(part, part, far_q)
    flow_qa = attention_flow((*grads_a, far_k, far_v), layers_a)
    far_q, *grads_a = meet([flow_u, flow_f], far_q, *grads_a)
    far_q, *grads_a = begin([flow_qa], far_q, *grads_a)
    near_a = unproject(grads_a, (0, 1, 2), group_a, mp // 2, None, F32, device)
    far_q, near_a = meet([flow_qa], far_q, near_a)
    far_q, near_a = begin([flow_d], far_q, near_a)
    grads_b = back(0, part, far_q)
    grads_b = ordered([flow_u, flow_qa, flow_d], grads_b)
    flow_qb = attention_flow((*grads_b, far_k, far_v), layers_b)
    grads_b = begin([flow_qb], *grads_b)
    grads_b = begin([flow_u, flow_qa, flow_d], *grads_b)
    near_b = unproject(grads_b, (0, 1, 2), group_a, 0, near_a, F32, device)
    near_b, *grads_a, sums_ffn, sums_back, sums_up = meet(
        [flow_qb, flow_qa], near_b, *grads_a, sums_ffn, sums_back, sums_up
    )
    near_b = meet([flow_u, flow_d], near_b)
    drain(flow_d)
    down_mine = flow_d.result.astype(BF16)
    down_all = lax.all_gather(down_mine, "dp", axis=0)
    grad_normed = near_b
    for value in flow_f.result:
        grad_normed = grad_normed + value.astype(F32)
    back_one, gain_one, shift_one = norm_backward(grad_normed, norm_one, inv_one, gains[0])
    input_grad = grad_middle + back_one
    table_part = jnp.dot(
        onehot.astype(F32).T, input_grad, precision=PRECISE, preferred_element_type=F32
    )
    grad_q_sum = jnp.concatenate([jnp.sum(g[0].astype(F32), axis=0) for g in (grads_b, grads_a)])
    grad_v_sum = jnp.concatenate([jnp.sum(g[2].astype(F32), axis=0) for g in (grads_b, grads_a)])
    grad_v_sum = grad_v_sum + jnp.sum(far_v.astype(F32), axis=0)
    ffn_sums = jnp.sum(sums_ffn.reshape(3, 8, full), axis=1)
    back_sums = jnp.sum(sums_back.reshape(5, 8, full), axis=1)
    up_bias_part = jnp.sum(sums_up, axis=0)
    by_layer = jnp.concatenate(
        [grad_q_sum.reshape(mp, -1), grad_v_sum.reshape(mp, -1), up_bias_part.reshape(mp, -1)],
        axis=1,
    )
    by_layer = jnp.take(by_layer, order_of, axis=0)
    wide = by_layer.shape[1]
    by_layer = jnp.pad(by_layer, ((0, 0), (0, -wide % full))).reshape(-1, full)
    input_grad, table_part, gain_one, shift_one = meet(
        [flow_qb, flow_qa, flow_u], input_grad, table_part, gain_one, shift_one
    )
    drain(flow_u)
    up_mine = flow_u.result.astype(BF16)
    up_all = lax.all_gather(up_mine, "dp", axis=0)
    parts = jnp.concatenate(
        [
            jnp.stack([gain_one, back_sums[2], back_sums[0], ffn_sums[0]]),
            jnp.stack([shift_one, back_sums[3], back_sums[1], ffn_sums[1]]),
            jnp.stack([back_sums[4], ffn_sums[2]]),
            table_part,
            by_layer,
        ]
    )
    flow_s = Flow(small_flow(parts))
    drain(flow_qa, flow_qb)
    mine = (flow_qa.result + flow_qb.result).astype(BF16)
    flow_o = Flow(spread_flow((mine[:, : 2 * width], mine[:, 2 * width :])))
    for _ in range(2 * (dp.bit_length() + mp.bit_length() - 3)):
        flow_s.move(flow_s.held)
    down_grad = fill_ffn(down_all, True)
    up_grad = fill_ffn(up_all, False)
    down_grad, up_grad = begin([flow_s], down_grad, up_grad)
    drain(flow_o, flow_s)
    qkv_grad, out_grad = fill_attention(flow_o.result, full, width, device)

    parts = flow_s.result
    gain_grad, shift_grad = parts[:4], parts[4:8]
    out_bias_grad, down_bias_grad = parts[8], parts[9]
    n_groups = group_table.shape[0]
    table_grad = parts[10 : 10 + n_groups]
    by_layer = parts[10 + n_groups :].reshape(mp, -1)
    mine = lax.dynamic_index_in_dim(by_layer, layer, keepdims=False)
    qv_bias_grad = mine[: 2 * width].reshape(2, width)
    up_bias_grad = mine[2 * width : 2 * width + hidden]
    return (
        output,
        input_grad,
        qkv_grad,
        qv_bias_grad,
        out_grad,
        out_bias_grad,
        up_grad,
        up_bias_grad,
        down_grad,
        down_bias_grad,
        gain_grad,
        shift_grad,
        table_grad,
    )


def rows_back(value, rows, blocks):
    (value,) = yield (value,)
    return (
        yield tuple(swap(value[(m - 1) * rows : m * rows], "mp", m) for m in range(1, blocks))
    )


def solution(mesh):
    placed = (
        P(("dp", "mp"), None),
        P(("dp", "mp")),
        P("dp"),
        P(None, None, "mp"),
        P(None, "mp"),
        P("mp", None),
        P(),
        P(None, "mp"),
        P("mp"),
        P("mp", None),
        P(),
        P(),
        P(),
        P(),
        P(("dp", "mp"), None),
    )
    return jax.shard_map(
        on_device,
        mesh=mesh,
        in_specs=placed,
        out_specs=(
            P(("dp", "mp"), None),
            P(("dp", "mp"), None),
            P(None, None, "mp"),
            P(None, "mp"),
            P("mp", None),
            P(),
            P(None, "mp"),
            P("mp"),
            P("mp", None),
            P(),
            P(),
            P(),
            P(),
        ),
        check_vma=False,
    )
```

```python
import functools
import math

import jax
import jax.numpy as jnp
from jax import lax
from jax.experimental import pallas as pl
from jax.experimental.pallas import tpu as pltpu
from jax.sharding import PartitionSpec as P

HEAD_DIM = 64
SEQ_LEN = 1088
RELAX_ALPHA = 32.0
NORM_EPSILON = 1e-05
MASKED_SCORE = -1000000000.0
PRECISE = lax.Precision.HIGHEST
BF16 = jnp.bfloat16
F32 = jnp.float32
LANES = 128
LIGHT = pl.CostEstimate(flops=1000, bytes_accessed=1000, transcendentals=0)


def swap(value, axis, mask):
    count = lax.axis_size(axis)
    return lax.ppermute(value, axis, [(i, i ^ mask) for i in range(count)])


def normalize(inputs):
    centred = inputs - jnp.mean(inputs, axis=-1, keepdims=True)
    factor = lax.rsqrt(jnp.mean(centred * centred, axis=-1, keepdims=True) + NORM_EPSILON)
    return centred * factor, factor


def norm_forward(inputs, gain_row, shift_row):
    centred = inputs - jnp.mean(inputs, axis=-1, keepdims=True)
    factor = lax.rsqrt(jnp.mean(centred * centred, axis=-1, keepdims=True) + NORM_EPSILON)
    normal = centred * factor
    return (normal * gain_row + shift_row, normal, factor)


def norm_backward(upstream, normal, factor, gain_row):
    scaled = upstream * gain_row
    adjusted = (
        scaled
        - jnp.mean(scaled, axis=-1, keepdims=True)
        - normal * jnp.mean(scaled * normal, axis=-1, keepdims=True)
    )
    return (adjusted * factor, jnp.sum(upstream * normal, axis=0), jnp.sum(upstream, axis=0))


def dot_nn(a, b):
    return lax.dot_general(a, b, (((1,), (0,)), ((), ())), preferred_element_type=F32)


def dot_nt(a, b):
    return lax.dot_general(a, b, (((1,), (1,)), ((), ())), preferred_element_type=F32)


def dot_tn(a, b):
    return lax.dot_general(a, b, (((0,), (0,)), ((), ())), preferred_element_type=F32)


def query_tile(rows):
    return rows // 2 if (rows // 2) % 16 == 0 else rows


def padded(rows):
    return -(-rows // LANES) * LANES


def three_parts(value):
    high = value.astype(BF16)
    rest = value - high.astype(F32)
    mid = rest.astype(BF16)
    return high, mid, (rest - mid.astype(F32)).astype(BF16)


def attend_kernel(blocks, rows, q_ref, k_ref, v_ref, kc_ref, out_ref, aug_ref):
    tile = query_tile(rows)
    far = (blocks - 1) * rows
    lane = lax.broadcasted_iota(jnp.int32, (1, LANES), 1)
    first = lane < HEAD_DIM
    mine = [first, jnp.logical_not(first)]
    keys = jnp.concatenate([k_ref[...], kc_ref[...]], axis=1)
    special = jnp.where(lane == 0, 1.0, 0.0).astype(BF16)
    special = jnp.broadcast_to(special, (tile, LANES))
    starts = list(range(0, rows, tile))

    def scores_of(start):
        q = q_ref[start : start + tile, :]
        zero = jnp.zeros_like(q)
        both = jnp.concatenate(
            [jnp.concatenate([jnp.where(m, q, zero), special], axis=1) for m in mine], axis=0
        )
        return dot_nt(both, keys[: far + start + tile])

    scores = [scores_of(start) for start in starts]
    for start, score in zip(starts, scores):
        limit = far + start + tile
        cut = (far + start) // LANES * LANES
        row_ids = lax.broadcasted_iota(jnp.int32, (2 * tile, limit - cut), 0)
        row_ids = start + far - cut + jnp.where(row_ids >= tile, row_ids - tile, row_ids)
        columns = lax.broadcasted_iota(jnp.int32, (2 * tile, limit - cut), 1)
        last = jnp.where(columns <= row_ids, score[:, cut:], MASKED_SCORE)
        score = jnp.concatenate([score[:, :cut], last], axis=1) if cut else last
        top = jnp.max(score, axis=-1, keepdims=True)
        exponent = jnp.exp(score - top)
        total = jnp.sum(exponent, axis=-1, keepdims=True)
        gathered = dot_nn(exponent.astype(BF16), v_ref[0:limit, :]) / total
        out_ref[start : start + tile, :] = jnp.where(
            first, gathered[:tile], gathered[tile:]
        ).astype(BF16)
        parts = three_parts(-(top + jnp.log(total)))
        spot = lane % HEAD_DIM
        augs = []
        for head in range(2):
            aug = jnp.where(spot == 0, 1.0, jnp.zeros((tile, LANES), F32)).astype(BF16)
            for index, value in enumerate(parts):
                aug = jnp.where(spot == index + 1, value[head * tile : (head + 1) * tile], aug)
            augs.append(aug)
        aug_ref[start : start + tile, :] = jnp.where(first, augs[0], augs[1])


def attend(queries, keys, values, key_const, begin, count):
    rows = queries.shape[0]
    span = keys.shape[0]
    first = begin // LANES
    pair = lambda height: pl.BlockSpec((height, LANES), lambda i: (0, first + i))
    made = lambda height: pl.BlockSpec((height, LANES), lambda i: (0, i))
    return pl.pallas_call(
        functools.partial(attend_kernel, span // rows, rows),
        grid=(count // LANES,),
        in_specs=[
            pair(rows),
            pair(span),
            pair(span),
            pl.BlockSpec((span, LANES), lambda i: (0, 0)),
        ],
        out_specs=[made(rows), made(rows)],
        out_shape=[
            jax.ShapeDtypeStruct((rows, count), BF16),
            jax.ShapeDtypeStruct((rows, count), BF16),
        ],
        name="attend",
        compiler_params=pltpu.CompilerParams(vmem_limit_bytes=14 << 20),
        cost_estimate=LIGHT,
    )(queries, keys, values, key_const)


def attend_back_kernel(
    causal, q_ref, k_ref, v_ref, kc_ref, aug_ref, go_ref, out_ref, *refs
):
    before, refs = (refs[0], refs[1:]) if causal else (None, refs)
    dq_ref, dk_ref, dv_ref, q_both, g_both, ds_ref = refs
    rows = q_ref.shape[0]
    span = k_ref.shape[0]
    key_tile = query_tile(rows)
    wide = padded(rows)
    lane = lax.broadcasted_iota(jnp.int32, (1, LANES), 1)
    first = lane < HEAD_DIM
    mine = [first, jnp.logical_not(first)]
    q_pair, aug, go = q_ref[...], aug_ref[...], go_ref[...]
    zero = jnp.zeros_like(q_pair)
    weighed = go.astype(F32) * out_ref[...].astype(F32)
    pad = jnp.zeros((wide - rows, 2 * LANES), BF16)
    for head in range(2):
        m = mine[head]
        place = head * wide
        q_both[place : place + rows, 0:LANES] = jnp.where(m, q_pair, zero)
        q_both[place : place + rows, LANES:] = jnp.where(m, aug, zero)
        parts = three_parts(-jnp.sum(jnp.where(m, weighed, 0.0), axis=-1, keepdims=True))
        g_aug = zero
        for index, value in enumerate(parts):
            g_aug = jnp.where(lane == index + 1, value, g_aug)
        g_both[place : place + rows, 0:LANES] = jnp.where(m, go, zero)
        g_both[place : place + rows, LANES:] = g_aug
        if wide > rows:
            q_both[place + rows : place + wide, :] = pad
            g_both[place + rows : place + wide, :] = pad
    keys = jnp.concatenate([k_ref[...], kc_ref[...]], axis=1)
    v_const = jnp.where((lane >= 1) & (lane <= 3), 1.0, 0.0).astype(BF16)
    values = jnp.concatenate([v_ref[...], jnp.broadcast_to(v_const, k_ref.shape)], axis=1)

    def dots_of(start):
        stop = start + key_tile
        return dot_nt(keys[start:stop], q_both[...]), dot_nt(values[start:stop], g_both[...])

    starts = list(range(0, span, key_tile))
    ahead = dots_of(starts[0])
    for index, start in enumerate(starts):
        stop = start + key_tile
        scores, centred = ahead
        if index + 1 < len(starts):
            ahead = dots_of(starts[index + 1])
        exact = jnp.exp(scores)
        if causal:
            key_ids = start + lax.broadcasted_iota(jnp.int32, (key_tile, 2 * wide), 0)
            query_ids = lax.broadcasted_iota(jnp.int32, (key_tile, 2 * wide), 1)
            query_ids = jnp.where(query_ids >= wide, query_ids - wide, query_ids)
            exact = jnp.where(key_ids <= query_ids, exact, 0.0)
        grad_scores = (exact * centred).astype(BF16)
        ds_ref[start:stop, :] = grad_scores
        dv_ref[start:stop, :] = dot_nn(exact.astype(BF16), g_both[:, 0:LANES]).astype(BF16)
        dk_ref[start:stop, :] = dot_nn(grad_scores, q_both[:, 0:LANES]).astype(BF16)
    grad_q = dot_tn(k_ref[...], ds_ref[...]).T
    grad_q = jnp.where(first, grad_q[0:rows], grad_q[wide : wide + rows])
    if causal:
        dq_ref[...] = ((grad_q + before[...]) * 0.125).astype(BF16)
    else:
        dq_ref[...] = grad_q


def attend_back(queries, keys, values, key_const, aug, grad_out, out, begin, count, before=None):
    rows = queries.shape[0]
    far = keys.shape[0] - rows
    causal = before is not None
    span, block = (rows, far // rows) if causal else (far, 0)
    first = begin // LANES
    wide = padded(rows)
    pair = pl.BlockSpec((rows, LANES), lambda i: (0, first + i))
    keys_of = pl.BlockSpec((span, LANES), lambda i: (block, first + i))
    made = lambda height: pl.BlockSpec((height, LANES), lambda i: (0, i))
    return pl.pallas_call(
        functools.partial(attend_back_kernel, causal),
        grid=(count // LANES,),
        in_specs=[
            pair,
            keys_of,
            keys_of,
            pl.BlockSpec((span, LANES), lambda i: (block, 0)),
            pair,
            pair,
            pair,
        ]
        + [pair] * causal,
        out_specs=[made(rows), made(span), made(span)],
        out_shape=[
            jax.ShapeDtypeStruct((rows, count), BF16 if causal else F32),
            jax.ShapeDtypeStruct((span, count), BF16),
            jax.ShapeDtypeStruct((span, count), BF16),
        ],
        scratch_shapes=[
            pltpu.VMEM((2 * wide, 2 * LANES), BF16),
            pltpu.VMEM((2 * wide, 2 * LANES), BF16),
            pltpu.VMEM((span, 2 * wide), BF16),
        ],
        name="attend_back",
        compiler_params=pltpu.CompilerParams(vmem_limit_bytes=14 << 20),
        cost_estimate=LIGHT,
    )(queries, keys, values, key_const, aug, grad_out, out, *([before] if causal else []))


def chip_masks(dp):
    bits = dp.bit_length() - 2
    low = bits // 2
    along_x = [2 << i for i in range(low)]
    along_y = [2 << i for i in range(low, bits)]
    return along_x, along_y


def position(device, mask, dp):
    other = device ^ mask
    return (other & 1) * (dp // 2) + (other >> 1)


def own_slice(weight, by_rows, device, width):
    dp = lax.axis_size("dp")
    if by_rows:
        full = weight.shape[1]
        start = position(device, 0, dp) * (full // dp)
        piece = lax.dynamic_slice(weight, (start % width, start // width * width), (full // dp, width))
        return piece[None]
    rows = weight.shape[1] // dp
    return lax.dynamic_slice_in_dim(weight, position(device, 0, dp) * rows, rows, axis=1)


class Flow:
    def __init__(self, steps):
        self.steps = steps
        self.result = None
        self.over = False
        self.held = None
        self.move(None)

    def move(self, value):
        try:
            self.held = self.steps.send(value)
        except StopIteration as stop:
            self.result, self.over, self.held = stop.value, True, None


def ordered(flows, values):
    live = [flow for flow in flows if not flow.over]
    values, held = lax.optimization_barrier((values, [flow.held for flow in live]))
    for flow, item in zip(live, held):
        flow.move(item)
    return values


def begin(flows, *values):
    values = ordered(flows, values)
    return values if len(values) > 1 else values[0]


def meet(flows, *values):
    values = ordered(flows, values)
    return begin(flows, *values)


def layer_steps(value):
    mp = lax.axis_size("mp")
    got = {0: value}
    for count in range(1, mp.bit_length()):
        ranks = [r for r in range(mp) if r.bit_count() == count]
        sent = [got[r & (r - 1)] for r in ranks]
        if count > 1:
            sent = yield tuple(sent)
        found = yield tuple(swap(item, "mp", r & -r) for r, item in zip(ranks, sent))
        got.update(zip(ranks, found))
    return [got[r] for r in range(mp)]


def spread_steps(sides):
    along_x, along_y = chip_masks(lax.axis_size("dp"))
    orders = (along_x + along_y, along_y + along_x)
    masks = [[0], [0]]
    held = [side[None] for side in sides]
    arrays = []
    for step in range(len(along_x + along_y)):
        held = yield tuple(held)
        got = yield tuple(swap(value, "dp", order[step]) for value, order in zip(held, orders))
        for side, order in enumerate(orders):
            moved = [m ^ order[step] for m in masks[side]]
            if step + 1 < len(order):
                masks[side] = masks[side] + moved
            else:
                arrays += [(side, masks[side], held[side]), (side, moved, got[side])]
        held = [jnp.concatenate([one, two], axis=0) for one, two in zip(held, got)]
    own = yield tuple(value for _, _, value in arrays)
    other = yield tuple(swap(value, "dp", 1) for value in own)
    return [(side, m, value) for (side, m, _), value in zip(arrays, own)] + [
        (side, [k ^ 1 for k in m], value) for (side, m, _), value in zip(arrays, other)
    ]


def gather_flow(stacked, extra=None):
    count, rows, width = stacked.shape
    flat = stacked.reshape(count * rows, width)
    if extra is not None:
        flat = jnp.concatenate([flat, extra], axis=0)
    (flat,) = yield (flat,)
    found = yield from layer_steps(flat)
    across = jnp.stack([item[: count * rows].reshape(count, rows, width) for item in found[1:]])
    half = rows // 2
    arrays = yield from spread_steps((across[:, :, :half], across[:, :, half:]))
    return arrays, [item[count * rows :] for item in found]


class Weights:
    def __init__(self, own, arrays):
        self.own, self.arrays = own, arrays
        sample = arrays[0][2]
        self.full, self.width = sample.shape[3] * 2 * lax.axis_size("dp"), sample.shape[4]
        self.inputs = [shard for shard, _, _ in own] + [value for _, _, value in arrays]
        self.n_own = len(own)

    def specs(self):
        return [pl.BlockSpec(memory_space=pl.ANY)] * len(self.inputs)

    def scratch(self, mp, which):
        count = self.full // self.width + sum(len(m) for _, m, _ in self.arrays)
        return [
            pltpu.VMEM((mp, len(which), self.full, self.width), BF16),
            pltpu.SemaphoreType.DMA((count + 4,)),
        ]

    def copies(self, refs, held, sems, device, mp, dp, which):
        made = [[], []]
        spot = 0

        def add(r, source, target):
            nonlocal spot
            made[r].append((source, target, sems.at[spot]))
            spot += 1

        first, last = which[0], which[-1] + 1
        for ref, (_, index, by_rows) in zip(refs, self.own):
            if by_rows and first <= index < last:
                for block in range(self.full // self.width):
                    columns = pl.ds(block * self.width, self.width)
                    add(0, ref.at[:, columns], held.at[0, index - first, columns, :])
            elif not by_rows and first == index:
                add(0, ref, held.at[0, 0 : ref.shape[0]])
        half = self.full // dp // 2
        for ref, (side, masks, _) in zip(refs[self.n_own :], self.arrays):
            for index, mask in enumerate(masks):
                start = pl.multiple_of((position(device, mask, dp) * 2 + side) * half, half)
                add(
                    1,
                    ref.at[index, :, first:last],
                    held.at[1:, :, pl.ds(start, half), :],
                )
        return made


def start_all(copies):
    for copy in copies:
        pltpu.make_async_copy(*copy).start()


def wait_all(copies):
    for copy in copies:
        pltpu.make_async_copy(*copy).wait()


def wait_step(step, copies, begin=0):
    for r in range(begin, len(copies)):

        @pl.when(step == r)
        def _():
            wait_all(copies[r])


def tiles(count, size, body):
    if count == size:
        body(0)
    else:

        for i in range(count // size):
            body(i * size)


def row_tile(rows):
    return 272 if rows % 272 == 0 else 16


COLUMNS = 256


def column_tile(width):
    return min(COLUMNS, width)


def whole(shape):
    return pl.BlockSpec(shape, lambda i, *_: (0,) * len(shape))


def project_kernel(group, blocks, scale, scal, *refs):
    n_in = len(group.inputs)
    x_refs, bias_ref = refs[:blocks], refs[blocks]
    w_refs = refs[blocks + 1 : blocks + 1 + n_in]
    q_ref, k_ref, v_ref, held, sems = refs[blocks + 1 + n_in :]
    r = pl.program_id(0)
    mp, dp = lax.axis_size("mp"), lax.axis_size("dp")
    copies = group.copies(w_refs, held, sems, scal[0], mp, dp, [0, 1, 2])
    rows = q_ref.shape[0]

    @pl.when(r == 0)
    def _():
        start_all(sum(copies, []))

    wait_step(r, copies)

    size = column_tile(group.width)
    for begin in range(0, group.width, size):
        columns = slice(begin, begin + size)
        q = dot_nn(x_refs[-1][...], held[r, 0, :, columns]) + bias_ref[0:1, columns].astype(F32)
        q_ref[:, columns] = ((q * scale).astype(BF16) * RELAX_ALPHA).astype(BF16)
        for block in range(blocks):
            x = x_refs[block][...]
            place = slice(block * rows, (block + 1) * rows)
            k_ref[place, columns] = dot_nn(x, held[r, 1, :, columns]).astype(BF16)
            v = dot_nn(x, held[r, 2, :, columns]) + bias_ref[1:2, columns].astype(F32)
            v_ref[place, columns] = v.astype(BF16)


def project(normed, biases, group, device):
    mp = lax.axis_size("mp")
    rows, full = normed[0].shape
    blocks = len(normed)
    width = group.width
    made = lambda height: pl.BlockSpec((height, width), lambda i, *_: (0, i))
    return pl.pallas_call(
        functools.partial(project_kernel, group, blocks, 1.0 / math.sqrt(HEAD_DIM) / RELAX_ALPHA),
        grid_spec=pltpu.PrefetchScalarGridSpec(
            num_scalar_prefetch=1,
            grid=(mp,),
            in_specs=[whole((rows, full))] * blocks
            + [pl.BlockSpec((8, width), lambda i, *_: (0, i))]
            + group.specs(),
            out_specs=[made(rows), made(blocks * rows), made(blocks * rows)],
            scratch_shapes=group.scratch(mp, [0, 1, 2]),
        ),
        out_shape=[
            jax.ShapeDtypeStruct((rows, full), BF16),
            jax.ShapeDtypeStruct((blocks * rows, full), BF16),
            jax.ShapeDtypeStruct((blocks * rows, full), BF16),
        ],
        name="project",
        compiler_params=pltpu.CompilerParams(vmem_limit_bytes=22 << 20),
        cost_estimate=LIGHT,
    )(device.reshape(1), *normed, biases, *group.inputs)


def up_kernel(group_a, group_u, scal, *refs):
    (att_a, att_b, residual_ref, rows_ref, bias_ref), refs = refs[:5], refs[5:]
    wa, refs = refs[: len(group_a.inputs)], refs[len(group_a.inputs) :]
    wu, refs = refs[: len(group_u.inputs)], refs[len(group_u.inputs) :]
    branch_ref, middle_ref, mid_ref, act_ref, slope_ref, held_o, sem_o, held_u, sem_u = refs
    r = pl.program_id(0)
    mp, dp = lax.axis_size("mp"), lax.axis_size("dp")
    copies_o = sum(group_a.copies(wa, held_o, sem_o, scal[0], mp, dp, [3]), [])
    copies_u = group_u.copies(wu, held_u, sem_u, scal[0], mp, dp, [0])
    rows, full = middle_ref.shape
    width = group_a.width
    part = att_a.shape[1]

    @pl.when(r == 0)
    def _():
        start_all(copies_o)
        start_all(sum(copies_u, []))
        wait_all(copies_o)
        for block in range(full // width):
            columns = slice(block * width, (block + 1) * width)
            total = jnp.zeros((rows, width), F32)
            for layer in range(mp):
                source = att_a if layer * width < part else att_b
                first = layer * width % part
                total = total + dot_nn(source[:, first : first + width], held_o[layer, 0, columns, :])
            branch_ref[:, columns] = total + rows_ref[0:1, columns]

        def norm_rows(start):
            place = pl.ds(start, row_tile(rows))
            normal, _ = normalize(branch_ref[place, :])
            middle = residual_ref[place, :] + normal * rows_ref[1:2, :] + rows_ref[2:3, :]
            middle_ref[place, :] = middle
            normal, _ = normalize(middle)
            mid_ref[place, :] = (normal * rows_ref[3:4, :] + rows_ref[4:5, :]).astype(BF16)

        tiles(rows, row_tile(rows), norm_rows)

    wait_step(r, copies_u)

    size = column_tile(group_u.width)

    def activate(start):
        columns = pl.ds(start, size)
        u = dot_nn(mid_ref[...], held_u[r, 0, :, columns]) + bias_ref[0:1, columns]
        scale = math.sqrt(2.0 / math.pi)
        square = u * u
        bent = jnp.tanh(scale * u * (1.0 + 0.044715 * square))
        lifted = 0.5 + 0.5 * bent
        act_ref[:, columns] = (u * lifted).astype(BF16)
        slope = lifted + (0.5 * scale) * u * (1.0 - bent * bent) * (
            1.0 + (3.0 * 0.044715) * square
        )
        slope_ref[:, columns] = slope.astype(BF16)

    tiles(group_u.width, size, activate)


def feed_up(att_a, att_b, residual, vectors, u_bias, group_a, group_u, device):
    mp = lax.axis_size("mp")
    rows, full = residual.shape
    hidden = group_u.width
    made = pl.BlockSpec((rows, hidden), lambda i, *_: (0, i))
    return pl.pallas_call(
        functools.partial(up_kernel, group_a, group_u),
        grid_spec=pltpu.PrefetchScalarGridSpec(
            num_scalar_prefetch=1,
            grid=(mp,),
            in_specs=[whole(att_a.shape), whole(att_b.shape), whole((rows, full)), whole((8, full))]
            + [pl.BlockSpec((8, hidden), lambda i, *_: (0, i))]
            + group_a.specs()
            + group_u.specs(),
            out_specs=[whole((rows, full)), whole((rows, full)), whole((rows, full)), made, made],
            scratch_shapes=group_a.scratch(mp, [3]) + group_u.scratch(mp, [0]),
        ),
        out_shape=[
            jax.ShapeDtypeStruct((rows, full), F32),
            jax.ShapeDtypeStruct((rows, full), F32),
            jax.ShapeDtypeStruct((rows, full), BF16),
            jax.ShapeDtypeStruct((rows, mp * hidden), BF16),
            jax.ShapeDtypeStruct((rows, mp * hidden), BF16),
        ],
        name="feed_up",
        compiler_params=pltpu.CompilerParams(vmem_limit_bytes=38 << 20),
        cost_estimate=LIGHT,
    )(
        device.reshape(1), att_a, att_b, residual, vectors, u_bias, *group_a.inputs, *group_u.inputs
    )


def down_kernel(group_d, scal, *refs):
    (act_ref, middle_ref, cot_ref, rows_ref), refs = refs[:4], refs[4:]
    wd, refs = refs[: len(group_d.inputs)], refs[len(group_d.inputs) :]
    out_ref, grad_ref, sums_ref, held, sems, total = refs
    r = pl.program_id(0)
    mp, dp = lax.axis_size("mp"), lax.axis_size("dp")
    copies = group_d.copies(wd, held, sems, scal[0], mp, dp, [0])
    rows, full = middle_ref.shape
    width = group_d.width

    @pl.when(r == 0)
    def _():
        start_all(sum(copies, []))
        total[...] = jnp.zeros_like(total)

    wait_step(r, copies)

    size = column_tile(width)
    for block in range(full // width):

        def add(start):
            columns = pl.ds(block * width + start, size)
            total[:, columns] += dot_nn(
                act_ref[...], held[r, 0, block * width : (block + 1) * width, pl.ds(start, size)]
            )

        tiles(width, size, add)

    @pl.when(r == mp - 1)
    def _():
        sums_ref[...] = jnp.zeros_like(sums_ref)

        def norm_rows(start):
            place = pl.ds(start, row_tile(rows))
            normal, factor = normalize(total[place, :] + rows_ref[0:1, :])
            gain = rows_ref[1:2, :]
            out_ref[place, :] = (
                middle_ref[place, :] + (normal * gain + rows_ref[2:3, :])
            ).astype(BF16)
            upstream = cot_ref[place, :].astype(F32)
            scaled = upstream * gain
            grad = (
                scaled
                - jnp.mean(scaled, axis=-1, keepdims=True)
                - normal * jnp.mean(scaled * normal, axis=-1, keepdims=True)
            ) * factor
            grad = grad.astype(BF16)
            grad_ref[place, :] = grad
            sums_ref[0:8, :] += fold(upstream * normal)
            sums_ref[8:16, :] += fold(upstream)
            sums_ref[16:24, :] += fold(grad.astype(F32))

        tiles(rows, row_tile(rows), norm_rows)


def fold(value):
    return functools.reduce(jnp.add, [value[i : i + 8] for i in range(0, value.shape[0], 8)])


def feed_down(act, middle, cotangent, vectors, group_d, device):
    mp = lax.axis_size("mp")
    rows, full = middle.shape
    hidden = group_d.width
    return pl.pallas_call(
        functools.partial(down_kernel, group_d),
        grid_spec=pltpu.PrefetchScalarGridSpec(
            num_scalar_prefetch=1,
            grid=(mp,),
            in_specs=[pl.BlockSpec((rows, hidden), lambda i, *_: (0, i))]
            + [whole((rows, full)), whole((rows, full)), whole((8, full))]
            + group_d.specs(),
            out_specs=[whole((rows, full)), whole((rows, full)), whole((24, full))],
            scratch_shapes=group_d.scratch(mp, [0]) + [pltpu.VMEM((rows, full), F32)],
        ),
        out_shape=[
            jax.ShapeDtypeStruct((rows, full), BF16),
            jax.ShapeDtypeStruct((rows, full), BF16),
            jax.ShapeDtypeStruct((24, full), F32),
        ],
        name="feed_down",
        compiler_params=pltpu.CompilerParams(vmem_limit_bytes=26 << 20),
        cost_estimate=LIGHT,
    )(device.reshape(1), act, middle, cotangent, vectors, *group_d.inputs)


def back_kernel(group_a, group_u, group_d, scal, *refs):
    (grad_ref, slope_ref, branch_ref, middle_ref, cot_ref, rows_ref), refs = refs[:6], refs[6:]
    wa, refs = refs[: len(group_a.inputs)], refs[len(group_a.inputs) :]
    wu, refs = refs[: len(group_u.inputs)], refs[len(group_u.inputs) :]
    wd, refs = refs[: len(group_d.inputs)], refs[len(group_d.inputs) :]
    (pre_ref, mid_ref, low_ref, att_ref, sums_ref, u_sum_ref), refs = refs[:6], refs[6:]
    held_o, sem_o, held_u, sem_u, held_d, sem_d, total = refs
    r = pl.program_id(0)
    mp, dp = lax.axis_size("mp"), lax.axis_size("dp")
    copies_o = sum(group_a.copies(wa, held_o, sem_o, scal[0], mp, dp, [3]), [])
    copies_u = group_u.copies(wu, held_u, sem_u, scal[0], mp, dp, [0])
    copies_d = group_d.copies(wd, held_d, sem_d, scal[0], mp, dp, [0])
    copies = [one + two for one, two in zip(copies_d, copies_u)]
    rows, full = middle_ref.shape
    hidden = group_d.width
    size = column_tile(hidden)

    @pl.when(r == 0)
    def _():
        start_all(sum(copies, []) + copies_o)
        total[...] = jnp.zeros_like(total)

    wait_step(r, copies)

    def slopes(start):
        columns = pl.ds(start, size)
        grad = jnp.zeros((rows, size), F32)
        for block in range(full // hidden):
            grad = grad + dot_nt(
                grad_ref[:, block * hidden : (block + 1) * hidden],
                held_d[r, 0, pl.ds(block * hidden + start, size), :],
            )
        pre = (grad * slope_ref[:, columns].astype(F32)).astype(BF16)
        pre_ref[:, columns] = pre
        u_sum_ref[:, columns] = fold(pre.astype(F32))

    tiles(hidden, size, slopes)
    wide = column_tile(full)

    def add(start):
        columns = pl.ds(start, wide)
        total[:, columns] += dot_nt(pre_ref[...], held_u[r, 0, columns, :])

    tiles(full, wide, add)

    @pl.when(r == mp - 1)
    def _():
        sums_ref[...] = jnp.zeros_like(sums_ref)

        def norm_rows(start):
            place = pl.ds(start, row_tile(rows))

            def backward(upstream, inputs, gain):
                normal, factor = normalize(inputs)
                scaled = upstream * gain
                grad = (
                    scaled
                    - jnp.mean(scaled, axis=-1, keepdims=True)
                    - normal * jnp.mean(scaled * normal, axis=-1, keepdims=True)
                ) * factor
                return grad, fold(upstream * normal), fold(upstream)

            grad_mid, gain_sum, shift_sum = backward(
                total[place, :], middle_ref[place, :], rows_ref[0:1, :]
            )
            sums_ref[0:8, :] += gain_sum
            sums_ref[8:16, :] += shift_sum
            grad_middle = cot_ref[place, :].astype(F32) + grad_mid
            mid_ref[place, :] = grad_middle
            grad_branch, gain_sum, shift_sum = backward(
                grad_middle, branch_ref[place, :], rows_ref[1:2, :]
            )
            sums_ref[16:24, :] += gain_sum
            sums_ref[24:32, :] += shift_sum
            low = grad_branch.astype(BF16)
            low_ref[place, :] = low
            sums_ref[32:40, :] += fold(low.astype(F32))

        tiles(rows, row_tile(rows), norm_rows)
        wait_all(copies_o)
        width = group_a.width
        for layer in range(mp):
            grad = jnp.zeros((rows, width), F32)
            for block in range(full // width):
                columns = slice(block * width, (block + 1) * width)
                grad = grad + dot_nt(low_ref[:, columns], held_o[layer, 0, columns, :])
            att_ref[:, layer * width : (layer + 1) * width] = grad.astype(BF16)


def feed_back(grad, slope, branch, middle, cotangent, vectors, group_a, group_u, group_d, device):
    mp = lax.axis_size("mp")
    rows, full = middle.shape
    hidden = group_d.width
    step = pl.BlockSpec((rows, hidden), lambda i, *_: (0, i))
    return pl.pallas_call(
        functools.partial(back_kernel, group_a, group_u, group_d),
        grid_spec=pltpu.PrefetchScalarGridSpec(
            num_scalar_prefetch=1,
            grid=(mp,),
            in_specs=[whole((rows, full)), step]
            + [whole((rows, full))] * 3
            + [whole((8, full))]
            + group_a.specs()
            + group_u.specs()
            + group_d.specs(),
            out_specs=[step]
            + [whole((rows, full))] * 3
            + [whole((40, full)), pl.BlockSpec((8, hidden), lambda i, *_: (0, i))],
            scratch_shapes=group_a.scratch(mp, [3])
            + group_u.scratch(mp, [0])
            + group_d.scratch(mp, [0])
            + [pltpu.VMEM((rows, full), F32)],
        ),
        out_shape=[
            jax.ShapeDtypeStruct((rows, mp * hidden), BF16),
            jax.ShapeDtypeStruct((rows, full), F32),
            jax.ShapeDtypeStruct((rows, full), BF16),
            jax.ShapeDtypeStruct((rows, full), BF16),
            jax.ShapeDtypeStruct((40, full), F32),
            jax.ShapeDtypeStruct((8, mp * hidden), F32),
        ],
        name="feed_back",
        compiler_params=pltpu.CompilerParams(vmem_limit_bytes=46 << 20),
        cost_estimate=LIGHT,
    )(
        device.reshape(1),
        grad,
        slope,
        branch,
        middle,
        cotangent,
        vectors,
        *group_a.inputs,
        *group_u.inputs,
        *group_d.inputs,
    )


def unproject_kernel(group, which, begin, steps, added, scal, *refs):
    grads, refs = refs[: len(which)], refs[len(which) :]
    before, refs = (refs[0], refs[1:]) if added else (None, refs)
    w_refs, refs = refs[: len(group.inputs)], refs[len(group.inputs) :]
    out_ref, held, sems, total = refs
    step = pl.program_id(0)
    mp, dp = lax.axis_size("mp"), lax.axis_size("dp")
    copies = group.copies(w_refs, held, sems, scal[0], mp, dp, [0, 1, 2])
    if begin:
        copies = copies[1:]
    elif steps == 1:
        copies = copies[:1]
    full = out_ref.shape[1]

    @pl.when(step == 0)
    def _():
        start_all(sum(copies, []))
        total[...] = before[...] if added else jnp.zeros_like(total)

    wait_step(step, copies)
    r = begin + step
    size = column_tile(full)

    def add(start):
        columns = pl.ds(start, size)
        total[:, columns] += functools.reduce(
            jnp.add,
            [dot_nt(g[...], held[r, index, columns, :]) for index, g in zip(which, grads)],
        )

    tiles(full, size, add)

    @pl.when(step == pl.num_programs(0) - 1)
    def _():
        out_ref[...] = total[...].astype(out_ref.dtype)


def unproject(grads, which, group, begin, before, dtype, device):
    mp = lax.axis_size("mp")
    rows, count = grads[0].shape
    full, width = group.full, group.width
    return pl.pallas_call(
        functools.partial(
            unproject_kernel, group, which, begin, count // width, before is not None
        ),
        grid_spec=pltpu.PrefetchScalarGridSpec(
            num_scalar_prefetch=1,
            grid=(count // width,),
            in_specs=[pl.BlockSpec((rows, width), lambda i, *_: (0, i))] * len(grads)
            + ([] if before is None else [whole((rows, full))])
            + group.specs(),
            out_specs=whole((rows, full)),
            scratch_shapes=group.scratch(mp, [0, 1, 2]) + [pltpu.VMEM((rows, full), F32)],
        ),
        out_shape=jax.ShapeDtypeStruct((rows, full), dtype),
        name="unproject",
        compiler_params=pltpu.CompilerParams(vmem_limit_bytes=16 << 20),
        cost_estimate=LIGHT,
    )(device.reshape(1), *grads, *([] if before is None else [before]), *group.inputs)


def other_half_kernel(scal, left_ref, right_ref, out_ref):
    out_ref[...] = dot_tn(left_ref[...], right_ref[...]).astype(BF16)


def split_rows(total, bit_at, bit, outs):
    send_ref, keep_ref = outs
    count, rows, _ = send_ref.shape
    for j in range(count):
        base = ((j >> bit_at) << (bit_at + 1)) | (j & ((1 << bit_at) - 1))
        for ref, value in ((send_ref, 1 - bit), (keep_ref, bit)):
            start = pl.multiple_of((base + (value << bit_at)) * rows, rows)
            ref[j] = total[pl.ds(start, rows), :].astype(BF16)


def this_half_kernel(bits_at, scal, left_ref, right_ref, got_ref, *refs):
    outs, total = refs[:-1], refs[-1]
    total[...] = dot_tn(left_ref[...], right_ref[...]) + got_ref[...].astype(F32)
    step = pl.program_id(0)
    count = pl.num_programs(0) // 2
    for side in range(2):

        @pl.when(step // count == side)
        def _():
            split_rows(
                total,
                bits_at[side],
                (scal[0] >> (bits_at[side] + 1)) & 1,
                outs[2 * side : 2 * side + 2],
            )


def first_bits():
    along_x, along_y = chip_masks(lax.axis_size("dp"))
    return [order[0].bit_length() - 2 for order in (along_x + along_y, along_y + along_x)]


def other_half(left, right, device):
    rows, full = left.shape
    size = right.shape[1] // lax.axis_size("mp")
    return pl.pallas_call(
        other_half_kernel,
        grid_spec=pltpu.PrefetchScalarGridSpec(
            num_scalar_prefetch=1,
            grid=(right.shape[1] // size,),
            in_specs=[
                pl.BlockSpec((rows, full // 2), lambda i, scal: (0, 1 - scal[0] % 2)),
                pl.BlockSpec((rows, size), lambda i, scal: (0, i)),
            ],
            out_specs=pl.BlockSpec((full // 2, size), lambda i, scal: (0, i)),
        ),
        out_shape=jax.ShapeDtypeStruct((full // 2, right.shape[1]), BF16),
        name="other_half",
        compiler_params=pltpu.CompilerParams(vmem_limit_bytes=12 << 20),
        cost_estimate=LIGHT,
    )(device.reshape(1), left, right)


def this_half(left, right, got, device):
    rows, full = left.shape
    mp = lax.axis_size("mp")
    size = right.shape[1] // mp
    quarters = lax.axis_size("dp") // 2
    shape = (quarters // 2, full // 2 // quarters, mp // 2 * size)
    block = (quarters // 2, full // 2 // quarters, size)
    last = mp // 2 - 1
    sides = [lambda i, scal: (0, 0, jnp.minimum(i, last))] * 2 + [
        lambda i, scal: (0, 0, jnp.maximum(i - last - 1, 0))
    ] * 2
    return pl.pallas_call(
        functools.partial(this_half_kernel, first_bits()),
        grid_spec=pltpu.PrefetchScalarGridSpec(
            num_scalar_prefetch=1,
            grid=(mp,),
            in_specs=[
                pl.BlockSpec((rows, full // 2), lambda i, scal: (0, scal[0] % 2)),
                pl.BlockSpec((rows, size), lambda i, scal: (0, i)),
                pl.BlockSpec((full // 2, size), lambda i, scal: (0, i)),
            ],
            out_specs=[pl.BlockSpec(block, index) for index in sides],
            scratch_shapes=[pltpu.VMEM((full // 2, size), F32)],
        ),
        out_shape=[jax.ShapeDtypeStruct(shape, BF16)] * 4,
        name="this_half",
        compiler_params=pltpu.CompilerParams(vmem_limit_bytes=18 << 20),
        cost_estimate=LIGHT,
    )(device.reshape(1), left, right, got)


def attention_dots(width, lefts, branch, grads, attended, layer, put):
    grad_q, near_k, near_v, far_k, far_v = grads
    rows = grad_q.shape[0]
    columns = slice(layer * width, (layer + 1) * width)
    put(0, dot_tn(lefts[-1][...], grad_q[:, columns]))
    for index, near, far in ((1, near_k, far_k), (2, near_v, far_v)):
        total = dot_tn(lefts[-1][...], near[:, columns])
        for block in range(len(lefts) - 1):
            total = total + dot_tn(lefts[block][...], far[block * rows : (block + 1) * rows, columns])
        put(index, total)
    put(3, dot_tn(branch[...], attended[:, columns]))


def attention_other_kernel(width, blocks, scal, *refs):
    lefts, (branch, *grads, attended, out_ref) = refs[:blocks], refs[blocks:]
    for layer in range(attended.shape[1] // width):

        def put(index, value):
            place = (layer * 4 + index) * width
            out_ref[:, place : place + width] = value.astype(BF16)

        attention_dots(width, lefts, branch, grads, attended, layer, put)


def attention_this_kernel(width, blocks, bits_at, scal, *refs):
    lefts, (branch, *grads, attended, got_ref) = refs[:blocks], refs[blocks : blocks + 8]
    outs, total = refs[blocks + 8 : -1], refs[-1]
    layers = attended.shape[1] // width
    for side in range(2):
        for local in range(layers // 2):
            layer = side * (layers // 2) + local

            def put(index, value):
                place = (layer * 4 + index) * width
                total[:, index * width : (index + 1) * width] = value + got_ref[
                    :, place : place + width
                ].astype(F32)

            attention_dots(width, lefts, branch, grads, attended, layer, put)
            columns = pl.ds(local * 4 * width, 4 * width)
            split_rows(
                total,
                bits_at[side],
                (scal[0] >> (bits_at[side] + 1)) & 1,
                [ref.at[:, :, columns] for ref in outs[2 * side : 2 * side + 2]],
            )


def attention_specs(normed, branch, grads, part, core_of):
    rows, full = branch.shape
    left = pl.BlockSpec((rows, full // 2), lambda i, scal: (0, core_of(scal)))
    wide = grads[0].shape[1]
    some = lambda height: pl.BlockSpec((height, wide), lambda i, scal: (0, part))
    return (
        [left] * (len(normed) + 1)
        + [whole(g.shape) for g in grads[:3]]
        + [some(g.shape[0]) for g in grads[3:]]
        + [some(rows)]
    )


def attention_other(normed, branch, grads, attended, part, width, device):
    full = branch.shape[1]
    out = (full // 2, 4 * grads[0].shape[1])
    return pl.pallas_call(
        functools.partial(attention_other_kernel, width, len(normed)),
        grid_spec=pltpu.PrefetchScalarGridSpec(
            num_scalar_prefetch=1,
            grid=(1,),
            in_specs=attention_specs(normed, branch, grads, part, lambda s: 1 - s[0] % 2),
            out_specs=whole(out),
        ),
        out_shape=jax.ShapeDtypeStruct(out, BF16),
        name="attention_other",
        compiler_params=pltpu.CompilerParams(vmem_limit_bytes=12 << 20),
        cost_estimate=LIGHT,
    )(device.reshape(1), *normed, branch, *grads, attended)


def attention_this(normed, branch, grads, attended, got, part, width, device):
    full = branch.shape[1]
    quarters = lax.axis_size("dp") // 2
    shape = (quarters // 2, full // 2 // quarters, 2 * grads[0].shape[1])
    return pl.pallas_call(
        functools.partial(attention_this_kernel, width, len(normed), first_bits()),
        grid_spec=pltpu.PrefetchScalarGridSpec(
            num_scalar_prefetch=1,
            grid=(1,),
            in_specs=attention_specs(normed, branch, grads, part, lambda s: s[0] % 2)
            + [whole(got.shape)],
            out_specs=[whole(shape)] * 4,
            scratch_shapes=[pltpu.VMEM((full // 2, 4 * width), F32)],
        ),
        out_shape=[jax.ShapeDtypeStruct(shape, BF16)] * 4,
        name="attention_this",
        compiler_params=pltpu.CompilerParams(vmem_limit_bytes=14 << 20),
        cost_estimate=LIGHT,
    )(device.reshape(1), *normed, branch, *grads, attended, got)


def next_stage_kernel(scal, *refs):
    ins, outs = refs[:8], refs[8:]
    for index, out in enumerate(outs):
        one, two = ins[2 * index], ins[2 * index + 1]
        out[...] = (one[0].astype(F32) + two[0].astype(F32)).astype(BF16)


def next_stage(keeps, gots, bits, device):
    _, rows, columns = keeps[0].shape
    specs, inputs = [], []
    for side in range(2):
        for flip in (1, 0):
            where = lambda i, scal, side=side, flip=flip: (
                ((scal[0] >> (bits[side] + 1)) & 1) ^ flip,
                0,
                0,
            )
            specs += [pl.BlockSpec((1, rows, columns), where)] * 2
            inputs += [keeps[side], gots[side]]
    return pl.pallas_call(
        next_stage_kernel,
        grid_spec=pltpu.PrefetchScalarGridSpec(
            num_scalar_prefetch=1,
            grid=(1,),
            in_specs=specs,
            out_specs=[whole((rows, columns))] * 4,
        ),
        out_shape=[jax.ShapeDtypeStruct((rows, columns), BF16)] * 4,
        name="next_stage",
        compiler_params=pltpu.CompilerParams(vmem_limit_bytes=10 << 20),
        cost_estimate=LIGHT,
    )(device.reshape(1), *inputs)


def by_layer_kernel(places, keep_a, got_a, keep_b, got_b, send_ref, rest_ref):
    width = send_ref.shape[2]
    each = len(places) // 2
    for index, (sent, spot) in enumerate(places):
        keep, got = ((keep_a, got_a), (keep_b, got_b))[index // each]
        columns = slice(index % each * width, (index % each + 1) * width)
        value = keep[:, columns].astype(F32) + got[:, columns].astype(F32)
        if sent:
            send_ref[spot] = value.astype(BF16)
        else:
            rest_ref[spot] = value


def by_layer_pieces(keeps, gots, layers):
    rows = keeps[0].shape[0]
    width = keeps[0].shape[1] * 2 // len(layers)
    odd = [r for r in layers if r & 1]
    even = [r for r in layers if not r & 1]
    places = [(r & 1, (odd if r & 1 else even).index(r)) for r in layers]
    send, rest = pl.pallas_call(
        functools.partial(by_layer_kernel, places),
        out_shape=[
            jax.ShapeDtypeStruct((len(odd), rows, width), BF16),
            jax.ShapeDtypeStruct((len(even), rows, width), F32),
        ],
        in_specs=[pl.BlockSpec(memory_space=pltpu.VMEM)] * 4,
        out_specs=[pl.BlockSpec(memory_space=pltpu.VMEM)] * 2,
        name="by_layer_pieces",
        compiler_params=pltpu.CompilerParams(vmem_limit_bytes=8 << 20),
        cost_estimate=LIGHT,
    )(keeps[0], gots[0], keeps[1], gots[1])
    return send, rest, odd, even


def reduce_flow(send, add, layers, device):
    (send,) = yield (send,)
    (got,) = yield (swap(send, "dp", 1),)
    send_a, keep_a, send_b, keep_b = add(got)
    along_x, along_y = chip_masks(lax.axis_size("dp"))
    orders = (along_x + along_y, along_y + along_x)
    bits = len(orders[0])
    sends, keeps = [send_a, send_b], [keep_a, keep_b]
    lefts = []
    for side, order in enumerate(orders):
        left = list(range(bits - 1, -1, -1))
        left.remove(order[0].bit_length() - 2)
        lefts.append(left)
        keeps[side] = keeps[side].reshape((2,) * (bits - 1) + keeps[side].shape[1:])
    for step in range(bits):
        sends = yield tuple(sends)
        gots = yield tuple(swap(value, "dp", order[step]) for value, order in zip(sends, orders))
        gots = [got.reshape(keep.shape) for got, keep in zip(gots, keeps)]
        if step + 1 == bits:
            break
        picks = [order[step + 1].bit_length() - 2 for order in orders]
        if keeps[0].ndim == 3:
            send_a, keep_a, send_b, keep_b = next_stage(keeps, gots, picks, device)
            sends, keeps = [send_a, send_b], [keep_a, keep_b]
            continue
        sends, next_keeps = [], []
        for side, which in enumerate(picks):
            axis = lefts[side].index(which)
            lefts[side].remove(which)
            bit = (device >> (which + 1)) & 1

            def part(value):
                summed = [
                    lax.dynamic_index_in_dim(item, value, axis, keepdims=False).astype(F32)
                    for item in (keeps[side], gots[side])
                ]
                return (summed[0] + summed[1]).astype(BF16)

            sends.append(part(1 - bit))
            next_keeps.append(part(bit))
        keeps = next_keeps
    send, rest, odd, even = by_layer_pieces(keeps, gots, layers)
    (send,) = yield (send,)
    (got,) = yield (swap(send, "mp", 1),)
    held = {r: rest[i] for i, r in enumerate(even)}
    for i, r in enumerate(odd):
        value = got[i].astype(F32)
        held[r ^ 1] = held[r ^ 1] + value if r ^ 1 in held else value
    for bit in range(1, lax.axis_size("mp").bit_length() - 1):
        mask = 1 << bit
        away = [r for r in sorted(held) if r & mask]
        if away:
            send = held[away[0]] if len(away) == 1 else jnp.stack([held[r] for r in away])
            (send,) = yield (send.astype(BF16),)
            (got,) = yield (swap(send, "mp", mask),)
            got = [got] if len(away) == 1 else list(got)
            for r, value in zip(away, got):
                del held[r]
                value = value.astype(F32)
                held[r ^ mask] = held[r ^ mask] + value if r ^ mask in held else value
    return held[0]


def fill_kernel(plan, rows, dp, scal, *refs):
    ins, (qkv_ref, out_ref, turned) = refs[:-3], refs[-3:]
    width = turned.shape[1]
    for ref, (side, masks) in zip(ins, plan):
        for index, mask in enumerate(masks):
            place = pl.ds(pl.multiple_of(position(scal[0], mask, dp) * rows, rows), rows)
            for inner in range(2):
                value = ref[index, :, inner * width : (inner + 1) * width].astype(F32)
                if side * 2 + inner < 3:
                    qkv_ref[side * 2 + inner, place, :] = value
                else:
                    turned[place, :] = value
    out_ref[...] = turned[...].T


def fill_attention(arrays, full, width, device):
    dp = lax.axis_size("dp")
    inputs = [value for _, _, value in arrays]
    vmem = pl.BlockSpec(memory_space=pltpu.VMEM)
    return pl.pallas_call(
        functools.partial(fill_kernel, [(side, m) for side, m, _ in arrays], full // dp, dp),
        grid_spec=pltpu.PrefetchScalarGridSpec(
            num_scalar_prefetch=1,
            grid=(),
            in_specs=[vmem] * len(inputs),
            out_specs=[vmem, vmem],
            scratch_shapes=[pltpu.VMEM((full, width), F32)],
        ),
        out_shape=[
            jax.ShapeDtypeStruct((3, full, width), F32),
            jax.ShapeDtypeStruct((width, full), F32),
        ],
        name="fill_attention",
        compiler_params=pltpu.CompilerParams(vmem_limit_bytes=32 << 20),
        cost_estimate=LIGHT,
    )(device.reshape(1), *inputs)


def fill_ffn_kernel(turn, in_ref, out_ref):
    group, _, rows, hidden = in_ref.shape
    value = in_ref[...].astype(F32).reshape(group * rows, hidden)
    out_ref[...] = value.T if turn else value


def fill_ffn(gathered, turn):
    dp, rows, hidden = gathered.shape
    quarters = dp // 2
    group = quarters
    count = quarters // group
    full = dp * rows
    block = (hidden, group * rows) if turn else (group * rows, hidden)
    shape = (hidden, full) if turn else (full, hidden)
    where = (lambda c, j: (0, c * count + j)) if turn else (lambda c, j: (c * count + j, 0))
    return pl.pallas_call(
        functools.partial(fill_ffn_kernel, turn),
        grid=(2, count),
        in_specs=[pl.BlockSpec((group, 1, rows, hidden), lambda c, j: (j, c, 0, 0))],
        out_specs=pl.BlockSpec(block, where),
        out_shape=jax.ShapeDtypeStruct(shape, F32),
        name="fill_ffn",
        compiler_params=pltpu.CompilerParams(vmem_limit_bytes=24 << 20),
        cost_estimate=LIGHT,
    )(gathered.reshape(quarters, 2, rows, hidden))


def small_flow(value):
    for axis in ("dp", "mp"):
        for bit in range(lax.axis_size(axis).bit_length() - 1):
            (value,) = yield (value,)
            (got,) = yield (swap(value, axis, 1 << bit),)
            value = value + got
    return value


def spread_flow(sides):
    return (yield from spread_steps(sides))


def finish(flows, *values):
    while any(not flow.over for flow in flows):
        out = meet(flows, *values)
        values = out if len(values) > 1 else (out,)
    return values


def drain(*flows):
    for flow in flows:
        while not flow.over:
            flow.move(flow.held)


def eight_rows(*rows):
    stacked = jnp.stack([row.astype(F32) for row in rows])
    return jnp.pad(stacked, ((0, 8 - stacked.shape[0]), (0, 0)))


def on_device(
    tokens,
    groups,
    lengths,
    qkv_weight,
    qv_bias,
    out_weight,
    out_bias,
    up_weight,
    up_bias,
    down_weight,
    down_bias,
    norm_gain,
    norm_bias,
    group_table,
    cotangent,
):
    dp, mp = lax.axis_size("dp"), lax.axis_size("mp")
    device, layer = lax.axis_index("dp"), lax.axis_index("mp")
    core = device & 1
    rows, full = tokens.shape
    width = qkv_weight.shape[2]
    hidden = up_weight.shape[1]
    blocks = SEQ_LEN // rows
    place_in_seq = layer % blocks
    length = lax.dynamic_index_in_dim(lengths, layer // blocks, keepdims=False)
    along_x, along_y = chip_masks(dp)
    stages = len(along_x + along_y)
    gains = norm_gain.astype(F32)
    shifts = norm_bias.astype(F32)
    part, half = full // 2, full // 2

    shard_a = [(qkv_weight, 0, False), (out_weight, 3, True)]
    shard_u, shard_d = [(up_weight[None], 0, False)], [(down_weight, 0, True)]
    small_here = jnp.concatenate([qv_bias[0], qv_bias[1], up_bias]).reshape(-1, width)
    n_small = small_here.shape[0]
    small_here = jnp.pad(small_here, ((0, -n_small % 16), (0, 0)))
    slice_a = jnp.concatenate(
        [
            own_slice(qkv_weight, False, device, width),
            own_slice(out_weight, True, device, width),
        ]
    )
    flow_a = Flow(gather_flow(slice_a, small_here))
    tokens = begin([flow_a], tokens)

    order_of = layer ^ jnp.arange(mp)
    onehot = (
        groups[:, None] == lax.broadcasted_iota(jnp.int32, (1, group_table.shape[0]), 1)
    ).astype(BF16)
    residual = tokens.astype(F32) + jnp.dot(onehot, group_table, preferred_element_type=F32)
    normed, norm_one, inv_one = norm_forward(residual, gains[0], shifts[0])
    normed_low = normed.astype(BF16)

    def rows_flow(value):
        (value,) = yield (value,)
        return (yield tuple(swap(value, "mp", m) for m in range(1, blocks)))

    key_ids = lax.broadcasted_iota(jnp.int32, (blocks, rows, 1), 1)
    block_ids = lax.broadcasted_iota(jnp.int32, (blocks, rows, 1), 0)
    block_ids = place_in_seq ^ ((block_ids + 1) % blocks)
    shown = (block_ids <= place_in_seq) & (block_ids * rows + key_ids < length)
    spot = lax.broadcasted_iota(jnp.int32, (blocks, rows, LANES), 2) % HEAD_DIM
    key_const = jnp.where(
        spot == 0,
        jnp.where(shown, 0.0, MASKED_SCORE),
        jnp.where(spot <= 3, 1.0, 0.0),
    )
    key_const = key_const.astype(BF16).reshape(blocks * rows, LANES)

    slice_u = own_slice(up_weight[None], False, device, hidden)
    slice_d = own_slice(down_weight, True, device, hidden)
    flow_r = Flow(rows_flow(normed_low))
    normed_low, slice_u, slice_d = meet([flow_a], normed_low, slice_u, slice_d)
    flow_u, flow_d = Flow(gather_flow(slice_u)), Flow(gather_flow(slice_d))
    layer_stages = mp.bit_length() - 1
    for _ in range(layer_stages - 1):
        normed_low = meet([flow_a], normed_low)
    normed_low = begin([flow_r, flow_u], normed_low)
    for _ in range(stages - 1):
        normed_low = meet([flow_a], normed_low)
    normed_low = meet([flow_a, flow_u, flow_r], normed_low)
    for _ in range(layer_stages - 2):
        normed_low = meet([flow_u], normed_low)
    normed_low = meet([flow_a, flow_u], normed_low)
    normed_low = begin([flow_d], normed_low)
    arrays_a, small_all = flow_a.result
    group_a = Weights(shard_a, arrays_a)
    small_all = jnp.stack(small_all)[:, :n_small].reshape(mp, -1).astype(F32)
    qv_rows = small_all[:, : 2 * width].reshape(mp, 2, width).transpose(1, 0, 2).reshape(2, full)
    u_rows = small_all[:, 2 * width :].reshape(1, -1)
    qv_rows = jnp.pad(qv_rows, ((0, 6), (0, 0)))
    u_rows = jnp.pad(u_rows, ((0, 7), (0, 0)))
    seq_normed = tuple(flow_r.result) + (normed_low,)
    queries, keys, values = project(seq_normed, qv_rows, group_a, device)
    queries, keys, values = meet([flow_d, flow_u], queries, keys, values)
    attended_a, aug_a = attend(queries, keys, values, key_const, 0, part)
    for _ in range(layer_stages - 1):
        attended_a, queries = meet([flow_d], attended_a, queries)
    attended_b, aug_b = attend(queries, keys, values, key_const, part, part)
    attended = jnp.concatenate([attended_a, attended_b], axis=1)
    aug = jnp.concatenate([aug_a, aug_b], axis=1)
    attended_b = meet([flow_u, flow_d], attended_b)
    for _ in range(stages - 2):
        attended_b = meet([flow_d], attended_b)
    (attended_b,) = finish([flow_u], attended_b)
    group_u = Weights(shard_u, flow_u.result[0])
    branch, middle, mid_low, act, slope = feed_up(
        attended_a,
        attended_b,
        residual,
        eight_rows(out_bias, gains[1], shifts[1], gains[2], shifts[2]),
        u_rows,
        group_a,
        group_u,
        device,
    )
    (act,) = finish([flow_d], act)
    group_d = Weights(shard_d, flow_d.result[0])
    output, grad_ffn, sums_ffn = feed_down(
        act, middle, cotangent, eight_rows(down_bias, gains[3], shifts[3]), group_d, device
    )

    everyone = list(range(mp))

    def weight_flow(left, right):
        return Flow(
            reduce_flow(
                other_half(left, right, device),
                lambda got: this_half(left, right, got, device),
                everyone,
                device,
            )
        )

    flow_d = weight_flow(grad_ffn, act)
    grad_ffn = begin([flow_d], grad_ffn)
    grad_ffn = meet([flow_d], grad_ffn)
    grad_pre, grad_middle, grad_branch, grad_attended, sums_back, sums_up = feed_back(
        grad_ffn,
        slope,
        branch,
        middle,
        cotangent,
        eight_rows(gains[2], gains[1]),
        group_a,
        group_u,
        group_d,
        device,
    )
    grad_pre, grad_branch, grad_attended = meet([flow_d], grad_pre, grad_branch, grad_attended)
    flow_u = weight_flow(mid_low, grad_pre)
    grad_branch, grad_attended = begin([flow_u], grad_branch, grad_attended)

    def attention_flow(grads, layers):
        index = layers[0] * width // part
        return Flow(
            reduce_flow(
                attention_other(seq_normed, grad_branch, grads, attended, index, width, device),
                lambda got: attention_this(
                    seq_normed, grad_branch, grads, attended, got, index, width, device
                ),
                layers,
                device,
            )
        )

    layers_b, layers_a = everyone[: mp // 2], everyone[mp // 2 :]
    back = functools.partial(
        attend_back, queries, keys, values, key_const, aug, grad_attended, attended
    )
    far_q, far_k, far_v = back(0, full)
    far_grad = unproject((far_k, far_v), (1, 2), group_a, 0, None, BF16, device)
    far_grad, far_q, far_k, far_v = ordered([flow_d, flow_u], (far_grad, far_q, far_k, far_v))
    flow_f = Flow(rows_back(far_grad, rows, blocks))
    far_q, far_k, far_v = begin([flow_f, flow_u], far_q, far_k, far_v)
    grads_a = back(part, part, far_q)
    flow_qa = attention_flow((*grads_a, far_k, far_v), layers_a)
    far_q, *grads_a = meet([flow_u, flow_f], far_q, *grads_a)
    far_q, *grads_a = begin([flow_qa], far_q, *grads_a)
    near_a = unproject(grads_a, (0, 1, 2), group_a, mp // 2, None, F32, device)
    far_q, near_a = meet([flow_qa], far_q, near_a)
    far_q, near_a = begin([flow_d], far_q, near_a)
    grads_b = back(0, part, far_q)
    grads_b = ordered([flow_u, flow_qa, flow_d], grads_b)
    flow_qb = attention_flow((*grads_b, far_k, far_v), layers_b)
    grads_b = begin([flow_qb], *grads_b)
    grads_b = begin([flow_u, flow_qa, flow_d], *grads_b)
    near_b = unproject(grads_b, (0, 1, 2), group_a, 0, near_a, F32, device)
    near_b, *grads_a, sums_ffn, sums_back, sums_up = meet(
        [flow_qb, flow_qa], near_b, *grads_a, sums_ffn, sums_back, sums_up
    )
    near_b = meet([flow_u, flow_d], near_b)
    drain(flow_d)
    down_mine = flow_d.result.astype(BF16)
    down_all = lax.all_gather(down_mine, "dp", axis=0)
    grad_normed = near_b
    for value in flow_f.result:
        grad_normed = grad_normed + value.astype(F32)
    back_one, gain_one, shift_one = norm_backward(grad_normed, norm_one, inv_one, gains[0])
    input_grad = grad_middle + back_one
    table_part = jnp.dot(
        onehot.astype(F32).T, input_grad, precision=PRECISE, preferred_element_type=F32
    )
    grad_q_sum = jnp.concatenate([jnp.sum(g[0].astype(F32), axis=0) for g in (grads_b, grads_a)])
    grad_v_sum = jnp.concatenate([jnp.sum(g[2].astype(F32), axis=0) for g in (grads_b, grads_a)])
    grad_v_sum = grad_v_sum + jnp.sum(far_v.astype(F32), axis=0)
    ffn_sums = jnp.sum(sums_ffn.reshape(3, 8, full), axis=1)
    back_sums = jnp.sum(sums_back.reshape(5, 8, full), axis=1)
    up_bias_part = jnp.sum(sums_up, axis=0)
    by_layer = jnp.concatenate(
        [grad_q_sum.reshape(mp, -1), grad_v_sum.reshape(mp, -1), up_bias_part.reshape(mp, -1)],
        axis=1,
    )
    by_layer = jnp.take(by_layer, order_of, axis=0)
    wide = by_layer.shape[1]
    by_layer = jnp.pad(by_layer, ((0, 0), (0, -wide % full))).reshape(-1, full)
    input_grad, table_part, gain_one, shift_one = meet(
        [flow_qb, flow_qa, flow_u], input_grad, table_part, gain_one, shift_one
    )
    drain(flow_u)
    up_mine = flow_u.result.astype(BF16)
    up_all = lax.all_gather(up_mine, "dp", axis=0)
    parts = jnp.concatenate(
        [
            jnp.stack([gain_one, back_sums[2], back_sums[0], ffn_sums[0]]),
            jnp.stack([shift_one, back_sums[3], back_sums[1], ffn_sums[1]]),
            jnp.stack([back_sums[4], ffn_sums[2]]),
            table_part,
            by_layer,
        ]
    )
    flow_s = Flow(small_flow(parts))
    drain(flow_qa, flow_qb)
    mine = (flow_qa.result + flow_qb.result).astype(BF16)
    flow_o = Flow(spread_flow((mine[:, : 2 * width], mine[:, 2 * width :])))
    for _ in range(2 * (dp.bit_length() + mp.bit_length() - 3)):
        flow_s.move(flow_s.held)
    down_grad = fill_ffn(down_all, True)
    up_grad = fill_ffn(up_all, False)
    down_grad, up_grad = begin([flow_s], down_grad, up_grad)
    drain(flow_o, flow_s)
    qkv_grad, out_grad = fill_attention(flow_o.result, full, width, device)

    parts = flow_s.result
    gain_grad, shift_grad = parts[:4], parts[4:8]
    out_bias_grad, down_bias_grad = parts[8], parts[9]
    n_groups = group_table.shape[0]
    table_grad = parts[10 : 10 + n_groups]
    by_layer = parts[10 + n_groups :].reshape(mp, -1)
    mine = lax.dynamic_index_in_dim(by_layer, layer, keepdims=False)
    qv_bias_grad = mine[: 2 * width].reshape(2, width)
    up_bias_grad = mine[2 * width : 2 * width + hidden]
    return (
        output,
        input_grad,
        qkv_grad,
        qv_bias_grad,
        out_grad,
        out_bias_grad,
        up_grad,
        up_bias_grad,
        down_grad,
        down_bias_grad,
        gain_grad,
        shift_grad,
        table_grad,
    )


def rows_back(value, rows, blocks):
    (value,) = yield (value,)
    return (
        yield tuple(swap(value[(m - 1) * rows : m * rows], "mp", m) for m in range(1, blocks))
    )


def solution(mesh):
    placed = (
        P(("dp", "mp"), None),
        P(("dp", "mp")),
        P("dp"),
        P(None, None, "mp"),
        P(None, "mp"),
        P("mp", None),
        P(),
        P(None, "mp"),
        P("mp"),
        P("mp", None),
        P(),
        P(),
        P(),
        P(),
        P(("dp", "mp"), None),
    )
    return jax.shard_map(
        on_device,
        mesh=mesh,
        in_specs=placed,
        out_specs=(
            P(("dp", "mp"), None),
            P(("dp", "mp"), None),
            P(None, None, "mp"),
            P(None, "mp"),
            P("mp", None),
            P(),
            P(None, "mp"),
            P("mp"),
            P("mp", None),
            P(),
            P(),
            P(),
            P(),
        ),
        check_vma=False,
    )
```
